32 devices in a mesh: region: 2 (over x), dom: 16 (over z, y, core).
Axes of the slice: x: 2, y: 2, z: 4, core: 2. Of those that a mesh axis runs over, the one named last changes fastest.
Arguments:
- descriptors: bfloat16 [49152, 768], P(('region', 'dom')), parts along dimension 0, may hold values from -8 to 8
- queries: bfloat16 [256, 768], P('region'), parts along dimension 0, may hold values from -0.21875 to 0.21875
- affinity: bfloat16 [384, 4, 128, 128], P(('region', 'dom')), parts along dimension 0, may hold values from 0 to 1, as said below
- tile_col: int32 [384, 4], P(('region', 'dom')), parts along dimension 0, may hold values from 0 to 191, as said below
Outputs:
- ranking: float32 [49152, 128], P(('region', 'dom')), parts along dimension 0
The draws below stay inside these ranges and needn't reach their ends.
There are 2 independent parts, one for each index of `region`. The reference program is written for one: setup_inputs(seed, part) draws one part's arguments, and reference() takes and returns one part's arrays. A program takes and returns all parts, laid end to end along the dimension named above; each array names one. Nothing has to cross between parts.
Inputs may be any that keep to these rules, and one draw needn't show every extreme that they name: `tile_col`: tile slot 0 of row block g names g, slot 1 names g - 1 and slot 2 names g + 1 around the cycle of 192 blocks. Every named block lies within 6 blocks of the named device's own blocks around the cycle, and of the 6 blocks of each neighbour nearest to a device, the device's tiles name exactly 3. `affinity`: the matrix S with these tiles is symmetric with nonnegative entries: D^-1/2 W D^-1/2 for a symmetric W positive on its tiles, D the row sums of W.
All inputs are finite; a program needn't handle non-finite values.
Results may differ from the reference program's by a relative error of at most 0.0029.
Values may be sent and summed in bfloat16 or wider, within the bound.
No kernel may reach another device: no remote copies, remote signals or barrier semaphores. Data moves between devices by JAX's collectives and lax.ppermute only.
A program may use at most 64 MiB of HBM per device.

```python
import jax
import jax.numpy as jnp
from jax import lax

DESC_DIM = 768
QUERIES = 128
TILE_ROWS = 128
TILE_SLOTS = 4
NB_DEV = 12
HALO_W = 6
CROSS_LINKS = 2
ITERATIONS = 5
NBLOCKS = 192
NODE_COUNT = 24576


def graph_layout(key):
    base_key = jax.random.fold_in(key, 11)
    device_count = NBLOCKS // NB_DEV
    devices = jnp.arange(device_count)

    def choose_edge(salt_value):

        def single_device(device_id):
            picked_key = jax.random.fold_in(jax.random.fold_in(base_key, salt_value), device_id)
            return jax.random.permutation(picked_key, HALO_W - 1)[:CROSS_LINKS]
        return jax.vmap(single_device)(devices)
    right_pick = choose_edge(1)
    left_pick = choose_edge(2)
    upper_ids = (devices[:, None] * NB_DEV + NB_DEV - HALO_W + right_pick).reshape(-1).astype(jnp.int32)
    lower_ids = ((devices[:, None] + 1) % device_count * NB_DEV + 1 + left_pick).reshape(-1).astype(jnp.int32)
    partner = jnp.full((NBLOCKS,), -1, jnp.int32)
    partner = partner.at[upper_ids].set(lower_ids)
    partner = partner.at[lower_ids].set(upper_ids)
    paired = (partner >= 0).reshape(device_count, NB_DEV)
    single = NB_DEV - 2 * CROSS_LINKS
    half_count = single // 2

    def local_pairs(device_id, flags):
        ranking = jax.random.permutation(jax.random.fold_in(jax.random.fold_in(base_key, 3), device_id), NB_DEV).astype(jnp.int32)
        positions = jnp.arange(NB_DEV, dtype=jnp.int32)
        priority = jnp.where(flags, NB_DEV + positions, ranking)
        ordering = jnp.argsort(priority).astype(jnp.int32)
        first_ids = ordering[0:2 * half_count:2]
        second_ids = ordering[1:2 * half_count:2]
        partner_ids = positions.at[first_ids].set(second_ids).at[second_ids].set(first_ids)
        return partner_ids + device_id * NB_DEV
    local_ids = jax.vmap(local_pairs)(devices, paired).reshape(-1).astype(jnp.int32)
    partner = jnp.where(partner >= 0, partner, local_ids)
    block_ids = jnp.arange(NBLOCKS, dtype=jnp.int32)
    column_ids = jnp.stack([block_ids, (block_ids - 1) % NBLOCKS, (block_ids + 1) % NBLOCKS, partner], axis=1)
    return column_ids.astype(jnp.int32)


def draw_tile_col(key, part):
    return graph_layout(key)


def draw_affinity(key, part):
    column_ids = graph_layout(key)
    base_key = jax.random.fold_in(key, 23)
    block_ids = jnp.arange(NBLOCKS, dtype=jnp.int32)

    def draw_tiles(salt_value):
        salt_key = jax.random.fold_in(base_key, salt_value)

        def single_tile(block_id):
            uniform_draw = jax.random.uniform(jax.random.fold_in(salt_key, block_id), (TILE_ROWS, TILE_ROWS), jnp.float32)
            return 0.05 + 0.95 * uniform_draw
        return jax.vmap(single_tile)(block_ids)
    own_tiles = draw_tiles(0)
    own_tiles = 0.5 * (own_tiles + jnp.swapaxes(own_tiles, 1, 2))
    chain_tiles = draw_tiles(1)
    down_tiles = jnp.swapaxes(jnp.roll(chain_tiles, 1, axis=0), 1, 2)
    cross_tiles = draw_tiles(2)
    partner = column_ids[:, 3]
    lowest = jnp.minimum(block_ids, partner)
    chosen = cross_tiles[lowest]
    transposed = jnp.swapaxes(chosen, 1, 2)
    symmetric = 0.5 * (chosen + transposed)
    extra_tiles = jnp.where((block_ids < partner)[:, None, None], chosen, jnp.where((block_ids > partner)[:, None, None], transposed, symmetric))
    weights = jnp.stack([own_tiles, down_tiles, chain_tiles, extra_tiles], axis=1)
    degrees = jnp.sum(weights, axis=(1, 3))
    inverse_root = lax.rsqrt(degrees)
    normed = weights * inverse_root[:, None, :, None] * inverse_root[column_ids][:, :, None, :]
    return normed.astype(jnp.bfloat16)


def draw_descriptors(key, part):
    positions = jnp.arange(NODE_COUNT, dtype=jnp.float32)
    row_scale = (1.0 + 2.0 * positions / NODE_COUNT) ** (1.0 / 6.0)
    values = jnp.clip(jax.random.normal(jax.random.fold_in(key, 31), (NODE_COUNT, DESC_DIM), jnp.float32), -6.0, 6.0)
    return (values * row_scale[:, None]).astype(jnp.bfloat16)


def gaussian(key, shape, deviation, most, kind=jnp.bfloat16):
    drawn = jax.random.normal(key, shape, jnp.float32) * deviation
    return jnp.minimum(jnp.maximum(drawn, -most), most).astype(kind)


def setup_inputs(seed: int = 0, part: int = 0) -> dict:
    arg_keys = jax.random.split(jax.random.key(seed), 5)
    part_keys = jax.random.split(jax.random.fold_in(arg_keys[4], part), 5)
    descriptors = draw_descriptors(jax.random.fold_in(jax.random.fold_in(arg_keys[4], part), 71), part)
    queries = gaussian(part_keys[1], (QUERIES, DESC_DIM), DESC_DIM ** -0.5, 0.21875)
    affinity = draw_affinity(jax.random.fold_in(jax.random.fold_in(arg_keys[4], part), 71), part)
    tile_col = draw_tile_col(jax.random.fold_in(jax.random.fold_in(arg_keys[4], part), 71), part)
    return {"descriptors": descriptors, "queries": queries, "affinity": affinity, "tile_col": tile_col}


def operate(direction, affinity, tile_col):
    block_total = affinity.shape[0]
    rounded = direction.astype(jnp.bfloat16).reshape(block_total, TILE_ROWS, QUERIES)

    def block_group(pieces):
        tile_group, column_ids = pieces
        picked = rounded[column_ids].astype(jnp.float32)
        return jnp.einsum("bkij,bkjq->biq", tile_group.astype(jnp.float32), picked, precision=lax.Precision.HIGHEST)

    groups = block_total // NB_DEV
    spread = lax.map(block_group, (affinity.reshape(groups, NB_DEV, TILE_SLOTS, TILE_ROWS, TILE_ROWS), tile_col.reshape(groups, NB_DEV, TILE_SLOTS)))
    return direction - 0.99 * spread.reshape(-1, QUERIES)


def reference(descriptors, queries, affinity, tile_col):
    scores = lax.dot_general(descriptors, queries, (((1,), (1,)), ((), ())), preferred_element_type=jnp.float32)
    targets = jnp.maximum(scores, 0.0) ** 3
    ranking = jnp.zeros_like(targets)
    residual = targets
    direction = targets
    norm_now = jnp.sum(residual * residual, axis=0)
    for step_index in range(ITERATIONS):
        applied = operate(direction, affinity, tile_col)
        step_size = norm_now / jnp.sum(direction * applied, axis=0)
        ranking = ranking + step_size * direction
        if step_index + 1 < ITERATIONS:
            residual = residual - step_size * applied
            norm_next = jnp.sum(residual * residual, axis=0)
            direction = residual + (norm_next / norm_now) * direction
            norm_now = norm_next
    return ranking
```

```python
import functools

import jax
import jax.numpy as jnp
from jax import lax
from jax.experimental import pallas as pl
from jax.experimental.pallas import tpu as pltpu
from jax.sharding import PartitionSpec as P

HALO_W = 6
NAMED = 3
ITERATIONS = 5
DAMP = 0.99
SHIFTS = (0.0, 1.0, -0.25, 0.5)
PIVOT_MIN = 1e-6
BF = jnp.bfloat16
F32 = jnp.float32
PAIRS = [(i, j) for i in range(ITERATIONS) for j in range(i, ITERATIONS)]
ROWS = len(PAIRS) + 1
ENTRIES = 2 + 2 * NAMED

VMEM = pl.BlockSpec(memory_space=pltpu.VMEM)
SMEM = pl.BlockSpec(memory_space=pltpu.SMEM)
ANY = pl.BlockSpec(memory_space=pl.ANY)


def params(mib):
    return pltpu.CompilerParams(vmem_limit_bytes=mib << 20)


def dot(a, b):
    return jnp.dot(a, b, preferred_element_type=F32)


def dot_t(a, b):
    return lax.dot_general(a, b, (((0,), (0,)), ((), ())), preferred_element_type=F32)


def put_split(ref, index, value):
    high = value.astype(BF)
    width = value.shape[-1]
    ref[index, :, :width] = high
    ref[index, :, width:] = (value - high.astype(F32)).astype(BF)


def row_product(aff, pos, base, g, hl):
    count = aff.shape[0]
    width = hl.shape[2] // 2
    lower = hl[g - 1] if g > 0 else hl[pos[2 * count + base // count]]
    upper = hl[g + 1] if g + 1 < count else hl[pos[2 * count + 2 + base // count]]
    left = jnp.concatenate([aff[g, 0], aff[g, 1]], axis=1)
    right = jnp.concatenate([hl[g], lower], axis=0)
    out = dot(left, right)
    left = jnp.concatenate([aff[g, 2], aff[g, 3]], axis=1)
    right = jnp.concatenate([upper, hl[pos[base + g]]], axis=0)
    out = out + dot(left, right)
    return out[:, :width] + out[:, width:]


def pack(meta, shift, t, y, send, base):
    for j in range(NAMED):
        g = meta[base + j]
        value = t[g]
        send[j] = value.astype(BF)
        send[NAMED + j] = (y[g] - shift * value).astype(BF)


def first_kernel(pos, lists, desc, queries, aff, t0, y0, send_a, send_b, hl, buf, sems, *, chunks):
    count, rows = t0.shape[0], t0.shape[1]
    per = count // chunks
    copies = []
    for c in range(chunks):
        copy = pltpu.make_async_copy(
            desc.at[pl.ds(c * per * rows, per * rows)], buf.at[c], sems.at[c]
        )
        copy.start()
        copies.append(copy)
    hl[count + 2 * NAMED] = jnp.zeros(hl.shape[1:], BF)
    for c in range(chunks):
        copies[c].wait()
        scores = lax.dot_general(
            buf[c], queries[...], (((1,), (1,)), ((), ())), preferred_element_type=F32
        )
        value = jnp.maximum(scores, 0.0)
        value = value * value * value
        for i in range(per):
            block = value[i * rows : (i + 1) * rows]
            t0[c * per + i] = block
            put_split(hl, c * per + i, block)
    for g in range(count):
        y0[g] = row_product(aff, pos, 0, g, hl)
    pack(lists, SHIFTS[0], t0, y0, send_b, NAMED)
    pack(lists, SHIFTS[0], t0, y0, send_a, 0)


def two_steps(pos, cross, aff, t, y, recv_a, recv_b, t1, t2, hl, hl2, acc, hacc, step):
    count, width = t.shape[0], t.shape[2]
    zero = count + 2 * NAMED
    hl[zero] = jnp.zeros(hl.shape[1:], BF)
    hl2[zero] = jnp.zeros(hl.shape[1:], BF)
    for h in range(NAMED):
        hl[count + h, :, :width] = recv_a[h]
        hl[count + NAMED + h, :, :width] = recv_b[h]
        hacc[h] = recv_a[NAMED + h].astype(F32)
        hacc[NAMED + h] = recv_b[NAMED + h].astype(F32)
    for g in range(count):
        acc[g] = y[g] - SHIFTS[step] * t[g]
    for e in range(ENTRIES):
        g, slot, h = cross[3 * e], cross[3 * e + 1], cross[3 * e + 2]
        row = jnp.minimum(g, count - 1)
        tile = aff[row, slot]
        acc[g] += dot(tile, hl[count + h, :, :width])
        hacc[h] += dot_t(tile, t[row].astype(BF))
    for g in range(count):
        value = acc[g]
        t1[g] = value
        put_split(hl, g, value)
    for h in range(2 * NAMED):
        put_split(hl, count + h, hacc[h])
    for g in range(count):
        value = row_product(aff, pos, count, g, hl) - SHIFTS[step + 1] * t1[g]
        t2[g] = value
        put_split(hl2, g, value)


def middle_kernel(
    pos, lists, cross, aff, t, y, recv_a, recv_b, t1, t2, y2, send_a, send_b, hl, hl2, acc, hacc
):
    two_steps(pos, cross, aff, t, y, recv_a, recv_b, t1, t2, hl, hl2, acc, hacc, 0)
    for g in range(t.shape[0]):
        y2[g] = row_product(aff, pos, 0, g, hl2)
    pack(lists, SHIFTS[2], t2, y2, send_b, NAMED)
    pack(lists, SHIFTS[2], t2, y2, send_a, 0)


def last_kernel(
    pos, lists, cross, aff, t, y, recv_a, recv_b, t3, t4, send, hl, hl2, acc, hacc
):
    two_steps(pos, cross, aff, t, y, recv_a, recv_b, t3, t4, hl, hl2, acc, hacc, 2)
    for j in range(NAMED):
        send[j] = t4[lists[2 * NAMED + j]].astype(BF)


def gram_kernel(pos, aff, t0, t1, t2, t3, t4, out, hl):
    count, rows, width = t0.shape
    hl[count + 2 * NAMED] = jnp.zeros(hl.shape[1:], BF)
    for g in range(count):
        put_split(hl, g, t4[g])
    fields = (t0, t1, t2, t3, t4)
    sums = [jnp.zeros((8, width), F32) for _ in range(ROWS)]
    for g in range(count):
        local = row_product(aff, pos, 0, g, hl)
        sums[-1] = sums[-1] + (t4[g] * local).reshape(rows // 8, 8, width).sum(0)

    def body(i, sums):
        sums = list(sums)
        g = i // (rows // 32)
        start = pl.multiple_of((i % (rows // 32)) * 32, 32)
        for part in range(4):
            v = [f[g, pl.ds(pl.multiple_of(start + 8 * part, 8), 8), :] for f in fields]
            for n, (a, b) in enumerate(PAIRS):
                sums[n] = sums[n] + v[a] * v[b]
        return tuple(sums)

    sums = lax.fori_loop(0, count * rows // 32, body, tuple(sums))
    for n in range(ROWS):
        out[pl.ds(n, 1), :] = jnp.sum(sums[n], axis=0, keepdims=True)


def cross_kernel(lists, cross, aff, t4, recv, gram, out):
    count = t4.shape[0]
    total = jnp.zeros((8, gram.shape[1]), F32)
    for e in range(1 + NAMED):
        g, slot, h = (cross[3 * ENTRIES + 3 * e + i] for i in range(3))
        row = jnp.minimum(g, count - 1)
        part = t4[row] * dot(aff[row, slot], recv[jnp.minimum(h, NAMED - 1)])
        part = part.reshape(-1, 8, part.shape[-1]).sum(0)
        total = total + jnp.where(g < count, part, 0.0)
    value = gram[...]
    extra = 2.0 * jnp.sum(total, axis=0, keepdims=True)
    index = lax.broadcasted_iota(jnp.int32, value.shape, 0)
    value = value + jnp.where(index == ROWS - 1, extra, 0.0)
    for d in range(out.shape[0]):
        out[d] = value


def final_kernel(parts, t0, t1, t2, t3, t4, out):
    n = ITERATIONS
    value = parts[0]
    for d in range(1, parts.shape[0]):
        value = value + parts[d]
    gram = {}
    for k, (i, j) in enumerate(PAIRS):
        gram[i, j] = gram[j, i] = value[k : k + 1]
    matrix = {}
    for i in range(n):
        for j in range(i, n):
            terms = []
            if j + 1 < n:
                terms.append(gram[i, j + 1] + SHIFTS[j] * gram[i, j])
            if i + 1 < n and i != j:
                terms.append(gram[i + 1, j] + SHIFTS[i] * gram[i, j])
            if not terms:
                terms = [value[ROWS - 1 : ROWS]]
            product = terms[0] if len(terms) == 1 else 0.5 * (terms[0] + terms[1])
            matrix[i, j] = gram[i, j] - DAMP * product
    scale = [
        jnp.where(matrix[i, i] > 0.0, lax.rsqrt(jnp.maximum(matrix[i, i], 1e-37)), 0.0)
        for i in range(n)
    ]
    for i in range(n):
        for j in range(i, n):
            matrix[i, j] = matrix[i, j] * (scale[i] * scale[j])
    right = [gram[i, 0] * scale[i] for i in range(n)]
    inverse = []
    for k in range(n):
        pivot = matrix[k, k]
        inverse.append(jnp.where(pivot > PIVOT_MIN, 1.0 / jnp.maximum(pivot, PIVOT_MIN), 0.0))
        for i in range(k + 1, n):
            factor = matrix[k, i] * inverse[k]
            for j in range(i, n):
                matrix[i, j] = matrix[i, j] - factor * matrix[k, j]
            right[i] = right[i] - factor * right[k]
    coef = [None] * n
    for k in range(n - 1, -1, -1):
        rest = right[k]
        for j in range(k + 1, n):
            rest = rest - matrix[k, j] * coef[j]
        coef[k] = rest * inverse[k]
    coef = [coef[k] * scale[k] for k in range(n)]
    fields = (t0, t1, t2, t3, t4)
    count, rows, width = t0.shape
    wide = [jnp.broadcast_to(c, (8, width)) for c in coef]
    for g in range(count):
        total = None
        for f, c in zip(fields, coef):
            term = f[g] * c
            total = term if total is None else total + term
        out[pl.ds(g * rows, rows), :] = total


def tables(tile_col, count, axis):
    devices = lax.axis_size(axis)
    total = count * devices
    me = lax.axis_index(axis)
    even = me % 2 == 0
    relative = (tile_col[:, 3] - me * count) % total
    local = relative < count
    up = (relative >= count) & (relative < count + HALO_W)
    low = relative >= total - HALO_W
    up_place = relative - count
    low_place = relative - (total - HALO_W)
    places = jnp.arange(HALO_W)
    blocks = jnp.arange(count)
    up_named = jnp.any(up[:, None] & (up_place[:, None] == places), 0) | (places == 0)
    low_named = jnp.any(low[:, None] & (low_place[:, None] == places), 0) | (places == HALO_W - 1)
    up_rank = jnp.sum(up_named[None] & (places[None] < up_place[:, None]), 1)
    low_rank = jnp.sum(low_named[None] & (places[None] < low_place[:, None]), 1)
    up_base = jnp.where(even, 0, NAMED)
    low_base = NAMED - up_base
    halo = jnp.where(up, up_base + up_rank, low_base + low_rank)
    halo = jnp.clip(halo, 0, 2 * NAMED - 1)
    zero = count + 2 * NAMED
    pos_local = jnp.where(local, relative, zero)
    pos_full = jnp.where(local, relative, count + halo)
    low_chain = low_base + NAMED - 1
    up_chain = up_base
    pos = jnp.concatenate(
        [pos_local, pos_full, jnp.stack([zero + 0 * me, count + low_chain, zero + 0 * me, count + up_chain])]
    )

    def members(flag, fill):
        rank = jnp.sum(flag[None] & (blocks[None] < blocks[:, None]), 1)
        hit = flag[None] & (rank[None] == jnp.arange(NAMED)[:, None])
        return jnp.sum(jnp.where(hit, blocks[None] + 1, 0), 1) - 1, hit

    up_list, _ = members(up | (blocks == count - 1), 0)
    low_list, _ = members(low | (blocks == 0), 0)
    up_list = jnp.clip(up_list, 0, count - 1)
    low_list = jnp.clip(low_list, 0, count - 1)
    lists = jnp.concatenate(
        [jnp.where(even, up_list, low_list), jnp.where(even, low_list, up_list), low_list]
    )

    def entries(flag, rank, base, chain_row, chain_slot, chain_rank):
        rows, hit = members(flag, count)
        used = rows >= 0
        ranks = jnp.sum(jnp.where(hit, rank[None], 0), 1)
        rows = jnp.where(used, rows, count)
        ranks = jnp.where(used, jnp.clip(base + ranks, 0, 2 * NAMED - 1), 2 * NAMED)
        first = jnp.stack([chain_row + 0 * base, chain_slot + 0 * base, base + chain_rank])
        rest = jnp.stack([rows, 3 + 0 * rows, ranks], 1).reshape(-1)
        return jnp.concatenate([first, rest])

    cross = jnp.concatenate(
        [
            entries(low, low_rank, low_base, 0, 1, NAMED - 1),
            entries(up, up_rank, up_base, count - 1, 2, 0),
            entries(up, up_rank, 0 * up_base, count - 1, 2, 0),
        ]
    )
    return pos.astype(jnp.int32), lists.astype(jnp.int32), cross.astype(jnp.int32)


def swap(block_a, block_b, axis):
    n = lax.axis_size(axis)
    pairs_a = [(i, i ^ 1) for i in range(n)]
    pairs_b = [(i, (i + 1) % n if i % 2 else (i - 1) % n) for i in range(n)]
    got_b = lax.ppermute(block_b, axis, pairs_b)
    got_a = lax.ppermute(block_a, axis, pairs_a)
    return got_a, got_b


def shards(descriptors, queries, affinity, tile_col):
    count, _, rows, _ = affinity.shape
    width = queries.shape[0]
    depth = descriptors.shape[1]
    axis = "dom"
    devices = lax.axis_size(axis)
    pos, lists, cross = tables(tile_col, count, axis)
    blocks = count + 2 * NAMED + 1
    field = jax.ShapeDtypeStruct((count, rows, width), F32)
    edge = jax.ShapeDtypeStruct((2 * NAMED, rows, width), BF)
    half = jax.ShapeDtypeStruct((NAMED, rows, width), BF)
    split = pltpu.VMEM((blocks, rows, 2 * width), BF)
    work = [
        split,
        split,
        pltpu.VMEM((count + 1, rows, width), F32),
        pltpu.VMEM((2 * NAMED + 1, rows, width), F32),
    ]
    chunks = 4
    flops = 2 * count * rows * 4 * rows * 2 * width

    def cost(products, extra=0, bytes_accessed=4 << 20):
        return pl.CostEstimate(
            flops=products * flops + extra, bytes_accessed=bytes_accessed, transcendentals=0
        )

    t0, y0, send_a, send_b = pl.pallas_call(
        functools.partial(first_kernel, chunks=chunks),
        out_shape=(field, field, edge, edge),
        in_specs=[SMEM, SMEM, ANY, VMEM, VMEM],
        out_specs=(VMEM,) * 4,
        scratch_shapes=[
            split,
            pltpu.VMEM((chunks, count * rows // chunks, depth), BF),
            pltpu.SemaphoreType.DMA((chunks,)),
        ],
        compiler_params=params(24),
        cost_estimate=cost(1, 2 * count * rows * depth * width),
        name="first",
    )(pos, lists, descriptors, queries, affinity)
    recv_a, recv_b = swap(send_a, send_b, axis)
    t1, t2, y2, send_a, send_b = pl.pallas_call(
        middle_kernel,
        out_shape=(field, field, field, edge, edge),
        in_specs=[SMEM] * 3 + [VMEM] * 5,
        out_specs=(VMEM,) * 5,
        scratch_shapes=work,
        compiler_params=params(24),
        cost_estimate=cost(2),
        name="middle",
    )(pos, lists, cross, affinity, t0, y0, recv_a, recv_b)
    recv_a, recv_b = swap(send_a, send_b, axis)
    t3, t4, send = pl.pallas_call(
        last_kernel,
        out_shape=(field, field, half),
        in_specs=[SMEM] * 3 + [VMEM] * 5,
        out_specs=(VMEM,) * 3,
        scratch_shapes=work,
        compiler_params=params(24),
        cost_estimate=cost(2),
        name="last",
    )(pos, lists, cross, affinity, t2, y2, recv_a, recv_b)
    recv = lax.ppermute(send, axis, [(i, (i - 1) % devices) for i in range(devices)])
    gram = pl.pallas_call(
        gram_kernel,
        out_shape=jax.ShapeDtypeStruct((ROWS, width), F32),
        in_specs=[SMEM] + [VMEM] * 6,
        out_specs=VMEM,
        scratch_shapes=[split],
        compiler_params=params(24),
        cost_estimate=cost(1),
        name="gram",
    )(pos, affinity, t0, t1, t2, t3, t4)
    parts = pl.pallas_call(
        cross_kernel,
        out_shape=jax.ShapeDtypeStruct((devices, ROWS, width), F32),
        in_specs=[SMEM] * 2 + [VMEM] * 4,
        out_specs=VMEM,
        compiler_params=params(8),
        name="cross",
    )(lists, cross, affinity, t4, recv, gram)
    parts = lax.all_to_all(parts, axis, 0, 0)
    return pl.pallas_call(
        final_kernel,
        out_shape=jax.ShapeDtypeStruct((count * rows, width), F32),
        in_specs=[VMEM] * 6,
        out_specs=VMEM,
        compiler_params=params(24),
        name="final",
    )(parts, t0, t1, t2, t3, t4)


def solution(mesh):
    return jax.shard_map(
        shards,
        mesh=mesh,
        in_specs=(
            P(("region", "dom"), None),
            P("region", None),
            P(("region", "dom"), None, None, None),
            P(("region", "dom"), None),
        ),
        out_specs=P(("region", "dom"), None),
        check_vma=False,
    )
```

```python
import functools

import jax
import jax.numpy as jnp
from jax import lax
from jax.experimental import pallas as pl
from jax.experimental.pallas import tpu as pltpu
from jax.sharding import PartitionSpec as P

HALO_W = 6
NAMED = 3
ITERATIONS = 5
DAMP = 0.99
SHIFTS = (0.0, 1.0, -0.25, 0.5)
PIVOT_MIN = 1e-6
BF = jnp.bfloat16
F32 = jnp.float32
PAIRS = [(i, j) for i in range(ITERATIONS) for j in range(i, ITERATIONS)]
ROWS = len(PAIRS) + 1
ENTRIES = 2 + 2 * NAMED

VMEM = pl.BlockSpec(memory_space=pltpu.VMEM)
SMEM = pl.BlockSpec(memory_space=pltpu.SMEM)
HBM = pl.BlockSpec(memory_space=pltpu.HBM)


def params(mib):
    return pltpu.CompilerParams(vmem_limit_bytes=mib << 20)


def dot(a, b):
    return jnp.dot(a, b, preferred_element_type=F32)


def dot_t(a, b):
    return lax.dot_general(a, b, (((0,), (0,)), ((), ())), preferred_element_type=F32)


def put_split(ref, index, value):
    high = value.astype(BF)
    width = value.shape[-1]
    ref[index, :, :width] = high
    ref[index, :, width:] = (value - high.astype(F32)).astype(BF)


def row_product(aff, tab, base, g, hl):
    count = aff.shape[0]
    width = hl.shape[2] // 2
    lower = hl[g - 1] if g > 0 else hl[tab[base + count]]
    upper = hl[g + 1] if g + 1 < count else hl[tab[base + count + 1]]
    left = jnp.concatenate([aff[g, 0], aff[g, 1]], axis=1)
    right = jnp.concatenate([hl[g], lower], axis=0)
    out = dot(left, right)
    left = jnp.concatenate([aff[g, 2], aff[g, 3]], axis=1)
    right = jnp.concatenate([upper, hl[tab[base + g]]], axis=0)
    out = out + dot(left, right)
    return out[:, :width] + out[:, width:]


def offsets(count):
    full = count + 2
    lists = 2 * full
    cross = lists + 3 * NAMED
    high = cross + 3 * ENTRIES
    return full, lists, cross, high, high + 3 * (1 + NAMED)


def fill_table(tile_col, tab, up_rows, low_rows, axis):
    count = tile_col.shape[1]
    total = count * lax.axis_size(axis)
    me = lax.axis_index(axis)
    even = lax.rem(me, 2) == 0
    full, lists, cross, high, _ = offsets(count)
    zero = count + 2 * NAMED
    up_base = jnp.where(even, 0, NAMED)
    low_base = NAMED - up_base
    relative, ups, lows = [], [], []
    up_mask = jnp.int32(1)
    low_mask = jnp.int32(1 << (HALO_W - 1))
    for g in range(count):
        rel = tile_col[3, g] - me * count
        rel = jnp.where(rel < 0, rel + total, rel)
        up = (rel >= count) & (rel < count + HALO_W)
        low = rel >= total - HALO_W
        place = jnp.where(up, rel - count, rel - (total - HALO_W))
        place = jnp.clip(place, 0, HALO_W - 1)
        bit = lax.shift_left(jnp.int32(1), place)
        up_mask = up_mask | jnp.where(up, bit, 0)
        low_mask = low_mask | jnp.where(low, bit, 0)
        relative.append((rel, place, bit))
        ups.append(up)
        lows.append(low)
    up_count = low_count = up_cross = low_cross = jnp.int32(0)
    for g in range(count):
        rel, place, bit = relative[g]
        below = jnp.where(ups[g], up_mask, low_mask) & (bit - 1)
        rank = below & 1
        for p in range(1, HALO_W - 1):
            rank = rank + (lax.shift_right_logical(below, jnp.int32(p)) & 1)
        halo = jnp.where(ups[g], up_base, low_base) + jnp.minimum(rank, NAMED - 1)
        local = rel < count
        tab[g] = jnp.where(local, rel, zero)
        tab[full + g] = jnp.where(local, rel, count + halo)
        up_rows[0, up_count] = g
        low_rows[0, low_count] = g
        up_rows[1, up_cross] = g
        low_rows[1, low_cross] = g
        up_rows[2, up_cross] = halo
        low_rows[2, low_cross] = halo
        up_cross = up_cross + jnp.where(ups[g], 1, 0)
        low_cross = low_cross + jnp.where(lows[g], 1, 0)
        up_count = up_count + (1 if g == count - 1 else jnp.where(ups[g], 1, 0))
        low_count = low_count + (1 if g == 0 else jnp.where(lows[g], 1, 0))
    tab[count] = zero
    tab[count + 1] = zero
    tab[full + count] = count + low_base + NAMED - 1
    tab[full + count + 1] = count + up_base
    for j in range(NAMED):
        up, low = up_rows[0, j], low_rows[0, j]
        tab[lists + j] = jnp.where(even, up, low)
        tab[lists + NAMED + j] = jnp.where(even, low, up)
        tab[lists + 2 * NAMED + j] = low
    chains = ((0, 1, low_base + NAMED - 1), (count - 1, 2, up_base))
    for side, (rows, used) in enumerate(((low_rows, low_cross), (up_rows, up_cross))):
        for i in range(3):
            tab[cross + 3 * side * (1 + NAMED) + i] = jnp.int32(chains[side][i])
        for j in range(NAMED):
            at = cross + 3 * (side * (1 + NAMED) + 1 + j)
            tab[at] = jnp.where(j < used, rows[1, j], count)
            tab[at + 1] = jnp.int32(3)
            tab[at + 2] = jnp.where(j < used, rows[2, j], 2 * NAMED)
    for j in range(1 + NAMED):
        at = cross + 3 * (1 + NAMED + j)
        tab[high + 3 * j] = tab[at]
        tab[high + 3 * j + 1] = tab[at + 1]
        tab[high + 3 * j + 2] = tab[at + 2] - up_base


def pack(tab, shift, t, y, send, base):
    for j in range(NAMED):
        g = tab[base + j]
        value = t[g]
        send[j] = value.astype(BF)
        send[NAMED + j] = (y[g] - shift * value).astype(BF)


def first_kernel(
    desc, queries, affinity, tile_col, t0, y0, send_a, send_b, aff, tab,
    hl, buf, wide, tall, cols, up_rows, low_rows, sems, *, chunks, axis,
):
    count, rows = t0.shape[0], t0.shape[1]
    per = count // chunks
    _, lists, _, _, _ = offsets(count)
    load_q = pltpu.make_async_copy(queries, wide, sems.at[chunks])
    load_c = pltpu.make_async_copy(tile_col, cols, sems.at[chunks + 1])
    load_q.start()
    load_c.start()
    copies = []
    for c in range(chunks):
        copy = pltpu.make_async_copy(
            desc.at[pl.ds(c * per * rows, per * rows)], buf.at[c], sems.at[c]
        )
        copy.start()
        copies.append(copy)
    load_a = pltpu.make_async_copy(affinity, aff, sems.at[chunks + 2])
    load_a.start()
    hl[count + 2 * NAMED] = jnp.zeros(hl.shape[1:], BF)
    load_q.wait()
    tall[...] = wide[...].T
    load_c.wait()
    fill_table(cols, tab, up_rows, low_rows, axis)
    for c in range(chunks):
        copies[c].wait()
        value = jnp.maximum(dot(buf[c], tall[...]), 0.0)
        value = value * value * value
        for i in range(per):
            block = value[i * rows : (i + 1) * rows]
            t0[c * per + i] = block
            put_split(hl, c * per + i, block)
    load_a.wait()
    for g in range(count):
        y0[g] = row_product(aff, tab, 0, g, hl)
    pack(tab, SHIFTS[0], t0, y0, send_b, lists + NAMED)
    pack(tab, SHIFTS[0], t0, y0, send_a, lists)


def two_steps(tab, aff, t, y, recv_a, recv_b, t1, t2, hl, hl2, acc, hacc, step):
    count, width = t.shape[0], t.shape[2]
    full, _, cross, _, _ = offsets(count)
    zero = count + 2 * NAMED
    hl[zero] = jnp.zeros(hl.shape[1:], BF)
    hl2[zero] = jnp.zeros(hl.shape[1:], BF)
    for h in range(NAMED):
        hl[count + h, :, :width] = recv_a[h]
        hl[count + NAMED + h, :, :width] = recv_b[h]
        hacc[h] = recv_a[NAMED + h].astype(F32)
        hacc[NAMED + h] = recv_b[NAMED + h].astype(F32)
    for g in range(count):
        acc[g] = y[g] - SHIFTS[step] * t[g]
    for e in range(ENTRIES):
        g, slot, h = (tab[cross + 3 * e + i] for i in range(3))
        row = jnp.minimum(g, count - 1)
        tile = aff[row, slot]
        acc[g] += dot(tile, hl[count + h, :, :width])
        hacc[h] += dot_t(tile, t[row].astype(BF))
    for g in range(count):
        value = acc[g]
        t1[g] = value
        put_split(hl, g, value)
    for h in range(2 * NAMED):
        put_split(hl, count + h, hacc[h])
    for g in range(count):
        value = row_product(aff, tab, full, g, hl) - SHIFTS[step + 1] * t1[g]
        t2[g] = value
        put_split(hl2, g, value)


def middle_kernel(
    tab, aff, t, y, recv_a, recv_b, t1, t2, y2, send_a, send_b, hl, hl2, acc, hacc
):
    _, lists, _, _, _ = offsets(t.shape[0])
    two_steps(tab, aff, t, y, recv_a, recv_b, t1, t2, hl, hl2, acc, hacc, 0)
    for g in range(t.shape[0]):
        y2[g] = row_product(aff, tab, 0, g, hl2)
    pack(tab, SHIFTS[2], t2, y2, send_b, lists + NAMED)
    pack(tab, SHIFTS[2], t2, y2, send_a, lists)


def last_kernel(tab, aff, t, y, recv_a, recv_b, t3, t4, send, hl, hl2, acc, hacc):
    _, lists, _, _, _ = offsets(t.shape[0])
    two_steps(tab, aff, t, y, recv_a, recv_b, t3, t4, hl, hl2, acc, hacc, 2)
    for j in range(NAMED):
        send[j] = t4[tab[lists + 2 * NAMED + j]].astype(BF)


def gram_kernel(tab, aff, t0, t1, t2, t3, t4, out, hl):
    count, rows, width = t0.shape
    hl[count + 2 * NAMED] = jnp.zeros(hl.shape[1:], BF)
    for g in range(count):
        put_split(hl, g, t4[g])
    fields = (t0, t1, t2, t3, t4)
    sums = [jnp.zeros((8, width), F32) for _ in range(ROWS)]
    for g in range(count):
        local = row_product(aff, tab, 0, g, hl)
        sums[-1] = sums[-1] + (t4[g] * local).reshape(rows // 8, 8, width).sum(0)

    def body(i, sums):
        sums = list(sums)
        g = i // (rows // 32)
        start = pl.multiple_of((i % (rows // 32)) * 32, 32)
        for part in range(4):
            v = [f[g, pl.ds(pl.multiple_of(start + 8 * part, 8), 8), :] for f in fields]
            for n, (a, b) in enumerate(PAIRS):
                sums[n] = sums[n] + v[a] * v[b]
        return tuple(sums)

    sums = lax.fori_loop(0, count * rows // 32, body, tuple(sums))
    for n in range(ROWS):
        out[pl.ds(n, 1), :] = jnp.sum(sums[n], axis=0, keepdims=True)


def cross_kernel(tab, aff, t4, recv, gram, out):
    count = t4.shape[0]
    _, _, _, high, _ = offsets(count)
    total = jnp.zeros((8, gram.shape[1]), F32)
    for e in range(1 + NAMED):
        g, slot, h = (tab[high + 3 * e + i] for i in range(3))
        row = jnp.minimum(g, count - 1)
        part = t4[row] * dot(aff[row, slot], recv[jnp.minimum(h, NAMED - 1)])
        part = part.reshape(-1, 8, part.shape[-1]).sum(0)
        total = total + jnp.where(g < count, part, 0.0)
    value = gram[...]
    extra = 2.0 * jnp.sum(total, axis=0, keepdims=True)
    index = lax.broadcasted_iota(jnp.int32, value.shape, 0)
    value = value + jnp.where(index == ROWS - 1, extra, 0.0)
    for d in range(out.shape[0]):
        out[d] = value


def final_kernel(parts, t0, t1, t2, t3, t4, out):
    n = ITERATIONS
    value = parts[0]
    for d in range(1, parts.shape[0]):
        value = value + parts[d]
    gram = {}
    for k, (i, j) in enumerate(PAIRS):
        gram[i, j] = gram[j, i] = value[k : k + 1]
    matrix = {}
    for i in range(n):
        for j in range(i, n):
            terms = []
            if j + 1 < n:
                terms.append(gram[i, j + 1] + SHIFTS[j] * gram[i, j])
            if i + 1 < n and i != j:
                terms.append(gram[i + 1, j] + SHIFTS[i] * gram[i, j])
            if not terms:
                terms = [value[ROWS - 1 : ROWS]]
            product = terms[0] if len(terms) == 1 else 0.5 * (terms[0] + terms[1])
            matrix[i, j] = gram[i, j] - DAMP * product
    scale = [
        jnp.where(matrix[i, i] > 0.0, lax.rsqrt(jnp.maximum(matrix[i, i], 1e-37)), 0.0)
        for i in range(n)
    ]
    for i in range(n):
        for j in range(i, n):
            matrix[i, j] = matrix[i, j] * (scale[i] * scale[j])
    right = [gram[i, 0] * scale[i] for i in range(n)]
    inverse = []
    for k in range(n):
        pivot = matrix[k, k]
        inverse.append(jnp.where(pivot > PIVOT_MIN, 1.0 / jnp.maximum(pivot, PIVOT_MIN), 0.0))
        for i in range(k + 1, n):
            factor = matrix[k, i] * inverse[k]
            for j in range(i, n):
                matrix[i, j] = matrix[i, j] - factor * matrix[k, j]
            right[i] = right[i] - factor * right[k]
    coef = [None] * n
    for k in range(n - 1, -1, -1):
        rest = right[k]
        for j in range(k + 1, n):
            rest = rest - matrix[k, j] * coef[j]
        coef[k] = rest * inverse[k]
    coef = [coef[k] * scale[k] for k in range(n)]
    fields = (t0, t1, t2, t3, t4)
    count, rows, width = t0.shape
    wide = [jnp.broadcast_to(c, (8, width)) for c in coef]
    for g in range(count):
        total = None
        for f, c in zip(fields, coef):
            term = f[g] * c
            total = term if total is None else total + term
        out[pl.ds(g * rows, rows), :] = total


def swap(block_a, block_b, axis):
    n = lax.axis_size(axis)
    pairs_a = [(i, i ^ 1) for i in range(n)]
    pairs_b = [(i, (i + 1) % n if i % 2 else (i - 1) % n) for i in range(n)]
    got_b = lax.ppermute(block_b, axis, pairs_b)
    got_a = lax.ppermute(block_a, axis, pairs_a)
    return got_a, got_b


def shards(descriptors, queries, affinity, tile_col):
    count, _, rows, _ = affinity.shape
    width = queries.shape[0]
    depth = descriptors.shape[1]
    axis = "dom"
    devices = lax.axis_size(axis)
    size = 128 * pl.cdiv(offsets(count)[-1], 128)
    blocks = count + 2 * NAMED + 1
    field = jax.ShapeDtypeStruct((count, rows, width), F32)
    edge = jax.ShapeDtypeStruct((2 * NAMED, rows, width), BF)
    half = jax.ShapeDtypeStruct((NAMED, rows, width), BF)
    split = pltpu.VMEM((blocks, rows, 2 * width), BF)
    work = [
        split,
        split,
        pltpu.VMEM((count + 1, rows, width), F32),
        pltpu.VMEM((2 * NAMED + 1, rows, width), F32),
    ]
    chunks = 4
    flops = 2 * count * rows * 4 * rows * 2 * width

    def cost(products, extra=0, bytes_accessed=4 << 20):
        return pl.CostEstimate(
            flops=products * flops + extra, bytes_accessed=bytes_accessed, transcendentals=0
        )

    t0, y0, send_a, send_b, aff, tab = pl.pallas_call(
        functools.partial(first_kernel, chunks=chunks, axis=axis),
        out_shape=(
            field,
            field,
            edge,
            edge,
            jax.ShapeDtypeStruct(affinity.shape, BF),
            jax.ShapeDtypeStruct((size,), jnp.int32),
        ),
        in_specs=[HBM] * 4,
        out_specs=(VMEM,) * 5 + (SMEM,),
        scratch_shapes=[
            split,
            pltpu.VMEM((chunks, count * rows // chunks, depth), BF),
            pltpu.VMEM((width, depth), BF),
            pltpu.VMEM((depth, width), BF),
            pltpu.SMEM((4, count), jnp.int32),
            pltpu.SMEM((3, count + 1), jnp.int32),
            pltpu.SMEM((3, count + 1), jnp.int32),
            pltpu.SemaphoreType.DMA((chunks + 3,)),
        ],
        compiler_params=params(24),
        cost_estimate=cost(1, 2 * count * rows * depth * width),
        name="first",
    )(descriptors, queries, affinity, tile_col.T)
    recv_a, recv_b = swap(send_a, send_b, axis)
    t1, t2, y2, send_a, send_b = pl.pallas_call(
        middle_kernel,
        out_shape=(field, field, field, edge, edge),
        in_specs=[SMEM] + [VMEM] * 5,
        out_specs=(VMEM,) * 5,
        scratch_shapes=work,
        compiler_params=params(24),
        cost_estimate=cost(2),
        name="middle",
    )(tab, aff, t0, y0, recv_a, recv_b)
    recv_a, recv_b = swap(send_a, send_b, axis)
    t3, t4, send = pl.pallas_call(
        last_kernel,
        out_shape=(field, field, half),
        in_specs=[SMEM] + [VMEM] * 5,
        out_specs=(VMEM,) * 3,
        scratch_shapes=work,
        compiler_params=params(24),
        cost_estimate=cost(2),
        name="last",
    )(tab, aff, t2, y2, recv_a, recv_b)
    recv = lax.ppermute(send, axis, [(i, (i - 1) % devices) for i in range(devices)])
    gram = pl.pallas_call(
        gram_kernel,
        out_shape=jax.ShapeDtypeStruct((ROWS, width), F32),
        in_specs=[SMEM] + [VMEM] * 6,
        out_specs=VMEM,
        scratch_shapes=[split],
        compiler_params=params(24),
        cost_estimate=cost(1),
        name="gram",
    )(tab, aff, t0, t1, t2, t3, t4)
    parts = pl.pallas_call(
        cross_kernel,
        out_shape=jax.ShapeDtypeStruct((devices, ROWS, width), F32),
        in_specs=[SMEM] + [VMEM] * 4,
        out_specs=VMEM,
        compiler_params=params(8),
        name="cross",
    )(tab, aff, t4, recv, gram)
    parts = lax.all_to_all(parts, axis, 0, 0)
    return pl.pallas_call(
        final_kernel,
        out_shape=jax.ShapeDtypeStruct((count * rows, width), F32),
        in_specs=[VMEM] * 6,
        out_specs=VMEM,
        compiler_params=params(24),
        name="final",
    )(parts, t0, t1, t2, t3, t4)


def solution(mesh):
    return jax.shard_map(
        shards,
        mesh=mesh,
        in_specs=(
            P(("region", "dom"), None),
            P("region", None),
            P(("region", "dom"), None, None, None),
            P(("region", "dom"), None),
        ),
        out_specs=P(("region", "dom"), None),
        check_vma=False,
    )
```

```python
import functools

import jax
import jax.numpy as jnp
from jax import lax
from jax.experimental import pallas as pl
from jax.experimental.pallas import tpu as pltpu
from jax.sharding import PartitionSpec as P

HALO_W = 6
NAMED = 3
ITERATIONS = 5
DAMP = 0.99
SHIFTS = (0.0, 1.0, -0.25, 0.5)
PIVOT_MIN = 1e-6
BF = jnp.bfloat16
F32 = jnp.float32
PAIRS = [(i, j) for i in range(ITERATIONS) for j in range(i, ITERATIONS)]
ROWS = len(PAIRS) + 1
ENTRIES = 2 + 2 * NAMED

VMEM = pl.BlockSpec(memory_space=pltpu.VMEM)
SMEM = pl.BlockSpec(memory_space=pltpu.SMEM)
HBM = pl.BlockSpec(memory_space=pltpu.HBM)


def params(mib):
    return pltpu.CompilerParams(vmem_limit_bytes=mib << 20)


def dot(a, b):
    return jnp.dot(a, b, preferred_element_type=F32)


def dot_t(a, b):
    return lax.dot_general(a, b, (((0,), (0,)), ((), ())), preferred_element_type=F32)


def put_split(ref, index, value):
    high = value.astype(BF)
    width = value.shape[-1]
    ref[index, :, :width] = high
    ref[index, :, width:] = (value - high.astype(F32)).astype(BF)


def row_product(aff, tab, base, g, hl):
    count = aff.shape[0]
    width = hl.shape[2] // 2
    lower = hl[g - 1] if g > 0 else hl[tab[base + count]]
    upper = hl[g + 1] if g + 1 < count else hl[tab[base + count + 1]]
    left = jnp.concatenate([aff[g, 0], aff[g, 1]], axis=1)
    right = jnp.concatenate([hl[g], lower], axis=0)
    out = dot(left, right)
    left = jnp.concatenate([aff[g, 2], aff[g, 3]], axis=1)
    right = jnp.concatenate([upper, hl[tab[base + g]]], axis=0)
    out = out + dot(left, right)
    return out[:, :width] + out[:, width:]


def offsets(count):
    full = count + 2
    lists = 2 * full
    cross = lists + 3 * NAMED
    high = cross + 3 * ENTRIES
    return full, lists, cross, high, high + 3 * (1 + NAMED)


def fill_table(tile_col, tab, up_rows, low_rows, axis):
    count = tile_col.shape[1]
    total = count * lax.axis_size(axis)
    me = lax.axis_index(axis)
    even = lax.rem(me, 2) == 0
    full, lists, cross, high, _ = offsets(count)
    zero = count + 2 * NAMED
    up_base = jnp.where(even, 0, NAMED)
    low_base = NAMED - up_base
    relative, ups, lows = [], [], []
    up_mask = jnp.int32(1)
    low_mask = jnp.int32(1 << (HALO_W - 1))
    for g in range(count):
        rel = tile_col[3, g] - me * count
        rel = jnp.where(rel < 0, rel + total, rel)
        up = (rel >= count) & (rel < count + HALO_W)
        low = rel >= total - HALO_W
        place = jnp.where(up, rel - count, rel - (total - HALO_W))
        place = jnp.clip(place, 0, HALO_W - 1)
        bit = lax.shift_left(jnp.int32(1), place)
        up_mask = up_mask | jnp.where(up, bit, 0)
        low_mask = low_mask | jnp.where(low, bit, 0)
        relative.append((rel, place, bit))
        ups.append(up)
        lows.append(low)
    up_count = low_count = up_cross = low_cross = jnp.int32(0)
    for g in range(count):
        rel, place, bit = relative[g]
        below = jnp.where(ups[g], up_mask, low_mask) & (bit - 1)
        rank = below & 1
        for p in range(1, HALO_W - 1):
            rank = rank + (lax.shift_right_logical(below, jnp.int32(p)) & 1)
        halo = jnp.where(ups[g], up_base, low_base) + jnp.minimum(rank, NAMED - 1)
        local = rel < count
        tab[g] = jnp.where(local, rel, zero)
        tab[full + g] = jnp.where(local, rel, count + halo)
        up_rows[0, up_count] = g
        low_rows[0, low_count] = g
        up_rows[1, up_cross] = g
        low_rows[1, low_cross] = g
        up_rows[2, up_cross] = halo
        low_rows[2, low_cross] = halo
        up_cross = up_cross + jnp.where(ups[g], 1, 0)
        low_cross = low_cross + jnp.where(lows[g], 1, 0)
        up_count = up_count + (1 if g == count - 1 else jnp.where(ups[g], 1, 0))
        low_count = low_count + (1 if g == 0 else jnp.where(lows[g], 1, 0))
    tab[count] = zero
    tab[count + 1] = zero
    tab[full + count] = count + low_base + NAMED - 1
    tab[full + count + 1] = count + up_base
    for j in range(NAMED):
        up, low = up_rows[0, j], low_rows[0, j]
        tab[lists + j] = jnp.where(even, up, low)
        tab[lists + NAMED + j] = jnp.where(even, low, up)
        tab[lists + 2 * NAMED + j] = low
    chains = ((0, 1, low_base + NAMED - 1), (count - 1, 2, up_base))
    for side, (rows, used) in enumerate(((low_rows, low_cross), (up_rows, up_cross))):
        for i in range(3):
            tab[cross + 3 * side * (1 + NAMED) + i] = jnp.int32(chains[side][i])
        for j in range(NAMED):
            at = cross + 3 * (side * (1 + NAMED) + 1 + j)
            tab[at] = jnp.where(j < used, rows[1, j], count)
            tab[at + 1] = jnp.int32(3)
            tab[at + 2] = jnp.where(j < used, rows[2, j], 2 * NAMED)
    for j in range(1 + NAMED):
        at = cross + 3 * (1 + NAMED + j)
        tab[high + 3 * j] = tab[at]
        tab[high + 3 * j + 1] = tab[at + 1]
        tab[high + 3 * j + 2] = tab[at + 2] - up_base


def pack(tab, shift, t, y, send, base):
    for j in range(NAMED):
        g = tab[base + j]
        value = t[g]
        send[j] = value.astype(BF)
        send[NAMED + j] = (y[g] - shift * value).astype(BF)


def first_kernel(
    desc, queries, affinity, tile_col, t0, y0, send_a, send_b, aff, tab,
    hl, buf, wide, tall, cols, up_rows, low_rows, sems, *, chunks, axis,
):
    count, rows = t0.shape[0], t0.shape[1]
    per = count // chunks
    _, lists, _, _, _ = offsets(count)
    load_q = pltpu.make_async_copy(queries, wide, sems.at[chunks])
    load_c = pltpu.make_async_copy(tile_col, cols, sems.at[chunks + 1])
    load_q.start()
    load_c.start()
    copies = []
    for c in range(chunks):
        copy = pltpu.make_async_copy(
            desc.at[pl.ds(c * per * rows, per * rows)], buf.at[c], sems.at[c]
        )
        copy.start()
        copies.append(copy)
    load_a = pltpu.make_async_copy(affinity, aff, sems.at[chunks + 2])
    load_a.start()
    hl[count + 2 * NAMED] = jnp.zeros(hl.shape[1:], BF)
    load_q.wait()
    tall[...] = wide[...].T
    load_c.wait()
    fill_table(cols, tab, up_rows, low_rows, axis)
    for c in range(chunks):
        copies[c].wait()
        value = jnp.maximum(dot(buf[c], tall[...]), 0.0)
        value = value * value * value
        for i in range(per):
            block = value[i * rows : (i + 1) * rows]
            t0[c * per + i] = block
            put_split(hl, c * per + i, block)
    load_a.wait()
    for g in range(count):
        y0[g] = row_product(aff, tab, 0, g, hl)
    pack(tab, SHIFTS[0], t0, y0, send_b, lists + NAMED)
    pack(tab, SHIFTS[0], t0, y0, send_a, lists)


def two_steps(tab, aff, t, y, recv_a, recv_b, t1, t2, hl, hl2, acc, hacc, step):
    count, width = t.shape[0], t.shape[2]
    full, _, cross, _, _ = offsets(count)
    zero = count + 2 * NAMED
    hl[zero] = jnp.zeros(hl.shape[1:], BF)
    hl2[zero] = jnp.zeros(hl.shape[1:], BF)
    for h in range(NAMED):
        hl[count + h, :, :width] = recv_a[h]
        hl[count + NAMED + h, :, :width] = recv_b[h]
        hacc[h] = recv_a[NAMED + h].astype(F32)
        hacc[NAMED + h] = recv_b[NAMED + h].astype(F32)
    for g in range(count):
        acc[g] = y[g] - SHIFTS[step] * t[g]
    for e in range(ENTRIES):
        g, slot, h = (tab[cross + 3 * e + i] for i in range(3))
        row = jnp.minimum(g, count - 1)
        tile = aff[row, slot]
        acc[g] += dot(tile, hl[count + h, :, :width])
        hacc[h] += dot_t(tile, t[row].astype(BF))
    for g in range(count):
        value = acc[g]
        t1[g] = value
        put_split(hl, g, value)
    for h in range(2 * NAMED):
        put_split(hl, count + h, hacc[h])
    for g in range(count):
        value = row_product(aff, tab, full, g, hl) - SHIFTS[step + 1] * t1[g]
        t2[g] = value
        put_split(hl2, g, value)


def middle_kernel(
    tab, aff, t, y, recv_a, recv_b, t1, t2, y2, send_a, send_b, hl, hl2, acc, hacc
):
    _, lists, _, _, _ = offsets(t.shape[0])
    two_steps(tab, aff, t, y, recv_a, recv_b, t1, t2, hl, hl2, acc, hacc, 0)
    for g in range(t.shape[0]):
        y2[g] = row_product(aff, tab, 0, g, hl2)
    pack(tab, SHIFTS[2], t2, y2, send_b, lists + NAMED)
    pack(tab, SHIFTS[2], t2, y2, send_a, lists)


def last_kernel(tab, aff, t, y, recv_a, recv_b, t3, t4, send, hl, hl2, acc, hacc):
    _, lists, _, _, _ = offsets(t.shape[0])
    two_steps(tab, aff, t, y, recv_a, recv_b, t3, t4, hl, hl2, acc, hacc, 2)
    for j in range(NAMED):
        send[j] = t4[tab[lists + 2 * NAMED + j]].astype(BF)


def gram_kernel(tab, aff, t0, t1, t2, t3, t4, out, hl):
    count, rows, width = t0.shape
    hl[count + 2 * NAMED] = jnp.zeros(hl.shape[1:], BF)
    for g in range(count):
        put_split(hl, g, t4[g])
    fields = (t0, t1, t2, t3, t4)
    sums = [jnp.zeros((8, width), F32) for _ in range(ROWS)]
    for g in range(count):
        local = row_product(aff, tab, 0, g, hl)
        sums[-1] = sums[-1] + (t4[g] * local).reshape(rows // 8, 8, width).sum(0)

    def body(i, sums):
        sums = list(sums)
        g = i // (rows // 32)
        start = pl.multiple_of((i % (rows // 32)) * 32, 32)
        for part in range(4):
            v = [f[g, pl.ds(pl.multiple_of(start + 8 * part, 8), 8), :] for f in fields]
            for n, (a, b) in enumerate(PAIRS):
                sums[n] = sums[n] + v[a] * v[b]
        return tuple(sums)

    sums = lax.fori_loop(0, count * rows // 32, body, tuple(sums))
    for n in range(ROWS):
        out[pl.ds(n, 1), :] = jnp.sum(sums[n], axis=0, keepdims=True)


def cross_kernel(tab, aff, t4, recv, gram, out):
    count = t4.shape[0]
    _, _, _, high, _ = offsets(count)
    total = jnp.zeros((8, gram.shape[1]), F32)
    for e in range(1 + NAMED):
        g, slot, h = (tab[high + 3 * e + i] for i in range(3))
        row = jnp.minimum(g, count - 1)
        part = t4[row] * dot(aff[row, slot], recv[jnp.minimum(h, NAMED - 1)])
        part = part.reshape(-1, 8, part.shape[-1]).sum(0)
        total = total + jnp.where(g < count, part, 0.0)
    value = gram[...]
    extra = 2.0 * jnp.sum(total, axis=0, keepdims=True)
    index = lax.broadcasted_iota(jnp.int32, value.shape, 0)
    value = value + jnp.where(index == ROWS - 1, extra, 0.0)
    for d in range(out.shape[0]):
        out[d] = value


def final_kernel(parts, t0, t1, t2, t3, t4, out):
    n = ITERATIONS
    value = parts[0]
    for d in range(1, parts.shape[0]):
        value = value + parts[d]
    gram = {}
    for k, (i, j) in enumerate(PAIRS):
        gram[i, j] = gram[j, i] = value[k : k + 1]
    matrix = {}
    for i in range(n):
        for j in range(i, n):
            terms = []
            if j + 1 < n:
                terms.append(gram[i, j + 1] + SHIFTS[j] * gram[i, j])
            if i + 1 < n and i != j:
                terms.append(gram[i + 1, j] + SHIFTS[i] * gram[i, j])
            if not terms:
                terms = [value[ROWS - 1 : ROWS]]
            product = terms[0] if len(terms) == 1 else 0.5 * (terms[0] + terms[1])
            matrix[i, j] = gram[i, j] - DAMP * product
    scale = [
        jnp.where(matrix[i, i] > 0.0, lax.rsqrt(jnp.maximum(matrix[i, i], 1e-37)), 0.0)
        for i in range(n)
    ]
    for i in range(n):
        for j in range(i, n):
            matrix[i, j] = matrix[i, j] * (scale[i] * scale[j])
    right = [gram[i, 0] * scale[i] for i in range(n)]
    inverse = []
    for k in range(n):
        pivot = matrix[k, k]
        inverse.append(jnp.where(pivot > PIVOT_MIN, 1.0 / jnp.maximum(pivot, PIVOT_MIN), 0.0))
        for i in range(k + 1, n):
            factor = matrix[k, i] * inverse[k]
            for j in range(i, n):
                matrix[i, j] = matrix[i, j] - factor * matrix[k, j]
            right[i] = right[i] - factor * right[k]
    coef = [None] * n
    for k in range(n - 1, -1, -1):
        rest = right[k]
        for j in range(k + 1, n):
            rest = rest - matrix[k, j] * coef[j]
        coef[k] = rest * inverse[k]
    coef = [coef[k] * scale[k] for k in range(n)]
    fields = (t0, t1, t2, t3, t4)
    count, rows, width = t0.shape
    wide = [jnp.broadcast_to(c, (8, width)) for c in coef]
    for g in range(count):
        total = None
        for f, c in zip(fields, coef):
            term = f[g] * c
            total = term if total is None else total + term
        out[pl.ds(g * rows, rows), :] = total


def swap(block_a, block_b, axis):
    n = lax.axis_size(axis)
    pairs_a = [(i, i ^ 1) for i in range(n)]
    pairs_b = [(i, (i + 1) % n if i % 2 else (i - 1) % n) for i in range(n)]
    got_b = lax.ppermute(block_b, axis, pairs_b)
    got_a = lax.ppermute(block_a, axis, pairs_a)
    return got_a, got_b


def shards(descriptors, queries, affinity, tile_col):
    count, _, rows, _ = affinity.shape
    width = queries.shape[0]
    depth = descriptors.shape[1]
    axis = "dom"
    devices = lax.axis_size(axis)
    size = 128 * pl.cdiv(offsets(count)[-1], 128)
    blocks = count + 2 * NAMED + 1
    field = jax.ShapeDtypeStruct((count, rows, width), F32)
    edge = jax.ShapeDtypeStruct((2 * NAMED, rows, width), BF)
    half = jax.ShapeDtypeStruct((NAMED, rows, width), BF)
    split = pltpu.VMEM((blocks, rows, 2 * width), BF)
    work = [
        split,
        split,
        pltpu.VMEM((count + 1, rows, width), F32),
        pltpu.VMEM((2 * NAMED + 1, rows, width), F32),
    ]
    chunks = 4
    flops = 2 * count * rows * 4 * rows * 2 * width

    def cost(products, extra=0, bytes_accessed=4 << 20):
        return pl.CostEstimate(
            flops=products * flops + extra, bytes_accessed=bytes_accessed, transcendentals=0
        )

    t0, y0, send_a, send_b, aff, tab = pl.pallas_call(
        functools.partial(first_kernel, chunks=chunks, axis=axis),
        out_shape=(
            field,
            field,
            edge,
            edge,
            jax.ShapeDtypeStruct(affinity.shape, BF),
            jax.ShapeDtypeStruct((size,), jnp.int32),
        ),
        in_specs=[HBM] * 4,
        out_specs=(VMEM,) * 5 + (SMEM,),
        scratch_shapes=[
            split,
            pltpu.VMEM((chunks, count * rows // chunks, depth), BF),
            pltpu.VMEM((width, depth), BF),
            pltpu.VMEM((depth, width), BF),
            pltpu.SMEM((4, count), jnp.int32),
            pltpu.SMEM((3, count + 1), jnp.int32),
            pltpu.SMEM((3, count + 1), jnp.int32),
            pltpu.SemaphoreType.DMA((chunks + 3,)),
        ],
        compiler_params=params(24),
        cost_estimate=cost(1, 2 * count * rows * depth * width),
        name="first",
    )(*(pltpu.with_memory_space_constraint(x, pltpu.HBM) for x in (descriptors, queries, affinity, tile_col.T)))
    recv_a, recv_b = swap(send_a, send_b, axis)
    t1, t2, y2, send_a, send_b = pl.pallas_call(
        middle_kernel,
        out_shape=(field, field, field, edge, edge),
        in_specs=[SMEM] + [VMEM] * 5,
        out_specs=(VMEM,) * 5,
        scratch_shapes=work,
        compiler_params=params(24),
        cost_estimate=cost(2),
        name="middle",
    )(tab, aff, t0, y0, recv_a, recv_b)
    recv_a, recv_b = swap(send_a, send_b, axis)
    t3, t4, send = pl.pallas_call(
        last_kernel,
        out_shape=(field, field, half),
        in_specs=[SMEM] + [VMEM] * 5,
        out_specs=(VMEM,) * 3,
        scratch_shapes=work,
        compiler_params=params(24),
        cost_estimate=cost(2),
        name="last",
    )(tab, aff, t2, y2, recv_a, recv_b)
    recv = lax.ppermute(send, axis, [(i, (i - 1) % devices) for i in range(devices)])
    gram = pl.pallas_call(
        gram_kernel,
        out_shape=jax.ShapeDtypeStruct((ROWS, width), F32),
        in_specs=[SMEM] + [VMEM] * 6,
        out_specs=VMEM,
        scratch_shapes=[split],
        compiler_params=params(24),
        cost_estimate=cost(1),
        name="gram",
    )(tab, aff, t0, t1, t2, t3, t4)
    parts = pl.pallas_call(
        cross_kernel,
        out_shape=jax.ShapeDtypeStruct((devices, ROWS, width), F32),
        in_specs=[SMEM] + [VMEM] * 4,
        out_specs=VMEM,
        compiler_params=params(8),
        name="cross",
    )(tab, aff, t4, recv, gram)
    parts = lax.all_to_all(parts, axis, 0, 0)
    return pl.pallas_call(
        final_kernel,
        out_shape=jax.ShapeDtypeStruct((count * rows, width), F32),
        in_specs=[VMEM] * 6,
        out_specs=VMEM,
        compiler_params=params(24),
        name="final",
    )(parts, t0, t1, t2, t3, t4)


def solution(mesh):
    return jax.shard_map(
        shards,
        mesh=mesh,
        in_specs=(
            P(("region", "dom"), None),
            P("region", None),
            P(("region", "dom"), None, None, None),
            P(("region", "dom"), None),
        ),
        out_specs=P(("region", "dom"), None),
        check_vma=False,
    )
```

```python
import functools

import jax
import jax.numpy as jnp
from jax import lax
from jax.experimental import pallas as pl
from jax.experimental.pallas import tpu as pltpu
from jax.sharding import PartitionSpec as P

HALO_W = 6
NAMED = 3
ITERATIONS = 5
DAMP = 0.99
SHIFTS = (0.0, 1.0, -0.25, 0.5)
PIVOT_MIN = 1e-6
BF = jnp.bfloat16
F32 = jnp.float32
EARLY = [(i, j) for i in range(3) for j in range(i, 3)]
LATE = [(i, j) for j in range(3, ITERATIONS) for i in range(j + 1)]
PAIRS = EARLY + LATE
ROWS = len(PAIRS) + 1
ENTRIES = 2 + 2 * NAMED

VMEM = pl.BlockSpec(memory_space=pltpu.VMEM)
SMEM = pl.BlockSpec(memory_space=pltpu.SMEM)
HBM = pl.BlockSpec(memory_space=pltpu.HBM)


def params(mib):
    return pltpu.CompilerParams(vmem_limit_bytes=mib << 20)


def dot(a, b):
    return jnp.dot(a, b, preferred_element_type=F32)


def dot_t(a, b):
    return lax.dot_general(a, b, (((0,), (0,)), ((), ())), preferred_element_type=F32)


def put_split(ref, index, value):
    high = value.astype(BF)
    width = value.shape[-1]
    ref[index, :, :width] = high
    ref[index, :, width:] = (value - high.astype(F32)).astype(BF)


def row_product(aff, tab, base, g, hl):
    count = aff.shape[0]
    width = hl.shape[2] // 2
    if isinstance(g, int):
        low = g - 1 if g > 0 else tab[base + count]
        high = g + 1 if g + 1 < count else tab[base + count + 1]
    else:
        low = jnp.where(g > 0, g - 1, tab[base + count])
        high = jnp.where(g + 1 < count, g + 1, tab[base + count + 1])
    left = jnp.concatenate([aff[g, 0], aff[g, 1]], axis=1)
    right = jnp.concatenate([hl[g], hl[low]], axis=0)
    out = dot(left, right)
    left = jnp.concatenate([aff[g, 2], aff[g, 3]], axis=1)
    right = jnp.concatenate([hl[high], hl[tab[base + g]]], axis=0)
    out = out + dot(left, right)
    return out[:, :width] + out[:, width:]


def shifted(value, shift, t):
    return value if shift == 0.0 else value - shift * t


def offsets(count):
    full = count + 2
    lists = 2 * full
    cross = lists + 3 * NAMED
    high = cross + 3 * ENTRIES
    return full, lists, cross, high, high + 3 * (1 + NAMED)


def fill_table(tile_col, tab, up_rows, low_rows, axis):
    count = tile_col.shape[1]
    total = count * lax.axis_size(axis)
    me = lax.axis_index(axis)
    even = lax.rem(me, 2) == 0
    full, lists, cross, high, _ = offsets(count)
    zero = count + 2 * NAMED
    up_base = jnp.where(even, 0, NAMED)
    low_base = NAMED - up_base
    relative, ups, lows = [], [], []
    up_mask = jnp.int32(1)
    low_mask = jnp.int32(1 << (HALO_W - 1))
    for g in range(count):
        rel = tile_col[3, g] - me * count
        rel = jnp.where(rel < 0, rel + total, rel)
        up = (rel >= count) & (rel < count + HALO_W)
        low = rel >= total - HALO_W
        place = jnp.where(up, rel - count, rel - (total - HALO_W))
        place = jnp.clip(place, 0, HALO_W - 1)
        bit = lax.shift_left(jnp.int32(1), place)
        up_mask = up_mask | jnp.where(up, bit, 0)
        low_mask = low_mask | jnp.where(low, bit, 0)
        relative.append((rel, place, bit))
        ups.append(up)
        lows.append(low)
    up_count = low_count = up_cross = low_cross = jnp.int32(0)
    for g in range(count):
        rel, place, bit = relative[g]
        below = jnp.where(ups[g], up_mask, low_mask) & (bit - 1)
        rank = below & 1
        for p in range(1, HALO_W - 1):
            rank = rank + (lax.shift_right_logical(below, jnp.int32(p)) & 1)
        halo = jnp.where(ups[g], up_base, low_base) + jnp.minimum(rank, NAMED - 1)
        local = rel < count
        tab[g] = jnp.where(local, rel, zero)
        tab[full + g] = jnp.where(local, rel, count + halo)
        up_rows[0, up_count] = g
        low_rows[0, low_count] = g
        up_rows[1, up_cross] = g
        low_rows[1, low_cross] = g
        up_rows[2, up_cross] = halo
        low_rows[2, low_cross] = halo
        up_cross = up_cross + jnp.where(ups[g], 1, 0)
        low_cross = low_cross + jnp.where(lows[g], 1, 0)
        up_count = up_count + (1 if g == count - 1 else jnp.where(ups[g], 1, 0))
        low_count = low_count + (1 if g == 0 else jnp.where(lows[g], 1, 0))
    tab[count] = zero
    tab[count + 1] = zero
    tab[full + count] = count + low_base + NAMED - 1
    tab[full + count + 1] = count + up_base
    for j in range(NAMED):
        up, low = up_rows[0, j], low_rows[0, j]
        tab[lists + j] = jnp.where(even, up, low)
        tab[lists + NAMED + j] = jnp.where(even, low, up)
        tab[lists + 2 * NAMED + j] = low
    chains = ((0, 1, low_base + NAMED - 1), (count - 1, 2, up_base))
    for side, (rows, used) in enumerate(((low_rows, low_cross), (up_rows, up_cross))):
        for i in range(3):
            tab[cross + 3 * side * (1 + NAMED) + i] = jnp.int32(chains[side][i])
        for j in range(NAMED):
            at = cross + 3 * (side * (1 + NAMED) + 1 + j)
            tab[at] = jnp.where(j < used, rows[1, j], 0)
            tab[at + 1] = jnp.int32(3)
            tab[at + 2] = jnp.where(j < used, rows[2, j], 2 * NAMED)
    for j in range(1 + NAMED):
        at = cross + 3 * (1 + NAMED + j)
        tab[high + 3 * j] = tab[at]
        tab[high + 3 * j + 1] = tab[at + 1]
        tab[high + 3 * j + 2] = jnp.where(tab[at + 2] < 2 * NAMED, tab[at + 2] - up_base, NAMED)


def pack(tab, shift, aff, t, hl, send, base):
    width = t.shape[2]
    for j in range(NAMED):
        g = tab[base + j]
        send[j] = hl[g, :, :width]
        send[NAMED + j] = shifted(row_product(aff, tab, 0, g, hl), shift, t[g]).astype(BF)


def first_kernel(
    desc, queries, affinity, tile_col, t0, hl, send_a, send_b, aff, tab,
    buf, wide, tall, cols, up_rows, low_rows, sems, *, chunks, axis,
):
    count, rows = t0.shape[0], t0.shape[1]
    per = count // chunks
    _, lists, _, _, _ = offsets(count)
    load_q = pltpu.make_async_copy(queries, wide, sems.at[chunks])
    load_c = pltpu.make_async_copy(tile_col, cols, sems.at[chunks + 1])
    load_q.start()
    load_c.start()
    copies = []
    for c in range(chunks):
        copy = pltpu.make_async_copy(
            desc.at[pl.ds(c * per * rows, per * rows)], buf.at[c], sems.at[c]
        )
        copy.start()
        copies.append(copy)
    load_a = pltpu.make_async_copy(affinity, aff, sems.at[chunks + 2])
    load_a.start()
    hl[count + 2 * NAMED] = jnp.zeros(hl.shape[1:], BF)
    load_q.wait()
    tall[...] = wide[...].T
    load_c.wait()
    for c in range(chunks):
        copies[c].wait()
        if c == 0:
            fill_table(cols, tab, up_rows, low_rows, axis)
        value = jnp.maximum(dot(buf[c], tall[...]), 0.0)
        value = value * value * value
        for i in range(per):
            block = value[i * rows : (i + 1) * rows]
            t0[c * per + i] = block
            put_split(hl, c * per + i, block)
    load_a.wait()
    pack(tab, SHIFTS[0], aff, t0, hl, send_b, lists + NAMED)
    pack(tab, SHIFTS[0], aff, t0, hl, send_a, lists)


def add_products(sums, pairs, fields):
    count, rows, _ = fields[0].shape
    group = 32

    def body(i, sums):
        sums = list(sums)
        g = i // (rows // group)
        start = (i % (rows // group)) * group
        for part in range(group // 8):
            at = pl.ds(pl.multiple_of(start + 8 * part, 8), 8)
            v = [f[g, at, :] for f in fields]
            for n, (a, b) in enumerate(pairs):
                sums[n] = sums[n] + v[a] * v[b]
        return tuple(sums)

    return list(lax.fori_loop(0, count * rows // group, body, tuple(sums)))


def rest_kernel(tab, aff, t, hl, *refs, step):
    count = t.shape[0]
    fields, (part, hl_next, *gram) = refs[: 2 * (step > 0)], refs[2 * (step > 0) :]
    hl_next[count + 2 * NAMED] = jnp.zeros(hl.shape[1:], BF)
    for g in range(count):
        value = shifted(row_product(aff, tab, 0, g, hl), SHIFTS[step], t[g])
        part[g] = value
        put_split(hl_next, g, value)
    if gram:
        width = t.shape[2]
        sums = [jnp.zeros((8, width), F32) for _ in EARLY]
        sums = add_products(sums, EARLY, (*fields, t))
        for n, total in enumerate(sums):
            gram[0][pl.ds(n, 1), :] = jnp.sum(total, axis=0, keepdims=True)


def two_steps(tab, aff, hl, hl1, t1, recv_a, recv_b, t2, hl2, halo, hacc, step):
    count, _, width = t2.shape
    full, lists, cross, _, _ = offsets(count)
    halo[2 * NAMED] = jnp.zeros(halo.shape[1:], BF)
    hacc[2 * NAMED] = jnp.zeros(hacc.shape[1:], F32)
    for h in range(NAMED):
        halo[h] = recv_a[h]
        halo[NAMED + h] = recv_b[h]
        hacc[h] = recv_a[NAMED + h].astype(F32)
        hacc[NAMED + h] = recv_b[NAMED + h].astype(F32)
    for e in range(ENTRIES):
        g, slot, h = (tab[cross + 3 * e + i] for i in range(3))
        tile = aff[g, slot]
        t1[g] += dot(tile, halo[h])
        hacc[h] += dot_t(tile, hl[g, :, :width])
    for j in range(2 * NAMED):
        g = tab[lists + j]
        put_split(hl1, g, t1[g])
    for h in range(2 * NAMED):
        put_split(hl1, count + h, hacc[h])
    for g in range(count):
        value = shifted(row_product(aff, tab, full, g, hl1), SHIFTS[step + 1], t1[g])
        t2[g] = value
        put_split(hl2, g, value)


def middle_kernel(
    tab, aff, hl, _, __, recv_a, recv_b, hl1, t1, t2, hl2, send_a, send_b, halo, hacc
):
    _, lists, _, _, _ = offsets(t1.shape[0])
    hl2[t1.shape[0] + 2 * NAMED] = jnp.zeros(hl2.shape[1:], BF)
    two_steps(tab, aff, hl, hl1, t1, recv_a, recv_b, t2, hl2, halo, hacc, 0)
    pack(tab, SHIFTS[2], aff, t2, hl2, send_b, lists + NAMED)
    pack(tab, SHIFTS[2], aff, t2, hl2, send_a, lists)


def last_kernel(tab, aff, hl, _, __, recv_a, recv_b, hl3, t3, t4, hl4, send, halo, hacc):
    count, _, width = t3.shape
    _, lists, _, _, _ = offsets(count)
    hl4[count + 2 * NAMED] = jnp.zeros(hl4.shape[1:], BF)
    two_steps(tab, aff, hl, hl3, t3, recv_a, recv_b, t4, hl4, halo, hacc, 2)
    for j in range(NAMED):
        send[j] = hl4[tab[lists + 2 * NAMED + j], :, :width]


def gram_kernel(tab, aff, t0, t1, t2, t3, t4, hl, early, out):
    count, rows, width = t0.shape
    sums = [jnp.zeros((8, width), F32) for _ in LATE]
    last = jnp.zeros((8, width), F32)
    for g in range(count):
        local = row_product(aff, tab, 0, g, hl)
        last = last + (t4[g] * local).reshape(rows // 8, 8, width).sum(0)
    sums = add_products(sums, LATE, (t0, t1, t2, t3, t4)) + [last]
    out[pl.ds(0, len(EARLY)), :] = early[...]
    for n, total in enumerate(sums):
        out[pl.ds(len(EARLY) + n, 1), :] = jnp.sum(total, axis=0, keepdims=True)


def cross_kernel(tab, aff, t4, recv, gram, out):
    count = t4.shape[0]
    _, _, _, high, _ = offsets(count)
    total = jnp.zeros((8, gram.shape[1]), F32)
    for e in range(1 + NAMED):
        g, slot, h = (tab[high + 3 * e + i] for i in range(3))
        part = t4[g] * dot(aff[g, slot], recv[jnp.minimum(h, NAMED - 1)])
        part = part.reshape(-1, 8, part.shape[-1]).sum(0)
        total = total + jnp.where(h < NAMED, part, 0.0)
    value = gram[...]
    extra = 2.0 * jnp.sum(total, axis=0, keepdims=True)
    index = lax.broadcasted_iota(jnp.int32, value.shape, 0)
    value = value + jnp.where(index == ROWS - 1, extra, 0.0)
    for d in range(out.shape[0]):
        out[d] = value


def final_kernel(parts, t0, t1, t2, t3, t4, out):
    n = ITERATIONS
    value = parts[0]
    for d in range(1, parts.shape[0]):
        value = value + parts[d]
    gram = {}
    for k, (i, j) in enumerate(PAIRS):
        gram[i, j] = gram[j, i] = value[k : k + 1]
    matrix = {}
    for i in range(n):
        for j in range(i, n):
            terms = []
            if j + 1 < n:
                terms.append(gram[i, j + 1] + SHIFTS[j] * gram[i, j])
            if i + 1 < n and i != j:
                terms.append(gram[i + 1, j] + SHIFTS[i] * gram[i, j])
            if not terms:
                terms = [value[ROWS - 1 : ROWS]]
            product = terms[0] if len(terms) == 1 else 0.5 * (terms[0] + terms[1])
            matrix[i, j] = gram[i, j] - DAMP * product
    scale = [
        jnp.where(matrix[i, i] > 0.0, lax.rsqrt(jnp.maximum(matrix[i, i], 1e-37)), 0.0)
        for i in range(n)
    ]
    for i in range(n):
        for j in range(i, n):
            matrix[i, j] = matrix[i, j] * (scale[i] * scale[j])
    right = [gram[i, 0] * scale[i] for i in range(n)]
    inverse = []
    for k in range(n):
        pivot = matrix[k, k]
        inverse.append(jnp.where(pivot > PIVOT_MIN, 1.0 / jnp.maximum(pivot, PIVOT_MIN), 0.0))
        for i in range(k + 1, n):
            factor = matrix[k, i] * inverse[k]
            for j in range(i, n):
                matrix[i, j] = matrix[i, j] - factor * matrix[k, j]
            right[i] = right[i] - factor * right[k]
    coef = [None] * n
    for k in range(n - 1, -1, -1):
        rest = right[k]
        for j in range(k + 1, n):
            rest = rest - matrix[k, j] * coef[j]
        coef[k] = rest * inverse[k]
    coef = [coef[k] * scale[k] for k in range(n)]
    fields = (t0, t1, t2, t3, t4)
    count, rows, width = t0.shape
    wide = [jnp.broadcast_to(c, (8, width)) for c in coef]
    for g in range(count):
        total = None
        for f, c in zip(fields, coef):
            term = f[g] * c
            total = term if total is None else total + term
        out[pl.ds(g * rows, rows), :] = total


def swap(block_a, block_b, axis):
    n = lax.axis_size(axis)
    pairs_a = [(i, i ^ 1) for i in range(n)]
    pairs_b = [(i, (i + 1) % n if i % 2 else (i - 1) % n) for i in range(n)]
    got_b = lax.ppermute(block_b, axis, pairs_b)
    got_a = lax.ppermute(block_a, axis, pairs_a)
    return got_a, got_b


def shards(descriptors, queries, affinity, tile_col):
    count, _, rows, _ = affinity.shape
    width = queries.shape[0]
    depth = descriptors.shape[1]
    axis = "dom"
    devices = lax.axis_size(axis)
    size = 128 * pl.cdiv(offsets(count)[-1], 128)
    blocks = count + 2 * NAMED + 1
    field = jax.ShapeDtypeStruct((count, rows, width), F32)
    split = jax.ShapeDtypeStruct((blocks, rows, 2 * width), BF)
    edge = jax.ShapeDtypeStruct((2 * NAMED, rows, width), BF)
    half = jax.ShapeDtypeStruct((NAMED, rows, width), BF)
    early = jax.ShapeDtypeStruct((len(EARLY), width), F32)
    work = [
        pltpu.VMEM((2 * NAMED + 1, rows, width), BF),
        pltpu.VMEM((2 * NAMED + 1, rows, width), F32),
    ]
    chunks = count // 2
    flops = 2 * count * rows * 4 * rows * 2 * width

    def call(kernel, out_shape, products, scratch=(), aliases=None, name=None, limit=24):
        outs = out_shape if isinstance(out_shape, tuple) else (out_shape,)

        def run(*args):
            specs = [SMEM if x.dtype == jnp.int32 else VMEM for x in args]
            return pl.pallas_call(
                kernel,
                out_shape=out_shape,
                in_specs=specs,
                out_specs=(VMEM,) * len(outs) if isinstance(out_shape, tuple) else VMEM,
                scratch_shapes=list(scratch),
                input_output_aliases=aliases or {},
                compiler_params=params(limit),
                cost_estimate=pl.CostEstimate(
                    flops=int(products * flops), bytes_accessed=4 << 20, transcendentals=0
                ),
                name=name,
            )(*args)

        return run

    operands = (descriptors, queries, affinity, tile_col.T)
    t0, hl0, send_a, send_b, aff, tab = pl.pallas_call(
        functools.partial(first_kernel, chunks=chunks, axis=axis),
        out_shape=(
            field,
            split,
            edge,
            edge,
            jax.ShapeDtypeStruct(affinity.shape, BF),
            jax.ShapeDtypeStruct((size,), jnp.int32),
        ),
        in_specs=[HBM] * 4,
        out_specs=(VMEM,) * 5 + (SMEM,),
        scratch_shapes=[
            pltpu.VMEM((chunks, count * rows // chunks, depth), BF),
            pltpu.VMEM((width, depth), BF),
            pltpu.VMEM((depth, width), BF),
            pltpu.SMEM((4, count), jnp.int32),
            pltpu.SMEM((3, count + 1), jnp.int32),
            pltpu.SMEM((3, count + 1), jnp.int32),
            pltpu.SemaphoreType.DMA((chunks + 3,)),
        ],
        compiler_params=params(24),
        cost_estimate=pl.CostEstimate(flops=flops, bytes_accessed=4 << 20, transcendentals=0),
        name="first",
    )(*(pltpu.with_memory_space_constraint(x, pltpu.HBM) for x in operands))
    recv_a, recv_b = swap(send_a, send_b, axis)
    part, hl1 = call(
        functools.partial(rest_kernel, step=0), (field, split), 1, name="rest0"
    )(tab, aff, t0, hl0)
    _, t1, t2, hl2, send_a, send_b = call(
        middle_kernel,
        (split, field, field, split, edge, edge),
        2,
        work,
        {3: 0, 4: 1},
        name="middle",
    )(tab, aff, hl0, hl1, part, recv_a, recv_b)
    recv_a, recv_b = swap(send_a, send_b, axis)
    part, hl3, gram = call(
        functools.partial(rest_kernel, step=2), (field, split, early), 1, name="rest2"
    )(tab, aff, t2, hl2, t0, t1)
    _, t3, t4, hl4, send = call(
        last_kernel,
        (split, field, field, split, half),
        2,
        work,
        {3: 0, 4: 1},
        name="last",
    )(tab, aff, hl2, hl3, part, recv_a, recv_b)
    recv = lax.ppermute(send, axis, [(i, (i - 1) % devices) for i in range(devices)])
    gram = call(
        gram_kernel, jax.ShapeDtypeStruct((ROWS, width), F32), 1, name="gram"
    )(tab, aff, t0, t1, t2, t3, t4, hl4, gram)
    parts = call(
        cross_kernel,
        jax.ShapeDtypeStruct((devices, ROWS, width), F32),
        0.1,
        name="cross",
        limit=8,
    )(tab, aff, t4, recv, gram)
    parts = lax.all_to_all(parts, axis, 0, 0)
    return call(
        final_kernel, jax.ShapeDtypeStruct((count * rows, width), F32), 0.1, name="final"
    )(parts, t0, t1, t2, t3, t4)


def solution(mesh):
    return jax.shard_map(
        shards,
        mesh=mesh,
        in_specs=(
            P(("region", "dom"), None),
            P("region", None),
            P(("region", "dom"), None, None, None),
            P(("region", "dom"), None),
        ),
        out_specs=P(("region", "dom"), None),
        check_vma=False,
    )
```

```python
import functools

import jax
import jax.numpy as jnp
from jax import lax
from jax.experimental import pallas as pl
from jax.experimental.pallas import tpu as pltpu
from jax.sharding import PartitionSpec as P

HALO_W = 6
NAMED = 3
ITERATIONS = 5
DAMP = 0.99
SHIFTS = (0.0, 1.0, -0.25, 0.5)
PIVOT_MIN = 1e-6
BF = jnp.bfloat16
F32 = jnp.float32
EARLY = [(i, j) for i in range(3) for j in range(i, 3)]
LATE = [(i, j) for j in range(3, ITERATIONS) for i in range(j + 1)]
PAIRS = EARLY + LATE
ROWS = len(PAIRS) + 1
ENTRIES = 2 + 2 * NAMED

VMEM = pl.BlockSpec(memory_space=pltpu.VMEM)
SMEM = pl.BlockSpec(memory_space=pltpu.SMEM)
HBM = pl.BlockSpec(memory_space=pltpu.HBM)


def params(mib):
    return pltpu.CompilerParams(vmem_limit_bytes=mib << 20)


def dot(a, b):
    return jnp.dot(a, b, preferred_element_type=F32)


def dot_t(a, b):
    return lax.dot_general(a, b, (((0,), (0,)), ((), ())), preferred_element_type=F32)


def put_split(ref, index, value):
    high = value.astype(BF)
    width = value.shape[-1]
    ref[index, :, :width] = high
    ref[index, :, width:] = (value - high.astype(F32)).astype(BF)


def row_product(aff, tab, base, g, hl):
    count = aff.shape[0]
    width = hl.shape[2] // 2
    if isinstance(g, int):
        low = g - 1 if g > 0 else tab[base + count]
        high = g + 1 if g + 1 < count else tab[base + count + 1]
    else:
        low = jnp.where(g > 0, g - 1, tab[base + count])
        high = jnp.where(g + 1 < count, g + 1, tab[base + count + 1])
    left = jnp.concatenate([aff[g, 0], aff[g, 1]], axis=1)
    right = jnp.concatenate([hl[g], hl[low]], axis=0)
    out = dot(left, right)
    left = jnp.concatenate([aff[g, 2], aff[g, 3]], axis=1)
    right = jnp.concatenate([hl[high], hl[tab[base + g]]], axis=0)
    out = out + dot(left, right)
    return out[:, :width] + out[:, width:]


def shifted(value, shift, t):
    return value if shift == 0.0 else value - shift * t


def offsets(count):
    full = count + 2
    lists = 2 * full
    cross = lists + 3 * NAMED
    high = cross + 3 * ENTRIES
    return full, lists, cross, high, high + 3 * (1 + NAMED)


def fill_table(tile_col, tab, up_rows, low_rows, axis):
    count = tile_col.shape[1]
    total = count * lax.axis_size(axis)
    me = lax.axis_index(axis)
    even = lax.rem(me, 2) == 0
    full, lists, cross, high, _ = offsets(count)
    zero = count + 2 * NAMED
    up_base = jnp.where(even, 0, NAMED)
    low_base = NAMED - up_base
    relative, ups, lows = [], [], []
    up_mask = jnp.int32(1)
    low_mask = jnp.int32(1 << (HALO_W - 1))
    for g in range(count):
        rel = tile_col[3, g] - me * count
        rel = jnp.where(rel < 0, rel + total, rel)
        up = (rel >= count) & (rel < count + HALO_W)
        low = rel >= total - HALO_W
        place = jnp.where(up, rel - count, rel - (total - HALO_W))
        place = jnp.clip(place, 0, HALO_W - 1)
        bit = lax.shift_left(jnp.int32(1), place)
        up_mask = up_mask | jnp.where(up, bit, 0)
        low_mask = low_mask | jnp.where(low, bit, 0)
        relative.append((rel, place, bit))
        ups.append(up)
        lows.append(low)
    up_count = low_count = up_cross = low_cross = jnp.int32(0)
    for g in range(count):
        rel, place, bit = relative[g]
        below = jnp.where(ups[g], up_mask, low_mask) & (bit - 1)
        rank = below & 1
        for p in range(1, HALO_W - 1):
            rank = rank + (lax.shift_right_logical(below, jnp.int32(p)) & 1)
        halo = jnp.where(ups[g], up_base, low_base) + jnp.minimum(rank, NAMED - 1)
        local = rel < count
        tab[g] = jnp.where(local, rel, zero)
        tab[full + g] = jnp.where(local, rel, count + halo)
        up_rows[0, up_count] = g
        low_rows[0, low_count] = g
        up_rows[1, up_cross] = g
        low_rows[1, low_cross] = g
        up_rows[2, up_cross] = halo
        low_rows[2, low_cross] = halo
        up_cross = up_cross + jnp.where(ups[g], 1, 0)
        low_cross = low_cross + jnp.where(lows[g], 1, 0)
        up_count = up_count + (1 if g == count - 1 else jnp.where(ups[g], 1, 0))
        low_count = low_count + (1 if g == 0 else jnp.where(lows[g], 1, 0))
    tab[count] = zero
    tab[count + 1] = zero
    tab[full + count] = count + low_base + NAMED - 1
    tab[full + count + 1] = count + up_base
    for j in range(NAMED):
        up, low = up_rows[0, j], low_rows[0, j]
        tab[lists + j] = jnp.where(even, up, low)
        tab[lists + NAMED + j] = jnp.where(even, low, up)
        tab[lists + 2 * NAMED + j] = low
    chains = ((0, 1, low_base + NAMED - 1), (count - 1, 2, up_base))
    for side, (rows, used) in enumerate(((low_rows, low_cross), (up_rows, up_cross))):
        for i in range(3):
            tab[cross + 3 * side * (1 + NAMED) + i] = jnp.int32(chains[side][i])
        for j in range(NAMED):
            at = cross + 3 * (side * (1 + NAMED) + 1 + j)
            tab[at] = jnp.where(j < used, rows[1, j], 0)
            tab[at + 1] = jnp.int32(3)
            tab[at + 2] = jnp.where(j < used, rows[2, j], 2 * NAMED)
    for j in range(1 + NAMED):
        at = cross + 3 * (1 + NAMED + j)
        tab[high + 3 * j] = tab[at]
        tab[high + 3 * j + 1] = tab[at + 1]
        tab[high + 3 * j + 2] = jnp.where(tab[at + 2] < 2 * NAMED, tab[at + 2] - up_base, NAMED)


def pack(tab, shift, aff, t, hl, send, base):
    width = t.shape[2]
    for j in range(NAMED):
        g = tab[base + j]
        send[j] = hl[g, :, :width]
        send[NAMED + j] = shifted(row_product(aff, tab, 0, g, hl), shift, t[g]).astype(BF)


def first_kernel(
    desc, queries, affinity, tile_col, t0, hl, send_a, send_b, aff, tab,
    buf, wide, tall, cols, up_rows, low_rows, sems, *, chunks, axis,
):
    count, rows = t0.shape[0], t0.shape[1]
    per = count // chunks
    _, lists, _, _, _ = offsets(count)
    load_q = pltpu.make_async_copy(queries, wide, sems.at[chunks])
    load_c = pltpu.make_async_copy(tile_col, cols, sems.at[chunks + 1])
    load_q.start()
    load_c.start()
    copies = []
    for c in range(chunks):
        copy = pltpu.make_async_copy(
            desc.at[pl.ds(c * per * rows, per * rows)], buf.at[c], sems.at[c]
        )
        copy.start()
        copies.append(copy)
    load_a = pltpu.make_async_copy(affinity, aff, sems.at[chunks + 2])
    load_a.start()
    hl[count + 2 * NAMED] = jnp.zeros(hl.shape[1:], BF)
    load_q.wait()
    tall[...] = wide[...].T
    load_c.wait()

    def finish(scores, c):
        value = jnp.maximum(scores, 0.0)
        value = value * value * value
        for i in range(per):
            block = value[i * rows : (i + 1) * rows]
            t0[c * per + i] = block
            put_split(hl, c * per + i, block)

    scores = None
    for c in range(chunks):
        copies[c].wait()
        if c == 0:
            fill_table(cols, tab, up_rows, low_rows, axis)
        ahead = dot(buf[c], tall[...])
        if c > 0:
            finish(scores, c - 1)
        scores = ahead
    finish(scores, chunks - 1)
    load_a.wait()
    pack(tab, SHIFTS[0], aff, t0, hl, send_b, lists + NAMED)
    pack(tab, SHIFTS[0], aff, t0, hl, send_a, lists)


def add_products(sums, pairs, fields):
    count, rows, _ = fields[0].shape
    group = 32

    def body(i, sums):
        sums = list(sums)
        g = i // (rows // group)
        start = (i % (rows // group)) * group
        for part in range(group // 8):
            at = pl.ds(pl.multiple_of(start + 8 * part, 8), 8)
            v = [f[g, at, :] for f in fields]
            for n, (a, b) in enumerate(pairs):
                sums[n] = sums[n] + v[a] * v[b]
        return tuple(sums)

    return list(lax.fori_loop(0, count * rows // group, body, tuple(sums)))


def rest_kernel(tab, aff, t, hl, *refs, step):
    count, _, width = t.shape
    fields, (part, hl_next, halo_part, *gram, sums_h) = refs[: 2 * (step > 0)], refs[2 * (step > 0) :]
    _, _, cross, _, _ = offsets(count)
    hl_next[count + 2 * NAMED] = jnp.zeros(hl.shape[1:], BF)
    sums_h[...] = jnp.zeros(sums_h.shape, F32)
    for g in range(count):
        value = shifted(row_product(aff, tab, 0, g, hl), SHIFTS[step], t[g])
        part[g] = value
        put_split(hl_next, g, value)
    for e in range(ENTRIES):
        g, slot, h = (tab[cross + 3 * e + i] for i in range(3))
        both = dot_t(aff[g, slot], hl[g])
        sums_h[h] += both[:, :width] + both[:, width:]
    for h in range(2 * NAMED):
        halo_part[h] = sums_h[h]
    if gram:
        sums = [jnp.zeros((8, width), F32) for _ in EARLY]
        sums = add_products(sums, EARLY, (*fields, t))
        for n, total in enumerate(sums):
            gram[0][pl.ds(n, 1), :] = jnp.sum(total, axis=0, keepdims=True)


def two_steps(tab, aff, hl1, t1, halo_part, recv_a, recv_b, t2, hl2, halo, step):
    count, _, width = t2.shape
    full, lists, cross, _, _ = offsets(count)
    zeros = jnp.zeros(hl2.shape[1:], BF)
    hl2[count + 2 * NAMED] = zeros
    halo[2 * NAMED] = zeros[:, :width]
    for h in range(NAMED):
        halo[h] = recv_a[h]
        halo[NAMED + h] = recv_b[h]
        low, high = h, NAMED + h
        put_split(hl1, count + low, recv_a[NAMED + h].astype(F32) + halo_part[low])
        put_split(hl1, count + high, recv_b[NAMED + h].astype(F32) + halo_part[high])
    for e in range(ENTRIES):
        g, slot, h = (tab[cross + 3 * e + i] for i in range(3))
        t1[g] += dot(aff[g, slot], halo[h])
    for j in range(2 * NAMED):
        g = tab[lists + j]
        put_split(hl1, g, t1[g])
    for g in range(count):
        value = shifted(row_product(aff, tab, full, g, hl1), SHIFTS[step + 1], t1[g])
        t2[g] = value
        put_split(hl2, g, value)


def middle_kernel(
    tab, aff, _, __, halo_part, recv_a, recv_b, hl1, t1, t2, hl2, send_a, send_b, halo
):
    _, lists, _, _, _ = offsets(t1.shape[0])
    two_steps(tab, aff, hl1, t1, halo_part, recv_a, recv_b, t2, hl2, halo, 0)
    pack(tab, SHIFTS[2], aff, t2, hl2, send_b, lists + NAMED)
    pack(tab, SHIFTS[2], aff, t2, hl2, send_a, lists)


def last_kernel(tab, aff, _, __, halo_part, recv_a, recv_b, hl3, t3, t4, hl4, send, halo):
    count, _, width = t3.shape
    _, lists, _, _, _ = offsets(count)
    two_steps(tab, aff, hl3, t3, halo_part, recv_a, recv_b, t4, hl4, halo, 2)
    for j in range(NAMED):
        send[j] = hl4[tab[lists + 2 * NAMED + j], :, :width]


def gram_kernel(tab, aff, t0, t1, t2, t3, t4, hl, early, out, weight, sums_h):
    count, rows, width = t0.shape
    _, _, _, cross, _ = offsets(count)
    sums = [jnp.zeros((8, width), F32) for _ in LATE]
    last = jnp.zeros((8, width), F32)
    sums_h[...] = jnp.zeros(sums_h.shape, F32)
    for e in range(1 + NAMED):
        g, slot, h = (tab[cross + 3 * e + i] for i in range(3))
        both = dot_t(aff[g, slot], hl[g])
        sums_h[h] += 2.0 * (both[:, :width] + both[:, width:])
    for h in range(NAMED):
        weight[h] = sums_h[h]
    for g in range(count):
        local = row_product(aff, tab, 0, g, hl)
        last = last + (t4[g] * local).reshape(rows // 8, 8, width).sum(0)
    sums = add_products(sums, LATE, (t0, t1, t2, t3, t4)) + [last]
    out[pl.ds(0, len(EARLY)), :] = early[...]
    for n, total in enumerate(sums):
        out[pl.ds(len(EARLY) + n, 1), :] = jnp.sum(total, axis=0, keepdims=True)


def cross_kernel(weight, recv, gram, out):
    _, rows, width = weight.shape
    total = jnp.zeros((8, width), F32)
    for h in range(NAMED):
        part = weight[h] * recv[h].astype(F32)
        total = total + part.reshape(rows // 8, 8, width).sum(0)
    value = gram[...]
    extra = jnp.sum(total, axis=0, keepdims=True)
    index = lax.broadcasted_iota(jnp.int32, value.shape, 0)
    value = value + jnp.where(index == ROWS - 1, extra, 0.0)
    for d in range(out.shape[0]):
        out[d] = value


def final_kernel(parts, t0, t1, t2, t3, t4, out, buf, sems):
    n = ITERATIONS
    value = parts[0]
    for d in range(1, parts.shape[0]):
        value = value + parts[d]
    gram = {}
    for k, (i, j) in enumerate(PAIRS):
        gram[i, j] = gram[j, i] = value[k : k + 1]
    matrix = {}
    for i in range(n):
        for j in range(i, n):
            terms = []
            if j + 1 < n:
                terms.append(gram[i, j + 1] + SHIFTS[j] * gram[i, j])
            if i + 1 < n and i != j:
                terms.append(gram[i + 1, j] + SHIFTS[i] * gram[i, j])
            if not terms:
                terms = [value[ROWS - 1 : ROWS]]
            product = terms[0] if len(terms) == 1 else 0.5 * (terms[0] + terms[1])
            matrix[i, j] = gram[i, j] - DAMP * product
    scale = [
        jnp.where(matrix[i, i] > 0.0, lax.rsqrt(jnp.maximum(matrix[i, i], 1e-37)), 0.0)
        for i in range(n)
    ]
    for i in range(n):
        for j in range(i, n):
            matrix[i, j] = matrix[i, j] * (scale[i] * scale[j])
    right = [gram[i, 0] * scale[i] for i in range(n)]
    inverse = []
    for k in range(n):
        pivot = matrix[k, k]
        inverse.append(jnp.where(pivot > PIVOT_MIN, 1.0 / jnp.maximum(pivot, PIVOT_MIN), 0.0))
        for i in range(k + 1, n):
            factor = matrix[k, i] * inverse[k]
            for j in range(i, n):
                matrix[i, j] = matrix[i, j] - factor * matrix[k, j]
            right[i] = right[i] - factor * right[k]
    coef = [None] * n
    for k in range(n - 1, -1, -1):
        rest = right[k]
        for j in range(k + 1, n):
            rest = rest - matrix[k, j] * coef[j]
        coef[k] = rest * inverse[k]
    coef = [coef[k] * scale[k] for k in range(n)]
    fields = (t0, t1, t2, t3, t4)
    count, rows, width = t0.shape
    chunks = sems.shape[0]
    per = count // chunks
    copies = []
    for c in range(chunks):
        for g in range(c * per, (c + 1) * per):
            total = None
            for f, k in zip(fields, coef):
                term = f[g] * k
                total = term if total is None else total + term
            buf[pl.ds(g * rows, rows), :] = total
        part = pl.ds(c * per * rows, per * rows)
        copy = pltpu.make_async_copy(buf.at[part], out.at[part], sems.at[c])
        copy.start()
        copies.append(copy)
    for copy in copies:
        copy.wait()


def swap(block_a, block_b, axis):
    n = lax.axis_size(axis)
    pairs_a = [(i, i ^ 1) for i in range(n)]
    pairs_b = [(i, (i + 1) % n if i % 2 else (i - 1) % n) for i in range(n)]
    got_b = lax.ppermute(block_b, axis, pairs_b)
    got_a = lax.ppermute(block_a, axis, pairs_a)
    return got_a, got_b


def shards(descriptors, queries, affinity, tile_col):
    count, _, rows, _ = affinity.shape
    width = queries.shape[0]
    depth = descriptors.shape[1]
    axis = "dom"
    devices = lax.axis_size(axis)
    size = 128 * pl.cdiv(offsets(count)[-1], 128)
    blocks = count + 2 * NAMED + 1
    field = jax.ShapeDtypeStruct((count, rows, width), F32)
    split = jax.ShapeDtypeStruct((blocks, rows, 2 * width), BF)
    edge = jax.ShapeDtypeStruct((2 * NAMED, rows, width), BF)
    half = jax.ShapeDtypeStruct((NAMED, rows, width), BF)
    early = jax.ShapeDtypeStruct((len(EARLY), width), F32)
    edge_sum = jax.ShapeDtypeStruct((2 * NAMED, rows, width), F32)
    half_sum = jax.ShapeDtypeStruct((NAMED, rows, width), F32)
    sums_h = pltpu.VMEM((2 * NAMED + 1, rows, width), F32)
    work = [pltpu.VMEM((2 * NAMED + 1, rows, width), BF)]
    chunks = count // 2
    flops = 2 * count * rows * 4 * rows * 2 * width

    def call(kernel, out_shape, products, scratch=(), aliases=None, name=None, limit=24):
        outs = out_shape if isinstance(out_shape, tuple) else (out_shape,)

        def run(*args):
            specs = [SMEM if x.dtype == jnp.int32 else VMEM for x in args]
            args = [
                pltpu.with_memory_space_constraint(x, pltpu.SMEM) if x.dtype == jnp.int32 else x
                for x in args
            ]
            return pl.pallas_call(
                kernel,
                out_shape=out_shape,
                in_specs=specs,
                out_specs=(VMEM,) * len(outs) if isinstance(out_shape, tuple) else VMEM,
                scratch_shapes=list(scratch),
                input_output_aliases=aliases or {},
                compiler_params=params(limit),
                cost_estimate=pl.CostEstimate(
                    flops=int(products * flops), bytes_accessed=4 << 20, transcendentals=0
                ),
                name=name,
            )(*args)

        return run

    operands = (descriptors, queries, affinity, tile_col.T)
    t0, hl0, send_a, send_b, aff, tab = pl.pallas_call(
        functools.partial(first_kernel, chunks=chunks, axis=axis),
        out_shape=(
            field,
            split,
            edge,
            edge,
            jax.ShapeDtypeStruct(affinity.shape, BF),
            pltpu.SMEM((size,), jnp.int32),
        ),
        in_specs=[HBM] * 4,
        out_specs=(VMEM,) * 5 + (SMEM,),
        scratch_shapes=[
            pltpu.VMEM((chunks, count * rows // chunks, depth), BF),
            pltpu.VMEM((width, depth), BF),
            pltpu.VMEM((depth, width), BF),
            pltpu.SMEM((4, count), jnp.int32),
            pltpu.SMEM((3, count + 1), jnp.int32),
            pltpu.SMEM((3, count + 1), jnp.int32),
            pltpu.SemaphoreType.DMA((chunks + 3,)),
        ],
        compiler_params=params(24),
        cost_estimate=pl.CostEstimate(flops=flops, bytes_accessed=4 << 20, transcendentals=0),
        name="first",
    )(*(pltpu.with_memory_space_constraint(x, pltpu.HBM) for x in operands))
    recv_a, recv_b = swap(send_a, send_b, axis)
    part, hl1, halo_part = call(
        functools.partial(rest_kernel, step=0), (field, split, edge_sum), 1, [sums_h], name="rest0"
    )(tab, aff, t0, hl0)
    _, t1, t2, hl2, send_a, send_b = call(
        middle_kernel,
        (split, field, field, split, edge, edge),
        2,
        work,
        {2: 0, 3: 1},
        name="middle",
    )(tab, aff, hl1, part, halo_part, recv_a, recv_b)
    recv_a, recv_b = swap(send_a, send_b, axis)
    part, hl3, halo_part, gram = call(
        functools.partial(rest_kernel, step=2),
        (field, split, edge_sum, early),
        1,
        [sums_h],
        name="rest2",
    )(tab, aff, t2, hl2, t0, t1)
    _, t3, t4, hl4, send = call(
        last_kernel,
        (split, field, field, split, half),
        2,
        work,
        {2: 0, 3: 1},
        name="last",
    )(tab, aff, hl3, part, halo_part, recv_a, recv_b)
    recv = lax.ppermute(send, axis, [(i, (i - 1) % devices) for i in range(devices)])
    gram, weight = call(
        gram_kernel,
        (jax.ShapeDtypeStruct((ROWS, width), F32), half_sum),
        1,
        [sums_h],
        name="gram",
    )(tab, aff, t0, t1, t2, t3, t4, hl4, gram)
    parts = call(
        cross_kernel,
        jax.ShapeDtypeStruct((devices, ROWS, width), F32),
        0.1,
        name="cross",
        limit=8,
    )(weight, recv, gram)
    parts = lax.all_to_all(parts, axis, 0, 0)
    return pl.pallas_call(
        final_kernel,
        out_shape=jax.ShapeDtypeStruct((count * rows, width), F32),
        in_specs=[VMEM] * 6,
        out_specs=HBM,
        scratch_shapes=[
            pltpu.VMEM((count * rows, width), F32),
            pltpu.SemaphoreType.DMA((count // 3,)),
        ],
        compiler_params=params(24),
        name="final",
    )(parts, t0, t1, t2, t3, t4)


def solution(mesh):
    return jax.shard_map(
        shards,
        mesh=mesh,
        in_specs=(
            P(("region", "dom"), None),
            P("region", None),
            P(("region", "dom"), None, None, None),
            P(("region", "dom"), None),
        ),
        out_specs=P(("region", "dom"), None),
        check_vma=False,
    )
```

```python
import functools

import jax
import jax.numpy as jnp
from jax import lax
from jax.experimental import pallas as pl
from jax.experimental.pallas import tpu as pltpu
from jax.sharding import PartitionSpec as P

HALO_W = 6
NAMED = 3
ITERATIONS = 5
DAMP = 0.99
SHIFTS = (0.0, 1.0, -0.25, 0.5)
PIVOT_MIN = 1e-6
BF = jnp.bfloat16
F32 = jnp.float32
EARLY = [(i, j) for i in range(3) for j in range(i, 3)]
LATE = [(i, j) for j in range(3, ITERATIONS) for i in range(j + 1)]
PAIRS = EARLY + LATE
ROWS = len(PAIRS) + 1
ENTRIES = 2 + 2 * NAMED

VMEM = pl.BlockSpec(memory_space=pltpu.VMEM)
SMEM = pl.BlockSpec(memory_space=pltpu.SMEM)
HBM = pl.BlockSpec(memory_space=pltpu.HBM)


def params(mib):
    return pltpu.CompilerParams(vmem_limit_bytes=mib << 20)


def dot(a, b):
    return jnp.dot(a, b, preferred_element_type=F32)


def dot_t(a, b):
    return lax.dot_general(a, b, (((0,), (0,)), ((), ())), preferred_element_type=F32)


def put_split(ref, index, value):
    high = value.astype(BF)
    width = value.shape[-1]
    ref[index, :, :width] = high
    ref[index, :, width:] = (value - high.astype(F32)).astype(BF)


def row_product(aff, tab, base, g, hl):
    count = aff.shape[0]
    width = hl.shape[2] // 2
    if isinstance(g, int):
        low = g - 1 if g > 0 else tab[base + count]
        high = g + 1 if g + 1 < count else tab[base + count + 1]
    else:
        low = jnp.where(g > 0, g - 1, tab[base + count])
        high = jnp.where(g + 1 < count, g + 1, tab[base + count + 1])
    left = jnp.concatenate([aff[g, 0], aff[g, 1]], axis=1)
    right = jnp.concatenate([hl[g], hl[low]], axis=0)
    out = dot(left, right)
    left = jnp.concatenate([aff[g, 2], aff[g, 3]], axis=1)
    right = jnp.concatenate([hl[high], hl[tab[base + g]]], axis=0)
    out = out + dot(left, right)
    return out[:, :width] + out[:, width:]


def shifted(value, shift, t):
    return value if shift == 0.0 else value - shift * t


def offsets(count):
    full = count + 2
    lists = 2 * full
    cross = lists + 2 * NAMED
    return full, lists, cross, cross + 3 * ENTRIES


def fill_table(tile_col, tab, up_rows, low_rows, axis):
    count = tile_col.shape[1]
    total = count * lax.axis_size(axis)
    me = lax.axis_index(axis)
    even = lax.rem(me, 2) == 0
    full, lists, cross, _ = offsets(count)
    zero = count + 2 * NAMED
    up_base = jnp.where(even, 0, NAMED)
    low_base = NAMED - up_base
    relative, ups, lows = [], [], []
    up_mask = jnp.int32(1)
    low_mask = jnp.int32(1 << (HALO_W - 1))
    for g in range(count):
        rel = tile_col[3, g] - me * count
        rel = jnp.where(rel < 0, rel + total, rel)
        up = (rel >= count) & (rel < count + HALO_W)
        low = rel >= total - HALO_W
        place = jnp.where(up, rel - count, rel - (total - HALO_W))
        place = jnp.clip(place, 0, HALO_W - 1)
        bit = lax.shift_left(jnp.int32(1), place)
        up_mask = up_mask | jnp.where(up, bit, 0)
        low_mask = low_mask | jnp.where(low, bit, 0)
        relative.append((rel, place, bit))
        ups.append(up)
        lows.append(low)
    up_count = low_count = up_cross = low_cross = jnp.int32(0)
    for g in range(count):
        rel, place, bit = relative[g]
        below = jnp.where(ups[g], up_mask, low_mask) & (bit - 1)
        rank = below & 1
        for p in range(1, HALO_W - 1):
            rank = rank + (lax.shift_right_logical(below, jnp.int32(p)) & 1)
        halo = jnp.where(ups[g], up_base, low_base) + jnp.minimum(rank, NAMED - 1)
        local = rel < count
        tab[g] = jnp.where(local, rel, zero)
        tab[full + g] = jnp.where(local, rel, count + halo)
        up_rows[0, up_count] = g
        low_rows[0, low_count] = g
        up_rows[1, up_cross] = g
        low_rows[1, low_cross] = g
        up_rows[2, up_cross] = halo
        low_rows[2, low_cross] = halo
        up_cross = up_cross + jnp.where(ups[g], 1, 0)
        low_cross = low_cross + jnp.where(lows[g], 1, 0)
        up_count = up_count + (1 if g == count - 1 else jnp.where(ups[g], 1, 0))
        low_count = low_count + (1 if g == 0 else jnp.where(lows[g], 1, 0))
    tab[count] = zero
    tab[count + 1] = zero
    tab[full + count] = count + low_base + NAMED - 1
    tab[full + count + 1] = count + up_base
    for j in range(NAMED):
        up, low = up_rows[0, j], low_rows[0, j]
        tab[lists + j] = jnp.where(even, up, low)
        tab[lists + NAMED + j] = jnp.where(even, low, up)
    chains = ((0, 1, low_base + NAMED - 1), (count - 1, 2, up_base))
    for side, (rows, used) in enumerate(((low_rows, low_cross), (up_rows, up_cross))):
        for i in range(3):
            tab[cross + 3 * side * (1 + NAMED) + i] = jnp.int32(chains[side][i])
        for j in range(NAMED):
            at = cross + 3 * (side * (1 + NAMED) + 1 + j)
            tab[at] = jnp.where(j < used, rows[1, j], 0)
            tab[at + 1] = jnp.int32(3)
            tab[at + 2] = jnp.where(j < used, rows[2, j], 2 * NAMED)


def pack(tab, shift, aff, t, hl, send, base):
    width = t.shape[2]
    for j in range(NAMED):
        g = tab[base + j]
        send[j] = hl[g, :, :width]
        send[NAMED + j] = shifted(row_product(aff, tab, 0, g, hl), shift, t[g]).astype(BF)


def first_kernel(
    desc, queries, affinity, tile_col, t0, hl, send_b, aff, tab,
    buf, wide, tall, cols, up_rows, low_rows, sems, *, chunks, axis,
):
    count, rows = t0.shape[0], t0.shape[1]
    per = count // chunks
    _, lists, _, _ = offsets(count)
    load_q = pltpu.make_async_copy(queries, wide, sems.at[chunks])
    load_c = pltpu.make_async_copy(tile_col, cols, sems.at[chunks + 1])
    load_q.start()
    load_c.start()
    copies = []
    for c in range(chunks):
        copy = pltpu.make_async_copy(
            desc.at[pl.ds(c * per * rows, per * rows)], buf.at[c], sems.at[c]
        )
        copy.start()
        copies.append(copy)
    load_a = pltpu.make_async_copy(affinity, aff, sems.at[chunks + 2])
    load_a.start()
    hl[count + 2 * NAMED] = jnp.zeros(hl.shape[1:], BF)
    load_q.wait()
    tall[...] = wide[...].T
    load_c.wait()

    def finish(scores, c):
        value = jnp.maximum(scores, 0.0)
        value = value * value * value
        for i in range(per):
            block = value[i * rows : (i + 1) * rows]
            t0[c * per + i] = block
            put_split(hl, c * per + i, block)

    scores = None
    for c in range(chunks):
        copies[c].wait()
        if c == 0:
            fill_table(cols, tab, up_rows, low_rows, axis)
        ahead = dot(buf[c], tall[...])
        if c > 0:
            finish(scores, c - 1)
        scores = ahead
    finish(scores, chunks - 1)
    load_a.wait()
    pack(tab, SHIFTS[0], aff, t0, hl, send_b, lists + NAMED)


def add_products(sums, pairs, fields):
    count, rows, _ = fields[0].shape
    group = 32

    def body(i, sums):
        sums = list(sums)
        g = i // (rows // group)
        start = (i % (rows // group)) * group
        for part in range(group // 8):
            at = pl.ds(pl.multiple_of(start + 8 * part, 8), 8)
            v = [f[g, at, :] for f in fields]
            for n, (a, b) in enumerate(pairs):
                sums[n] = sums[n] + v[a] * v[b]
        return tuple(sums)

    return list(lax.fori_loop(0, count * rows // group, body, tuple(sums)))


def halo_products(tab, aff, hl, sums, factor):
    count = aff.shape[0]
    width = sums.shape[2]
    _, _, cross, _ = offsets(count)
    sums[...] = jnp.zeros(sums.shape, F32)
    for e in range(ENTRIES):
        g, slot, h = (tab[cross + 3 * e + i] for i in range(3))
        both = dot_t(aff[g, slot], hl[g])
        both = both[:, :width] + both[:, width:]
        sums[h] += both if factor == 1.0 else factor * both


def rest_kernel(tab, aff, t, hl, part, hl_next, halo_part, send_a, sums, *, step):
    count = t.shape[0]
    _, lists, _, _ = offsets(count)
    pack(tab, SHIFTS[step], aff, t, hl, send_a, lists)
    hl_next[count + 2 * NAMED] = jnp.zeros(hl.shape[1:], BF)
    for g in range(count):
        value = shifted(row_product(aff, tab, 0, g, hl), SHIFTS[step], t[g])
        part[g] = value
        put_split(hl_next, g, value)
    halo_products(tab, aff, hl, sums, 1.0)
    for h in range(2 * NAMED):
        halo_part[h] = sums[h]


def early_kernel(t0, t1, t2, out):
    sums = [jnp.zeros((8, t0.shape[2]), F32) for _ in EARLY]
    for n, total in enumerate(add_products(sums, EARLY, (t0, t1, t2))):
        out[pl.ds(n, 1), :] = jnp.sum(total, axis=0, keepdims=True)


def two_steps(tab, aff, hl1, t1, halo_part, recv_a, recv_b, t2, hl2, halo, step):
    count, _, width = t2.shape
    full, lists, cross, _ = offsets(count)
    zeros = jnp.zeros(hl2.shape[1:], BF)
    hl2[count + 2 * NAMED] = zeros
    halo[2 * NAMED] = zeros[:, :width]
    for h in range(NAMED):
        halo[h] = recv_a[h]
        halo[NAMED + h] = recv_b[h]
        low, high = h, NAMED + h
        put_split(hl1, count + low, recv_a[NAMED + h].astype(F32) + halo_part[low])
        put_split(hl1, count + high, recv_b[NAMED + h].astype(F32) + halo_part[high])
    for e in range(ENTRIES):
        g, slot, h = (tab[cross + 3 * e + i] for i in range(3))
        t1[g] += dot(aff[g, slot], halo[h])
    for j in range(2 * NAMED):
        g = tab[lists + j]
        put_split(hl1, g, t1[g])
    for g in range(count):
        value = shifted(row_product(aff, tab, full, g, hl1), SHIFTS[step + 1], t1[g])
        t2[g] = value
        put_split(hl2, g, value)


def middle_kernel(
    tab, aff, _, __, halo_part, recv_a, recv_b, hl1, t1, t2, hl2, send_b, halo
):
    _, lists, _, _ = offsets(t1.shape[0])
    two_steps(tab, aff, hl1, t1, halo_part, recv_a, recv_b, t2, hl2, halo, 0)
    pack(tab, SHIFTS[2], aff, t2, hl2, send_b, lists + NAMED)


def last_kernel(tab, aff, _, __, halo_part, recv_a, recv_b, hl3, t3, t4, hl4, send, halo):
    count, _, width = t3.shape
    _, lists, _, _ = offsets(count)
    two_steps(tab, aff, hl3, t3, halo_part, recv_a, recv_b, t4, hl4, halo, 2)
    for j in range(NAMED):
        send[j] = hl4[tab[lists + NAMED + j], :, :width]


def gram_kernel(tab, aff, t0, t1, t2, t3, t4, hl, early, out, weight, send_a, sums_h):
    count, rows, width = t0.shape
    _, lists, _, _ = offsets(count)
    for j in range(NAMED):
        send_a[j] = hl[tab[lists + j], :, :width]
    sums = [jnp.zeros((8, width), F32) for _ in LATE]
    last = jnp.zeros((8, width), F32)
    halo_products(tab, aff, hl, sums_h, 2.0)
    for h in range(2 * NAMED):
        weight[h] = sums_h[h]
    for g in range(count):
        local = row_product(aff, tab, 0, g, hl)
        last = last + (t4[g] * local).reshape(rows // 8, 8, width).sum(0)
    sums = add_products(sums, LATE, (t0, t1, t2, t3, t4)) + [last]
    out[pl.ds(0, len(EARLY)), :] = early[...]
    for n, total in enumerate(sums):
        out[pl.ds(len(EARLY) + n, 1), :] = jnp.sum(total, axis=0, keepdims=True)


def cross_kernel(weight, recv_a, recv_b, gram, other, out):
    _, rows, width = weight.shape
    total = jnp.zeros((8, width), F32)
    for h in range(NAMED):
        part = weight[h] * recv_a[h].astype(F32) + weight[NAMED + h] * recv_b[h].astype(F32)
        total = total + part.reshape(rows // 8, 8, width).sum(0)
    value = gram[...] + other[...]
    extra = jnp.sum(total, axis=0, keepdims=True)
    index = lax.broadcasted_iota(jnp.int32, value.shape, 0)
    value = value + jnp.where(index == ROWS - 1, extra, 0.0)
    for d in range(out.shape[0]):
        out[d] = value


def final_kernel(parts, t0, t1, t2, t3, t4, out, buf, sems):
    n = ITERATIONS
    value = parts[0]
    for d in range(1, parts.shape[0]):
        value = value + parts[d]
    gram = {}
    for k, (i, j) in enumerate(PAIRS):
        gram[i, j] = gram[j, i] = value[k : k + 1]
    matrix = {}
    for i in range(n):
        for j in range(i, n):
            terms = []
            if j + 1 < n:
                terms.append(gram[i, j + 1] + SHIFTS[j] * gram[i, j])
            if i + 1 < n and i != j:
                terms.append(gram[i + 1, j] + SHIFTS[i] * gram[i, j])
            if not terms:
                terms = [value[ROWS - 1 : ROWS]]
            product = terms[0] if len(terms) == 1 else 0.5 * (terms[0] + terms[1])
            matrix[i, j] = gram[i, j] - DAMP * product
    scale = [
        jnp.where(matrix[i, i] > 0.0, lax.rsqrt(jnp.maximum(matrix[i, i], 1e-37)), 0.0)
        for i in range(n)
    ]
    for i in range(n):
        for j in range(i, n):
            matrix[i, j] = matrix[i, j] * (scale[i] * scale[j])
    right = [gram[i, 0] * scale[i] for i in range(n)]
    inverse = []
    for k in range(n):
        pivot = matrix[k, k]
        inverse.append(jnp.where(pivot > PIVOT_MIN, 1.0 / jnp.maximum(pivot, PIVOT_MIN), 0.0))
        for i in range(k + 1, n):
            factor = matrix[k, i] * inverse[k]
            for j in range(i, n):
                matrix[i, j] = matrix[i, j] - factor * matrix[k, j]
            right[i] = right[i] - factor * right[k]
    coef = [None] * n
    for k in range(n - 1, -1, -1):
        rest = right[k]
        for j in range(k + 1, n):
            rest = rest - matrix[k, j] * coef[j]
        coef[k] = rest * inverse[k]
    coef = [coef[k] * scale[k] for k in range(n)]
    fields = (t0, t1, t2, t3, t4)
    count, rows, _ = t0.shape
    chunks = sems.shape[0]
    per = count // chunks
    copies = []
    for c in range(chunks):
        for g in range(c * per, (c + 1) * per):
            total = None
            for f, k in zip(fields, coef):
                term = f[g] * k
                total = term if total is None else total + term
            buf[pl.ds(g * rows, rows), :] = total
        part = pl.ds(c * per * rows, per * rows)
        copy = pltpu.make_async_copy(buf.at[part], out.at[part], sems.at[c])
        copy.start()
        copies.append(copy)
    for copy in copies:
        copy.wait()


def to_chip_partner(block, axis):
    return lax.ppermute(block, axis, [(i, i ^ 1) for i in range(lax.axis_size(axis))])


def to_other_chip(block, axis):
    n = lax.axis_size(axis)
    return lax.ppermute(block, axis, [(i, (i + 1) % n if i % 2 else (i - 1) % n) for i in range(n)])


def shards(descriptors, queries, affinity, tile_col):
    count, _, rows, _ = affinity.shape
    width = queries.shape[0]
    depth = descriptors.shape[1]
    axis = "dom"
    devices = lax.axis_size(axis)
    size = 128 * pl.cdiv(offsets(count)[-1], 128)
    blocks = count + 2 * NAMED + 1
    field = jax.ShapeDtypeStruct((count, rows, width), F32)
    split = jax.ShapeDtypeStruct((blocks, rows, 2 * width), BF)
    edge = jax.ShapeDtypeStruct((2 * NAMED, rows, width), BF)
    half = jax.ShapeDtypeStruct((NAMED, rows, width), BF)
    early = jax.ShapeDtypeStruct((len(EARLY), width), F32)
    edge_sum = jax.ShapeDtypeStruct((2 * NAMED, rows, width), F32)
    sums_h = pltpu.VMEM((2 * NAMED + 1, rows, width), F32)
    work = [pltpu.VMEM((2 * NAMED + 1, rows, width), BF)]
    chunks = count // 2
    flops = 2 * count * rows * 4 * rows * 2 * width

    def call(kernel, out_shape, products, scratch=(), aliases=None, limit=24):
        outs = out_shape if isinstance(out_shape, tuple) else (out_shape,)

        def run(*args):
            specs = [SMEM if x.dtype == jnp.int32 else VMEM for x in args]
            args = [
                pltpu.with_memory_space_constraint(x, pltpu.SMEM) if x.dtype == jnp.int32 else x
                for x in args
            ]
            return pl.pallas_call(
                kernel,
                out_shape=out_shape,
                in_specs=specs,
                out_specs=(VMEM,) * len(outs) if isinstance(out_shape, tuple) else VMEM,
                scratch_shapes=list(scratch),
                input_output_aliases=aliases or {},
                compiler_params=params(limit),
                cost_estimate=pl.CostEstimate(
                    flops=int(products * flops), bytes_accessed=4 << 20, transcendentals=0
                ),
            )(*args)

        return run

    operands = (descriptors, queries, affinity, tile_col.T)
    t0, hl0, send_b, aff, tab = pl.pallas_call(
        functools.partial(first_kernel, chunks=chunks, axis=axis),
        out_shape=(
            field,
            split,
            edge,
            jax.ShapeDtypeStruct(affinity.shape, BF),
            pltpu.SMEM((size,), jnp.int32),
        ),
        in_specs=[HBM] * 4,
        out_specs=(VMEM,) * 4 + (SMEM,),
        scratch_shapes=[
            pltpu.VMEM((chunks, count * rows // chunks, depth), BF),
            pltpu.VMEM((width, depth), BF),
            pltpu.VMEM((depth, width), BF),
            pltpu.SMEM((4, count), jnp.int32),
            pltpu.SMEM((3, count + 1), jnp.int32),
            pltpu.SMEM((3, count + 1), jnp.int32),
            pltpu.SemaphoreType.DMA((chunks + 3,)),
        ],
        compiler_params=params(24),
        cost_estimate=pl.CostEstimate(flops=flops, bytes_accessed=4 << 20, transcendentals=0),
        name="first",
    )(*(pltpu.with_memory_space_constraint(x, pltpu.HBM) for x in operands))
    recv_b = to_other_chip(send_b, axis)
    part, hl1, halo_part, send_a = call(
        functools.partial(rest_kernel, step=0), (field, split, edge_sum, edge), 1, [sums_h]
    )(tab, aff, t0, hl0)
    recv_a = to_chip_partner(send_a, axis)
    _, t1, t2, hl2, send_b = call(
        middle_kernel, (split, field, field, split, edge), 2, work, {2: 0, 3: 1}
    )(tab, aff, hl1, part, halo_part, recv_a, recv_b)
    recv_b = to_other_chip(send_b, axis)
    part, hl3, halo_part, send_a = call(
        functools.partial(rest_kernel, step=2), (field, split, edge_sum, edge), 1, [sums_h]
    )(tab, aff, t2, hl2)
    recv_a = to_chip_partner(send_a, axis)
    gram = call(early_kernel, early, 0.1)(t0, t1, t2)
    _, t3, t4, hl4, send_b = call(
        last_kernel, (split, field, field, split, half), 2, work, {2: 0, 3: 1}
    )(tab, aff, hl3, part, halo_part, recv_a, recv_b)
    recv_b = to_other_chip(send_b, axis)
    gram, weight, send_a = call(
        gram_kernel, (jax.ShapeDtypeStruct((ROWS, width), F32), edge_sum, half), 1, [sums_h]
    )(tab, aff, t0, t1, t2, t3, t4, hl4, gram)
    recv_a = to_chip_partner(send_a, axis)
    other = to_chip_partner(gram, axis)
    parts = call(
        cross_kernel, jax.ShapeDtypeStruct((devices // 2, ROWS, width), F32), 0.1, limit=8
    )(weight, recv_a, recv_b, gram, other)
    groups = [list(range(core, devices, 2)) for core in range(2)]
    parts = lax.all_to_all(parts, axis, 0, 0, axis_index_groups=groups)
    return pl.pallas_call(
        final_kernel,
        out_shape=jax.ShapeDtypeStruct((count * rows, width), F32),
        in_specs=[VMEM] * 6,
        out_specs=HBM,
        scratch_shapes=[
            pltpu.VMEM((count * rows, width), F32),
            pltpu.SemaphoreType.DMA((count // 3,)),
        ],
        compiler_params=params(24),
        name="final",
    )(parts, t0, t1, t2, t3, t4)


def solution(mesh):
    return jax.shard_map(
        shards,
        mesh=mesh,
        in_specs=(
            P(("region", "dom"), None),
            P("region", None),
            P(("region", "dom"), None, None, None),
            P(("region", "dom"), None),
        ),
        out_specs=P(("region", "dom"), None),
        check_vma=False,
    )
```

```python
import functools

import jax
import jax.numpy as jnp
from jax import lax
from jax.experimental import pallas as pl
from jax.experimental.pallas import tpu as pltpu
from jax.sharding import PartitionSpec as P

HALO_W = 6
NAMED = 3
ITERATIONS = 5
DAMP = 0.99
SHIFTS = (0.0, 1.0, -0.25, 0.5)
PIVOT_MIN = 1e-6
BF = jnp.bfloat16
F32 = jnp.float32
EARLY = [(i, j) for i in range(3) for j in range(i, 3)]
LATE = [(i, j) for j in range(3, ITERATIONS) for i in range(j + 1)]
PAIRS = EARLY + LATE
ROWS = len(PAIRS) + 1
ENTRIES = 2 + 2 * NAMED

VMEM = pl.BlockSpec(memory_space=pltpu.VMEM)
SMEM = pl.BlockSpec(memory_space=pltpu.SMEM)
HBM = pl.BlockSpec(memory_space=pltpu.HBM)


def params(mib):
    return pltpu.CompilerParams(vmem_limit_bytes=mib << 20)


def dot(a, b):
    return jnp.dot(a, b, preferred_element_type=F32)


def dot_t(a, b):
    return lax.dot_general(a, b, (((0,), (0,)), ((), ())), preferred_element_type=F32)


def put_split(ref, index, value):
    high = value.astype(BF)
    width = value.shape[-1]
    ref[index, :, :width] = high
    ref[index, :, width:] = (value - high.astype(F32)).astype(BF)


def row_product(aff, tab, base, g, hl):
    count = aff.shape[0]
    width = hl.shape[2] // 2
    if isinstance(g, int):
        low = g - 1 if g > 0 else tab[base + count]
        high = g + 1 if g + 1 < count else tab[base + count + 1]
    else:
        low = jnp.where(g > 0, g - 1, tab[base + count])
        high = jnp.where(g + 1 < count, g + 1, tab[base + count + 1])
    left = jnp.concatenate([aff[g, 0], aff[g, 1]], axis=1)
    right = jnp.concatenate([hl[g], hl[low]], axis=0)
    out = dot(left, right)
    left = jnp.concatenate([aff[g, 2], aff[g, 3]], axis=1)
    right = jnp.concatenate([hl[high], hl[tab[base + g]]], axis=0)
    out = out + dot(left, right)
    return out[:, :width] + out[:, width:]


def shifted(value, shift, t):
    return value if shift == 0.0 else value - shift * t


def offsets(count):
    full = count + 2
    lists = 2 * full
    cross = lists + 2 * NAMED
    return full, lists, cross, cross + 3 * ENTRIES


def fill_table(tile_col, tab, up_rows, low_rows, axis):
    count = tile_col.shape[1]
    total = count * lax.axis_size(axis)
    me = lax.axis_index(axis)
    even = lax.rem(me, 2) == 0
    full, lists, cross, _ = offsets(count)
    zero = count + 2 * NAMED
    up_base = jnp.where(even, 0, NAMED)
    low_base = NAMED - up_base
    relative, ups, lows = [], [], []
    up_mask = jnp.int32(1)
    low_mask = jnp.int32(1 << (HALO_W - 1))
    for g in range(count):
        rel = tile_col[3, g] - me * count
        rel = jnp.where(rel < 0, rel + total, rel)
        up = (rel >= count) & (rel < count + HALO_W)
        low = rel >= total - HALO_W
        place = jnp.where(up, rel - count, rel - (total - HALO_W))
        place = jnp.clip(place, 0, HALO_W - 1)
        bit = lax.shift_left(jnp.int32(1), place)
        up_mask = up_mask | jnp.where(up, bit, 0)
        low_mask = low_mask | jnp.where(low, bit, 0)
        relative.append((rel, place, bit))
        ups.append(up)
        lows.append(low)
    up_count = low_count = up_cross = low_cross = jnp.int32(0)
    for g in range(count):
        rel, place, bit = relative[g]
        below = jnp.where(ups[g], up_mask, low_mask) & (bit - 1)
        rank = below & 1
        for p in range(1, HALO_W - 1):
            rank = rank + (lax.shift_right_logical(below, jnp.int32(p)) & 1)
        halo = jnp.where(ups[g], up_base, low_base) + jnp.minimum(rank, NAMED - 1)
        local = rel < count
        tab[g] = jnp.where(local, rel, zero)
        tab[full + g] = jnp.where(local, rel, count + halo)
        up_rows[0, up_count] = g
        low_rows[0, low_count] = g
        up_rows[1, up_cross] = g
        low_rows[1, low_cross] = g
        up_rows[2, up_cross] = halo
        low_rows[2, low_cross] = halo
        up_cross = up_cross + jnp.where(ups[g], 1, 0)
        low_cross = low_cross + jnp.where(lows[g], 1, 0)
        up_count = up_count + (1 if g == count - 1 else jnp.where(ups[g], 1, 0))
        low_count = low_count + (1 if g == 0 else jnp.where(lows[g], 1, 0))
    tab[count] = zero
    tab[count + 1] = zero
    tab[full + count] = count + low_base + NAMED - 1
    tab[full + count + 1] = count + up_base
    for j in range(NAMED):
        up, low = up_rows[0, j], low_rows[0, j]
        tab[lists + j] = jnp.where(even, up, low)
        tab[lists + NAMED + j] = jnp.where(even, low, up)
    chains = ((0, 1, low_base + NAMED - 1), (count - 1, 2, up_base))
    for side, (rows, used) in enumerate(((low_rows, low_cross), (up_rows, up_cross))):
        for i in range(3):
            tab[cross + 3 * side * (1 + NAMED) + i] = jnp.int32(chains[side][i])
        for j in range(NAMED):
            at = cross + 3 * (side * (1 + NAMED) + 1 + j)
            tab[at] = jnp.where(j < used, rows[1, j], 0)
            tab[at + 1] = jnp.int32(3)
            tab[at + 2] = jnp.where(j < used, rows[2, j], 2 * NAMED)


def pack(tab, shift, aff, t, hl, send, base):
    width = t.shape[2]
    for j in range(NAMED):
        g = tab[base + j]
        send[j] = hl[g, :, :width]
        send[NAMED + j] = shifted(row_product(aff, tab, 0, g, hl), shift, t[g]).astype(BF)


def first_kernel(
    desc, queries, affinity, tile_col, t0, hl, send_b, aff, tab,
    buf, wide, tall, cols, up_rows, low_rows, sems, *, chunks, axis,
):
    count, rows = t0.shape[0], t0.shape[1]
    per = count // chunks
    _, lists, _, _ = offsets(count)
    load_q = pltpu.make_async_copy(queries, wide, sems.at[chunks])
    load_c = pltpu.make_async_copy(tile_col, cols, sems.at[chunks + 1])
    load_q.start()
    load_c.start()
    copies = []
    for c in range(chunks):
        copy = pltpu.make_async_copy(
            desc.at[pl.ds(c * per * rows, per * rows)], buf.at[c], sems.at[c]
        )
        copy.start()
        copies.append(copy)
    load_a = pltpu.make_async_copy(affinity, aff, sems.at[chunks + 2])
    load_a.start()
    hl[count + 2 * NAMED] = jnp.zeros(hl.shape[1:], BF)
    load_q.wait()
    tall[...] = wide[...].T
    load_c.wait()

    def finish(scores, c):
        value = jnp.maximum(scores, 0.0)
        value = value * value * value
        for i in range(per):
            block = value[i * rows : (i + 1) * rows]
            t0[c * per + i] = block
            put_split(hl, c * per + i, block)

    scores = None
    for c in range(chunks):
        copies[c].wait()
        if c == 0:
            fill_table(cols, tab, up_rows, low_rows, axis)
        ahead = dot(buf[c], tall[...])
        if c > 0:
            finish(scores, c - 1)
        scores = ahead
    finish(scores, chunks - 1)
    load_a.wait()
    pack(tab, SHIFTS[0], aff, t0, hl, send_b, lists + NAMED)


def add_products(sums, pairs, fields):
    count, rows, _ = fields[0].shape
    group = 32

    def body(i, sums):
        sums = list(sums)
        g = i // (rows // group)
        start = (i % (rows // group)) * group
        for part in range(group // 8):
            at = pl.ds(pl.multiple_of(start + 8 * part, 8), 8)
            v = [f[g, at, :] for f in fields]
            for n, (a, b) in enumerate(pairs):
                sums[n] = sums[n] + v[a] * v[b]
        return tuple(sums)

    return list(lax.fori_loop(0, count * rows // group, body, tuple(sums)))


def halo_products(tab, aff, hl, sums, factor):
    count = aff.shape[0]
    width = sums.shape[2]
    _, _, cross, _ = offsets(count)
    sums[...] = jnp.zeros(sums.shape, F32)
    for e in range(ENTRIES):
        g, slot, h = (tab[cross + 3 * e + i] for i in range(3))
        both = dot_t(aff[g, slot], hl[g])
        both = both[:, :width] + both[:, width:]
        sums[h] += both if factor == 1.0 else factor * both


def rest_kernel(tab, aff, t, hl, part, hl_next, halo_part, send_a, sums, *, step):
    count = t.shape[0]
    _, lists, _, _ = offsets(count)
    pack(tab, SHIFTS[step], aff, t, hl, send_a, lists)
    hl_next[count + 2 * NAMED] = jnp.zeros(hl.shape[1:], BF)
    for g in range(count):
        value = shifted(row_product(aff, tab, 0, g, hl), SHIFTS[step], t[g])
        part[g] = value
        put_split(hl_next, g, value)
    halo_products(tab, aff, hl, sums, 1.0)
    for h in range(2 * NAMED):
        halo_part[h] = sums[h]


def early_kernel(t0, t1, t2, out):
    sums = [jnp.zeros((8, t0.shape[2]), F32) for _ in EARLY]
    for n, total in enumerate(add_products(sums, EARLY, (t0, t1, t2))):
        out[pl.ds(n, 1), :] = jnp.sum(total, axis=0, keepdims=True)


def two_steps(tab, aff, hl1, t1, halo_part, recv_a, recv_b, t2, hl2, halo, step):
    count, _, width = t2.shape
    full, lists, cross, _ = offsets(count)
    zeros = jnp.zeros(hl2.shape[1:], BF)
    hl2[count + 2 * NAMED] = zeros
    halo[2 * NAMED] = zeros[:, :width]
    for h in range(NAMED):
        halo[h] = recv_a[h]
        halo[NAMED + h] = recv_b[h]
        low, high = h, NAMED + h
        put_split(hl1, count + low, recv_a[NAMED + h].astype(F32) + halo_part[low])
        put_split(hl1, count + high, recv_b[NAMED + h].astype(F32) + halo_part[high])
    for e in range(ENTRIES):
        g, slot, h = (tab[cross + 3 * e + i] for i in range(3))
        t1[g] += dot(aff[g, slot], halo[h])
    for j in range(2 * NAMED):
        g = tab[lists + j]
        put_split(hl1, g, t1[g])
    for g in range(count):
        value = shifted(row_product(aff, tab, full, g, hl1), SHIFTS[step + 1], t1[g])
        t2[g] = value
        put_split(hl2, g, value)


def middle_kernel(tab, aff, *refs, parity, axis):
    halo_part, recv_a, recv_b = refs[-9:-6]
    hl1, t1, t2, hl2, send_b, halo = refs[-6:]
    _, lists, _, _ = offsets(t1.shape[0])
    active = lax.rem(lax.axis_index(axis), 2) == parity

    @pl.when(active)
    def _():
        two_steps(tab, aff, hl1, t1, halo_part, recv_a, recv_b, t2, hl2, halo, 0)
        pack(tab, SHIFTS[2], aff, t2, hl2, send_b, lists + NAMED)

    @pl.when(jnp.logical_not(active))
    def _():
        send_b[...] = jnp.zeros(send_b.shape, BF)


def last_kernel(tab, aff, *refs, parity, axis):
    halo_part, recv_a, recv_b = refs[-9:-6]
    hl3, t3, t4, hl4, send_b, halo = refs[-6:]
    width = t3.shape[2]
    _, lists, _, _ = offsets(t3.shape[0])
    active = lax.rem(lax.axis_index(axis), 2) == parity

    @pl.when(active)
    def _():
        two_steps(tab, aff, hl3, t3, halo_part, recv_a, recv_b, t4, hl4, halo, 2)
        for j in range(NAMED):
            send_b[j] = hl4[tab[lists + NAMED + j], :, :width]

    @pl.when(jnp.logical_not(active))
    def _():
        send_b[...] = jnp.zeros(send_b.shape, BF)


def gram_kernel(tab, aff, t0, t1, t2, t3, t4, hl, early, out, weight, send_a, sums_h):
    count, rows, width = t0.shape
    _, lists, _, _ = offsets(count)
    for j in range(NAMED):
        send_a[j] = hl[tab[lists + j], :, :width]
    sums = [jnp.zeros((8, width), F32) for _ in LATE]
    last = jnp.zeros((8, width), F32)
    halo_products(tab, aff, hl, sums_h, 2.0)
    for h in range(2 * NAMED):
        weight[h] = sums_h[h]
    for g in range(count):
        local = row_product(aff, tab, 0, g, hl)
        last = last + (t4[g] * local).reshape(rows // 8, 8, width).sum(0)
    sums = add_products(sums, LATE, (t0, t1, t2, t3, t4)) + [last]
    out[pl.ds(0, len(EARLY)), :] = early[...]
    for n, total in enumerate(sums):
        out[pl.ds(len(EARLY) + n, 1), :] = jnp.sum(total, axis=0, keepdims=True)


def cross_kernel(weight, recv_a, recv_even, recv_odd, gram, other, out, recv_b, *, axis):
    _, rows, width = weight.shape
    even = lax.rem(lax.axis_index(axis), 2) == 0

    @pl.when(even)
    def _():
        recv_b[...] = recv_even[...]

    @pl.when(jnp.logical_not(even))
    def _():
        recv_b[...] = recv_odd[...]

    total = jnp.zeros((8, width), F32)
    for h in range(NAMED):
        part = weight[h] * recv_a[h].astype(F32) + weight[NAMED + h] * recv_b[h].astype(F32)
        total = total + part.reshape(rows // 8, 8, width).sum(0)
    value = gram[...] + other[...]
    extra = jnp.sum(total, axis=0, keepdims=True)
    index = lax.broadcasted_iota(jnp.int32, value.shape, 0)
    value = value + jnp.where(index == ROWS - 1, extra, 0.0)
    for d in range(out.shape[0]):
        out[d] = value


def final_kernel(parts, t0, t1, t2, t3, t4, out, buf, sems):
    n = ITERATIONS
    value = parts[0]
    for d in range(1, parts.shape[0]):
        value = value + parts[d]
    gram = {}
    for k, (i, j) in enumerate(PAIRS):
        gram[i, j] = gram[j, i] = value[k : k + 1]
    matrix = {}
    for i in range(n):
        for j in range(i, n):
            terms = []
            if j + 1 < n:
                terms.append(gram[i, j + 1] + SHIFTS[j] * gram[i, j])
            if i + 1 < n and i != j:
                terms.append(gram[i + 1, j] + SHIFTS[i] * gram[i, j])
            if not terms:
                terms = [value[ROWS - 1 : ROWS]]
            product = terms[0] if len(terms) == 1 else 0.5 * (terms[0] + terms[1])
            matrix[i, j] = gram[i, j] - DAMP * product
    scale = [
        jnp.where(matrix[i, i] > 0.0, lax.rsqrt(jnp.maximum(matrix[i, i], 1e-37)), 0.0)
        for i in range(n)
    ]
    for i in range(n):
        for j in range(i, n):
            matrix[i, j] = matrix[i, j] * (scale[i] * scale[j])
    right = [gram[i, 0] * scale[i] for i in range(n)]
    inverse = []
    for k in range(n):
        pivot = matrix[k, k]
        inverse.append(jnp.where(pivot > PIVOT_MIN, 1.0 / jnp.maximum(pivot, PIVOT_MIN), 0.0))
        for i in range(k + 1, n):
            factor = matrix[k, i] * inverse[k]
            for j in range(i, n):
                matrix[i, j] = matrix[i, j] - factor * matrix[k, j]
            right[i] = right[i] - factor * right[k]
    coef = [None] * n
    for k in range(n - 1, -1, -1):
        rest = right[k]
        for j in range(k + 1, n):
            rest = rest - matrix[k, j] * coef[j]
        coef[k] = rest * inverse[k]
    coef = [coef[k] * scale[k] for k in range(n)]
    fields = (t0, t1, t2, t3, t4)
    count, rows, _ = t0.shape
    chunks = sems.shape[0]
    per = count // chunks
    copies = []
    for c in range(chunks):
        for g in range(c * per, (c + 1) * per):
            total = None
            for f, k in zip(fields, coef):
                term = f[g] * k
                total = term if total is None else total + term
            buf[pl.ds(g * rows, rows), :] = total
        part = pl.ds(c * per * rows, per * rows)
        copy = pltpu.make_async_copy(buf.at[part], out.at[part], sems.at[c])
        copy.start()
        copies.append(copy)
    for copy in copies:
        copy.wait()


def to_chip_partner(block, axis):
    return lax.ppermute(block, axis, [(i, i ^ 1) for i in range(lax.axis_size(axis))])


def shift(block, by, axis):
    n = lax.axis_size(axis)
    return lax.ppermute(block, axis, [(i, (i + by) % n) for i in range(n)])


def shards(descriptors, queries, affinity, tile_col):
    count, _, rows, _ = affinity.shape
    width = queries.shape[0]
    depth = descriptors.shape[1]
    axis = "dom"
    devices = lax.axis_size(axis)
    size = 128 * pl.cdiv(offsets(count)[-1], 128)
    blocks = count + 2 * NAMED + 1
    field = jax.ShapeDtypeStruct((count, rows, width), F32)
    split = jax.ShapeDtypeStruct((blocks, rows, 2 * width), BF)
    edge = jax.ShapeDtypeStruct((2 * NAMED, rows, width), BF)
    half = jax.ShapeDtypeStruct((NAMED, rows, width), BF)
    early = jax.ShapeDtypeStruct((len(EARLY), width), F32)
    edge_sum = jax.ShapeDtypeStruct((2 * NAMED, rows, width), F32)
    sums_h = pltpu.VMEM((2 * NAMED + 1, rows, width), F32)
    work = [pltpu.VMEM((2 * NAMED + 1, rows, width), BF)]
    chunks = count // 2
    flops = 2 * count * rows * 4 * rows * 2 * width

    def call(kernel, out_shape, products, scratch=(), aliases=None, limit=24):
        outs = out_shape if isinstance(out_shape, tuple) else (out_shape,)

        def run(*args):
            specs = [SMEM if x.dtype == jnp.int32 else VMEM for x in args]
            args = [
                pltpu.with_memory_space_constraint(x, pltpu.SMEM) if x.dtype == jnp.int32 else x
                for x in args
            ]
            return pl.pallas_call(
                kernel,
                out_shape=out_shape,
                in_specs=specs,
                out_specs=(VMEM,) * len(outs) if isinstance(out_shape, tuple) else VMEM,
                scratch_shapes=list(scratch),
                input_output_aliases=aliases or {},
                compiler_params=params(limit),
                cost_estimate=pl.CostEstimate(
                    flops=int(products * flops), bytes_accessed=4 << 20, transcendentals=0
                ),
            )(*args)

        return run

    operands = (descriptors, queries, affinity, tile_col.T)
    t0, hl0, send_b, aff, tab = pl.pallas_call(
        functools.partial(first_kernel, chunks=chunks, axis=axis),
        out_shape=(
            field,
            split,
            edge,
            jax.ShapeDtypeStruct(affinity.shape, BF),
            pltpu.SMEM((size,), jnp.int32),
        ),
        in_specs=[HBM] * 4,
        out_specs=(VMEM,) * 4 + (SMEM,),
        scratch_shapes=[
            pltpu.VMEM((chunks, count * rows // chunks, depth), BF),
            pltpu.VMEM((width, depth), BF),
            pltpu.VMEM((depth, width), BF),
            pltpu.SMEM((4, count), jnp.int32),
            pltpu.SMEM((3, count + 1), jnp.int32),
            pltpu.SMEM((3, count + 1), jnp.int32),
            pltpu.SemaphoreType.DMA((chunks + 3,)),
        ],
        compiler_params=params(24),
        cost_estimate=pl.CostEstimate(flops=flops, bytes_accessed=4 << 20, transcendentals=0),
        name="first",
    )(*(pltpu.with_memory_space_constraint(x, pltpu.HBM) for x in operands))
    recv_even = shift(send_b, 1, axis)
    recv_odd = shift(send_b, -1, axis)
    part, hl1, halo_part, send_a = call(
        functools.partial(rest_kernel, step=0), (field, split, edge_sum, edge), 1, [sums_h]
    )(tab, aff, t0, hl0)
    recv_a = to_chip_partner(send_a, axis)

    def by_parity(kernel, parity, edges, aliased):
        fields = (split, field, field, split)
        return call(
            functools.partial(kernel, parity=parity, axis=axis),
            fields + (edges,),
            2,
            work,
            {2 + i: i for i in range(aliased)},
        )

    hl1, t1, t2, hl2, send = by_parity(middle_kernel, 0, edge, 2)(
        tab, aff, hl1, part, halo_part, recv_a, recv_even
    )
    got_odd = shift(send, -1, axis)
    hl1, t1, t2, hl2, send = by_parity(middle_kernel, 1, edge, 4)(
        tab, aff, hl1, t1, t2, hl2, halo_part, recv_a, recv_odd
    )
    got_even = shift(send, 1, axis)
    part, hl3, halo_part, send_a = call(
        functools.partial(rest_kernel, step=2), (field, split, edge_sum, edge), 1, [sums_h]
    )(tab, aff, t2, hl2)
    recv_a = to_chip_partner(send_a, axis)
    gram = call(early_kernel, early, 0.1)(t0, t1, t2)
    hl3, t3, t4, hl4, send = by_parity(last_kernel, 1, half, 2)(
        tab, aff, hl3, part, halo_part, recv_a, got_odd
    )
    recv_even = shift(send, 1, axis)
    hl3, t3, t4, hl4, send = by_parity(last_kernel, 0, half, 4)(
        tab, aff, hl3, t3, t4, hl4, halo_part, recv_a, got_even
    )
    recv_odd = shift(send, -1, axis)
    gram, weight, send_a = call(
        gram_kernel, (jax.ShapeDtypeStruct((ROWS, width), F32), edge_sum, half), 1, [sums_h]
    )(tab, aff, t0, t1, t2, t3, t4, hl4, gram)
    recv_a = to_chip_partner(send_a, axis)
    other = to_chip_partner(gram, axis)
    parts = call(
        functools.partial(cross_kernel, axis=axis),
        jax.ShapeDtypeStruct((devices // 2, ROWS, width), F32),
        0.1,
        [pltpu.VMEM((NAMED, rows, width), BF)],
        limit=8,
    )(weight, recv_a, recv_even, recv_odd, gram, other)
    groups = [list(range(core, devices, 2)) for core in range(2)]
    parts = lax.all_to_all(parts, axis, 0, 0, axis_index_groups=groups)
    return pl.pallas_call(
        final_kernel,
        out_shape=jax.ShapeDtypeStruct((count * rows, width), F32),
        in_specs=[VMEM] * 6,
        out_specs=HBM,
        scratch_shapes=[
            pltpu.VMEM((count * rows, width), F32),
            pltpu.SemaphoreType.DMA((count // 3,)),
        ],
        compiler_params=params(24),
        name="final",
    )(parts, t0, t1, t2, t3, t4)


def solution(mesh):
    return jax.shard_map(
        shards,
        mesh=mesh,
        in_specs=(
            P(("region", "dom"), None),
            P("region", None),
            P(("region", "dom"), None, None, None),
            P(("region", "dom"), None),
        ),
        out_specs=P(("region", "dom"), None),
        check_vma=False,
    )
```

```python
import functools

import jax
import jax.numpy as jnp
from jax import lax
from jax.experimental import pallas as pl
from jax.experimental.pallas import tpu as pltpu
from jax.sharding import PartitionSpec as P

HALO_W = 6
NAMED = 3
ITERATIONS = 5
DAMP = 0.99
SHIFTS = (0.0, 1.0, -0.25, 0.5)
PIVOT_MIN = 1e-6
BF = jnp.bfloat16
F32 = jnp.float32
EARLY = [(i, j) for i in range(3) for j in range(i, 3)]
LATE = [(2, 3), (3, 3), (3, 4), (4, 4)]
PAIRS = EARLY + LATE
ROWS = len(PAIRS) + 1
ENTRIES = 2 + 2 * NAMED

VMEM = pl.BlockSpec(memory_space=pltpu.VMEM)
SMEM = pl.BlockSpec(memory_space=pltpu.SMEM)
HBM = pl.BlockSpec(memory_space=pltpu.HBM)


def params(mib):
    return pltpu.CompilerParams(vmem_limit_bytes=mib << 20)


def dot(a, b):
    return jnp.dot(a, b, preferred_element_type=F32)


def dot_t(a, b):
    return lax.dot_general(a, b, (((0,), (0,)), ((), ())), preferred_element_type=F32)


def put_split(ref, index, value):
    high = value.astype(BF)
    width = value.shape[-1]
    ref[index, :, :width] = high
    ref[index, :, width:] = (value - high.astype(F32)).astype(BF)


def row_product(aff, tab, base, g, hl):
    count = aff.shape[0]
    width = hl.shape[2] // 2
    if isinstance(g, int):
        low = g - 1 if g > 0 else tab[base + count]
        high = g + 1 if g + 1 < count else tab[base + count + 1]
    else:
        low = jnp.where(g > 0, g - 1, tab[base + count])
        high = jnp.where(g + 1 < count, g + 1, tab[base + count + 1])
    left = jnp.concatenate([aff[g, 0], aff[g, 1]], axis=1)
    right = jnp.concatenate([hl[g], hl[low]], axis=0)
    out = dot(left, right)
    left = jnp.concatenate([aff[g, 2], aff[g, 3]], axis=1)
    right = jnp.concatenate([hl[high], hl[tab[base + g]]], axis=0)
    out = out + dot(left, right)
    return out[:, :width] + out[:, width:]


def shifted(value, shift, t):
    return value if shift == 0.0 else value - shift * t


def offsets(count):
    full = count + 2
    lists = 2 * full
    cross = lists + 2 * NAMED
    return full, lists, cross, cross + 3 * ENTRIES


def fill_table(tile_col, tab, up_rows, low_rows, axis):
    count = tile_col.shape[1]
    total = count * lax.axis_size(axis)
    me = lax.axis_index(axis)
    even = lax.rem(me, 2) == 0
    full, lists, cross, _ = offsets(count)
    zero = count + 2 * NAMED
    up_base = jnp.where(even, 0, NAMED)
    low_base = NAMED - up_base
    relative, ups, lows = [], [], []
    up_mask = jnp.int32(1)
    low_mask = jnp.int32(1 << (HALO_W - 1))
    for g in range(count):
        rel = tile_col[3, g] - me * count
        rel = jnp.where(rel < 0, rel + total, rel)
        up = (rel >= count) & (rel < count + HALO_W)
        low = rel >= total - HALO_W
        place = jnp.where(up, rel - count, rel - (total - HALO_W))
        place = jnp.clip(place, 0, HALO_W - 1)
        bit = lax.shift_left(jnp.int32(1), place)
        up_mask = up_mask | jnp.where(up, bit, 0)
        low_mask = low_mask | jnp.where(low, bit, 0)
        relative.append((rel, place, bit))
        ups.append(up)
        lows.append(low)
    yield
    up_count = low_count = up_cross = low_cross = jnp.int32(0)
    for g in range(count):
        if g == count // 2:
            yield
        rel, place, bit = relative[g]
        below = jnp.where(ups[g], up_mask, low_mask) & (bit - 1)
        rank = below & 1
        for p in range(1, HALO_W - 1):
            rank = rank + (lax.shift_right_logical(below, jnp.int32(p)) & 1)
        halo = jnp.where(ups[g], up_base, low_base) + jnp.minimum(rank, NAMED - 1)
        local = rel < count
        tab[g] = jnp.where(local, rel, zero)
        tab[full + g] = jnp.where(local, rel, count + halo)
        up_rows[0, up_count] = g
        low_rows[0, low_count] = g
        up_rows[1, up_cross] = g
        low_rows[1, low_cross] = g
        up_rows[2, up_cross] = halo
        low_rows[2, low_cross] = halo
        up_cross = up_cross + jnp.where(ups[g], 1, 0)
        low_cross = low_cross + jnp.where(lows[g], 1, 0)
        up_count = up_count + (1 if g == count - 1 else jnp.where(ups[g], 1, 0))
        low_count = low_count + (1 if g == 0 else jnp.where(lows[g], 1, 0))
    tab[count] = zero
    tab[count + 1] = zero
    tab[full + count] = count + low_base + NAMED - 1
    tab[full + count + 1] = count + up_base
    for j in range(NAMED):
        up, low = up_rows[0, j], low_rows[0, j]
        tab[lists + j] = jnp.where(even, up, low)
        tab[lists + NAMED + j] = jnp.where(even, low, up)
    chains = ((0, 1, low_base + NAMED - 1), (count - 1, 2, up_base))
    for side, (rows, used) in enumerate(((low_rows, low_cross), (up_rows, up_cross))):
        for i in range(3):
            tab[cross + 3 * side * (1 + NAMED) + i] = jnp.int32(chains[side][i])
        for j in range(NAMED):
            at = cross + 3 * (side * (1 + NAMED) + 1 + j)
            tab[at] = jnp.where(j < used, rows[1, j], 0)
            tab[at + 1] = jnp.int32(3)
            tab[at + 2] = jnp.where(j < used, rows[2, j], 2 * NAMED)
    yield


def pack(tab, shift, aff, t, hl, send, base):
    width = t.shape[2]
    for j in range(NAMED):
        g = tab[base + j]
        send[j] = hl[g, :, :width]
        send[NAMED + j] = shifted(row_product(aff, tab, 0, g, hl), shift, t[g]).astype(BF)


def first_kernel(
    desc, queries, affinity, tile_col, t0, hl, send_b, aff, tab,
    buf, wide, tall, cols, up_rows, low_rows, sems, *, chunks, axis,
):
    count, rows = t0.shape[0], t0.shape[1]
    per = count // chunks
    _, lists, _, _ = offsets(count)
    load_q = pltpu.make_async_copy(queries, wide, sems.at[chunks])
    load_c = pltpu.make_async_copy(tile_col, cols, sems.at[chunks + 1])
    load_q.start()
    load_c.start()
    copies = []
    for c in range(chunks):
        copy = pltpu.make_async_copy(
            desc.at[pl.ds(c * per * rows, per * rows)], buf.at[c], sems.at[c]
        )
        copy.start()
        copies.append(copy)
    load_a = pltpu.make_async_copy(affinity, aff, sems.at[chunks + 2])
    load_a.start()
    hl[count + 2 * NAMED] = jnp.zeros(hl.shape[1:], BF)
    load_q.wait()
    tall[...] = wide[...].T
    load_c.wait()

    def finish(c):
        for g in range(c * per, (c + 1) * per):
            value = jnp.maximum(t0[g], 0.0)
            value = value * value * value
            t0[g] = value
            put_split(hl, g, value)

    stages = fill_table(cols, tab, up_rows, low_rows, axis)
    for c in range(chunks):
        copies[c].wait()
        next(stages)
        scores = dot(buf[c], tall[...])
        for i in range(per):
            t0[c * per + i] = scores[i * rows : (i + 1) * rows]
        if c > 0:
            finish(c - 1)
    finish(chunks - 1)
    load_a.wait()
    pack(tab, SHIFTS[0], aff, t0, hl, send_b, lists + NAMED)


def add_products(sums, pairs, fields):
    count, rows, _ = fields[0].shape
    group = 32

    def body(i, sums):
        sums = list(sums)
        g = i // (rows // group)
        start = (i % (rows // group)) * group
        for part in range(group // 8):
            at = pl.ds(pl.multiple_of(start + 8 * part, 8), 8)
            v = [f[g, at, :] for f in fields]
            for n, (a, b) in enumerate(pairs):
                sums[n] = sums[n] + v[a] * v[b]
        return tuple(sums)

    return list(lax.fori_loop(0, count * rows // group, body, tuple(sums)))


def halo_products(tab, aff, hl, sums, factor):
    count = aff.shape[0]
    width = sums.shape[2]
    _, _, cross, _ = offsets(count)
    sums[...] = jnp.zeros(sums.shape, F32)
    for e in range(ENTRIES):
        g, slot, h = (tab[cross + 3 * e + i] for i in range(3))
        both = dot_t(aff[g, slot], hl[g])
        both = both[:, :width] + both[:, width:]
        sums[h] += both if factor == 1.0 else factor * both


def rest_kernel(tab, aff, t, hl, part, hl_next, halo_part, send_a, sums, *, step):
    count = t.shape[0]
    _, lists, _, _ = offsets(count)
    pack(tab, SHIFTS[step], aff, t, hl, send_a, lists)
    hl_next[count + 2 * NAMED] = jnp.zeros(hl.shape[1:], BF)
    for g in range(count):
        value = shifted(row_product(aff, tab, 0, g, hl), SHIFTS[step], t[g])
        part[g] = value
        put_split(hl_next, g, value)
    halo_products(tab, aff, hl, sums, 1.0)
    for h in range(2 * NAMED):
        halo_part[h] = sums[h]


def early_kernel(t0, t1, t2, out):
    sums = [jnp.zeros((8, t0.shape[2]), F32) for _ in EARLY]
    for n, total in enumerate(add_products(sums, EARLY, (t0, t1, t2))):
        out[pl.ds(n, 1), :] = jnp.sum(total, axis=0, keepdims=True)


def two_steps(tab, aff, hl1, t1, halo_part, recv_a, recv_b, t2, hl2, halo, step):
    count, _, width = t2.shape
    full, lists, cross, _ = offsets(count)
    zeros = jnp.zeros(hl2.shape[1:], BF)
    hl2[count + 2 * NAMED] = zeros
    halo[2 * NAMED] = zeros[:, :width]
    for h in range(NAMED):
        halo[h] = recv_a[h]
        halo[NAMED + h] = recv_b[h]
        low, high = h, NAMED + h
        put_split(hl1, count + low, recv_a[NAMED + h].astype(F32) + halo_part[low])
        put_split(hl1, count + high, recv_b[NAMED + h].astype(F32) + halo_part[high])
    for e in range(ENTRIES):
        g, slot, h = (tab[cross + 3 * e + i] for i in range(3))
        t1[g] += dot(aff[g, slot], halo[h])
    for j in range(2 * NAMED):
        g = tab[lists + j]
        put_split(hl1, g, t1[g])
    for g in range(count):
        value = shifted(row_product(aff, tab, full, g, hl1), SHIFTS[step + 1], t1[g])
        t2[g] = value
        put_split(hl2, g, value)


def middle_kernel(tab, aff, *refs, parity, axis):
    halo_part, recv_a, recv_b = refs[-9:-6]
    hl1, t1, t2, hl2, send_b, halo = refs[-6:]
    _, lists, _, _ = offsets(t1.shape[0])
    active = lax.rem(lax.axis_index(axis), 2) == parity

    @pl.when(active)
    def _():
        two_steps(tab, aff, hl1, t1, halo_part, recv_a, recv_b, t2, hl2, halo, 0)
        pack(tab, SHIFTS[2], aff, t2, hl2, send_b, lists + NAMED)

    @pl.when(jnp.logical_not(active))
    def _():
        send_b[...] = jnp.zeros(send_b.shape, BF)


def last_kernel(tab, aff, *refs, parity, axis):
    halo_part, recv_a, recv_b = refs[-10:-7]
    hl3, t3, t4, hl4, send_b, send_a, halo = refs[-7:]
    width = t3.shape[2]
    _, lists, _, _ = offsets(t3.shape[0])
    active = lax.rem(lax.axis_index(axis), 2) == parity

    @pl.when(active)
    def _():
        two_steps(tab, aff, hl3, t3, halo_part, recv_a, recv_b, t4, hl4, halo, 2)
        for j in range(NAMED):
            send_b[j] = hl4[tab[lists + NAMED + j], :, :width]
            send_a[j] = hl4[tab[lists + j], :, :width]

    @pl.when(jnp.logical_not(active))
    def _():
        send_b[...] = jnp.zeros(send_b.shape, BF)


def gram_kernel(tab, aff, t2, t3, t4, hl, early, out):
    count, rows, width = t2.shape
    sums = [jnp.zeros((8, width), F32) for _ in range(len(LATE) + 1)]
    fields = (None, None, t2, t3, t4)
    for g in range(count):
        local = row_product(aff, tab, 0, g, hl)
        v = [None if f is None else f[g] for f in fields]
        terms = [v[i] * v[j] for i, j in LATE] + [v[-1] * local]
        for n, term in enumerate(terms):
            sums[n] = sums[n] + term.reshape(rows // 8, 8, width).sum(0)
    out[pl.ds(0, len(EARLY)), :] = early[...]
    for n, total in enumerate(sums):
        out[pl.ds(len(EARLY) + n, 1), :] = jnp.sum(total, axis=0, keepdims=True)


def weight_kernel(tab, aff, hl, weight, sums):
    halo_products(tab, aff, hl, sums, 2.0)
    for h in range(2 * NAMED):
        weight[h] = sums[h]


def cross_kernel(weight, recv_a, recv_even, recv_odd, gram, other, out, recv_b, *, axis):
    _, rows, width = weight.shape
    even = lax.rem(lax.axis_index(axis), 2) == 0

    @pl.when(even)
    def _():
        recv_b[...] = recv_even[...]

    @pl.when(jnp.logical_not(even))
    def _():
        recv_b[...] = recv_odd[...]

    total = jnp.zeros((8, width), F32)
    for h in range(NAMED):
        part = weight[h] * recv_a[h].astype(F32) + weight[NAMED + h] * recv_b[h].astype(F32)
        total = total + part.reshape(rows // 8, 8, width).sum(0)
    value = gram[...] + other[...]
    extra = jnp.sum(total, axis=0, keepdims=True)
    index = lax.broadcasted_iota(jnp.int32, value.shape, 0)
    value = value + jnp.where(index == ROWS - 1, extra, 0.0)
    for d in range(out.shape[0]):
        out[d] = value


def final_kernel(parts, t0, t1, t2, t3, t4, out, buf, sems):
    n = ITERATIONS
    value = parts[0]
    for d in range(1, parts.shape[0]):
        value = value + parts[d]
    gram = {}
    for k, (i, j) in enumerate(PAIRS):
        gram[i, j] = gram[j, i] = value[k : k + 1]
    for j in range(2, n - 1):
        for i in range(n - 2):
            if (i, j + 1) not in gram:
                entry = gram[i + 1, j] + (SHIFTS[i] - SHIFTS[j]) * gram[i, j]
                gram[i, j + 1] = gram[j + 1, i] = entry
    matrix = {}
    for i in range(n):
        for j in range(i, n):
            if i + 1 < n and j + 1 == n:
                product = gram[i + 1, j] + SHIFTS[i] * gram[i, j]
            elif j + 1 < n:
                product = gram[i, j + 1] + SHIFTS[j] * gram[i, j]
            else:
                product = value[ROWS - 1 : ROWS]
            matrix[i, j] = gram[i, j] - DAMP * product
    scale = [
        jnp.where(matrix[i, i] > 0.0, lax.rsqrt(jnp.maximum(matrix[i, i], 1e-37)), 0.0)
        for i in range(n)
    ]
    for i in range(n):
        for j in range(i, n):
            matrix[i, j] = matrix[i, j] * (scale[i] * scale[j])
    right = [gram[i, 0] * scale[i] for i in range(n)]
    inverse = []
    for k in range(n):
        pivot = matrix[k, k]
        inverse.append(jnp.where(pivot > PIVOT_MIN, 1.0 / jnp.maximum(pivot, PIVOT_MIN), 0.0))
        for i in range(k + 1, n):
            factor = matrix[k, i] * inverse[k]
            for j in range(i, n):
                matrix[i, j] = matrix[i, j] - factor * matrix[k, j]
            right[i] = right[i] - factor * right[k]
    coef = [None] * n
    for k in range(n - 1, -1, -1):
        rest = right[k]
        for j in range(k + 1, n):
            rest = rest - matrix[k, j] * coef[j]
        coef[k] = rest * inverse[k]
    coef = [coef[k] * scale[k] for k in range(n)]
    fields = (t0, t1, t2, t3, t4)
    count, rows, _ = t0.shape
    chunks = sems.shape[0]
    per = count // chunks
    copies = []
    for c in range(chunks):
        for g in range(c * per, (c + 1) * per):
            total = None
            for f, k in zip(fields, coef):
                term = f[g] * k
                total = term if total is None else total + term
            buf[pl.ds(g * rows, rows), :] = total
        part = pl.ds(c * per * rows, per * rows)
        copy = pltpu.make_async_copy(buf.at[part], out.at[part], sems.at[c])
        copy.start()
        copies.append(copy)
    for copy in copies:
        copy.wait()


def to_chip_partner(block, axis):
    return lax.ppermute(block, axis, [(i, i ^ 1) for i in range(lax.axis_size(axis))])


def shift(block, by, axis):
    n = lax.axis_size(axis)
    return lax.ppermute(block, axis, [(i, (i + by) % n) for i in range(n)])


def shards(descriptors, queries, affinity, tile_col):
    count, _, rows, _ = affinity.shape
    width = queries.shape[0]
    depth = descriptors.shape[1]
    axis = "dom"
    devices = lax.axis_size(axis)
    size = 128 * pl.cdiv(offsets(count)[-1], 128)
    blocks = count + 2 * NAMED + 1
    field = jax.ShapeDtypeStruct((count, rows, width), F32)
    split = jax.ShapeDtypeStruct((blocks, rows, 2 * width), BF)
    edge = jax.ShapeDtypeStruct((2 * NAMED, rows, width), BF)
    half = jax.ShapeDtypeStruct((NAMED, rows, width), BF)
    early = jax.ShapeDtypeStruct((len(EARLY), width), F32)
    edge_sum = jax.ShapeDtypeStruct((2 * NAMED, rows, width), F32)
    sums_h = pltpu.VMEM((2 * NAMED + 1, rows, width), F32)
    work = [pltpu.VMEM((2 * NAMED + 1, rows, width), BF)]
    chunks = 3
    flops = 2 * count * rows * 4 * rows * 2 * width

    def call(kernel, out_shape, products, scratch=(), aliases=None, limit=24):
        outs = out_shape if isinstance(out_shape, tuple) else (out_shape,)

        def run(*args):
            specs = [SMEM if x.dtype == jnp.int32 else VMEM for x in args]
            args = [
                pltpu.with_memory_space_constraint(x, pltpu.SMEM) if x.dtype == jnp.int32 else x
                for x in args
            ]
            return pl.pallas_call(
                kernel,
                out_shape=out_shape,
                in_specs=specs,
                out_specs=(VMEM,) * len(outs) if isinstance(out_shape, tuple) else VMEM,
                scratch_shapes=list(scratch),
                input_output_aliases=aliases or {},
                compiler_params=params(limit),
                cost_estimate=pl.CostEstimate(
                    flops=int(products * flops), bytes_accessed=4 << 20, transcendentals=0
                ),
            )(*args)

        return run

    operands = (descriptors, queries, affinity, tile_col.T)
    t0, hl0, send_b, aff, tab = pl.pallas_call(
        functools.partial(first_kernel, chunks=chunks, axis=axis),
        out_shape=(
            field,
            split,
            edge,
            jax.ShapeDtypeStruct(affinity.shape, BF),
            pltpu.SMEM((size,), jnp.int32),
        ),
        in_specs=[HBM] * 4,
        out_specs=(VMEM,) * 4 + (SMEM,),
        scratch_shapes=[
            pltpu.VMEM((chunks, count * rows // chunks, depth), BF),
            pltpu.VMEM((width, depth), BF),
            pltpu.VMEM((depth, width), BF),
            pltpu.SMEM((4, count), jnp.int32),
            pltpu.SMEM((3, count + 1), jnp.int32),
            pltpu.SMEM((3, count + 1), jnp.int32),
            pltpu.SemaphoreType.DMA((chunks + 3,)),
        ],
        compiler_params=params(24),
        cost_estimate=pl.CostEstimate(flops=flops, bytes_accessed=4 << 20, transcendentals=0),
        name="first",
    )(*(pltpu.with_memory_space_constraint(x, pltpu.HBM) for x in operands))
    recv_even = shift(send_b, 1, axis)
    recv_odd = shift(send_b, -1, axis)
    part, hl1, halo_part, send_a = call(
        functools.partial(rest_kernel, step=0), (field, split, edge_sum, edge), 1, [sums_h]
    )(tab, aff, t0, hl0)
    recv_a = to_chip_partner(send_a, axis)

    def by_parity(kernel, parity, edges, aliases):
        return call(
            functools.partial(kernel, parity=parity, axis=axis),
            (split, field, field, split, *edges),
            2,
            work,
            dict(aliases),
        )

    first_half = {2: 0, 3: 1}
    second_half = {2: 0, 3: 1, 4: 2, 5: 3}
    hl1, t1, t2, hl2, send = by_parity(middle_kernel, 0, (edge,), first_half)(
        tab, aff, hl1, part, halo_part, recv_a, recv_even
    )
    got_odd = shift(send, -1, axis)
    hl1, t1, t2, hl2, send = by_parity(middle_kernel, 1, (edge,), second_half)(
        tab, aff, hl1, t1, t2, hl2, halo_part, recv_a, recv_odd
    )
    got_even = shift(send, 1, axis)
    part, hl3, halo_part, send_a = call(
        functools.partial(rest_kernel, step=2), (field, split, edge_sum, edge), 1, [sums_h]
    )(tab, aff, t2, hl2)
    recv_a = to_chip_partner(send_a, axis)
    gram = call(early_kernel, early, 0.1)(t0, t1, t2)
    hl3, t3, t4, hl4, send, send_a = by_parity(last_kernel, 1, (half, half), first_half)(
        tab, aff, hl3, part, halo_part, recv_a, got_odd
    )
    recv_even = shift(send, 1, axis)
    last0 = by_parity(last_kernel, 0, (half, half), {**second_half, 6: 5})
    _, t3, t4, hl4, send, send_a = last0(
        tab, aff, hl3, t3, t4, hl4, send_a, halo_part, recv_a, got_even
    )
    recv_odd = shift(send, -1, axis)
    recv_a = to_chip_partner(send_a, axis)
    gram = call(
        gram_kernel, jax.ShapeDtypeStruct((ROWS, width), F32), 1
    )(tab, aff, t2, t3, t4, hl4, gram)
    other = to_chip_partner(gram, axis)
    weight = call(weight_kernel, edge_sum, 0.2, [sums_h])(tab, aff, hl4)
    parts = call(
        functools.partial(cross_kernel, axis=axis),
        jax.ShapeDtypeStruct((devices // 2, ROWS, width), F32),
        0.1,
        [pltpu.VMEM((NAMED, rows, width), BF)],
        limit=8,
    )(weight, recv_a, recv_even, recv_odd, gram, other)
    groups = [list(range(core, devices, 2)) for core in range(2)]
    parts = lax.all_to_all(parts, axis, 0, 0, axis_index_groups=groups)
    return pl.pallas_call(
        final_kernel,
        out_shape=jax.ShapeDtypeStruct((count * rows, width), F32),
        in_specs=[VMEM] * 6,
        out_specs=HBM,
        scratch_shapes=[
            pltpu.VMEM((count * rows, width), F32),
            pltpu.SemaphoreType.DMA((count // 3,)),
        ],
        compiler_params=params(24),
        name="final",
    )(parts, t0, t1, t2, t3, t4)


def solution(mesh):
    return jax.shard_map(
        shards,
        mesh=mesh,
        in_specs=(
            P(("region", "dom"), None),
            P("region", None),
            P(("region", "dom"), None, None, None),
            P(("region", "dom"), None),
        ),
        out_specs=P(("region", "dom"), None),
        check_vma=False,
    )
```

```python
import functools

import jax
import jax.numpy as jnp
from jax import lax
from jax.experimental import pallas as pl
from jax.experimental.pallas import tpu as pltpu
from jax.sharding import PartitionSpec as P

HALO_W = 6
NAMED = 3
ITERATIONS = 5
DAMP = 0.99
SHIFTS = (0.0, 1.0, -0.25, 0.5)
PIVOT_MIN = 1e-6
BF = jnp.bfloat16
F32 = jnp.float32
EARLY = [(i, j) for i in range(3) for j in range(i, 3)]
LATE = [(2, 3), (3, 3), (3, 4), (4, 4)]
PAIRS = EARLY + LATE
ROWS = len(PAIRS) + 1
ENTRIES = 2 + 2 * NAMED

VMEM = pl.BlockSpec(memory_space=pltpu.VMEM)
SMEM = pl.BlockSpec(memory_space=pltpu.SMEM)
HBM = pl.BlockSpec(memory_space=pltpu.HBM)


def params(mib):
    return pltpu.CompilerParams(vmem_limit_bytes=mib << 20)


def dot(a, b):
    return jnp.dot(a, b, preferred_element_type=F32)


def dot_t(a, b):
    return lax.dot_general(a, b, (((0,), (0,)), ((), ())), preferred_element_type=F32)


def put_rounded(ref, index, value):
    high = value.astype(BF)
    width = value.shape[-1]
    ref[index, :, :width] = high
    if ref.shape[2] > width:
        ref[index, :, width:] = (value - high.astype(F32)).astype(BF)


def folded(out):
    width = out.shape[0]
    return out if out.shape[1] == width else out[:, :width] + out[:, width:]


def row_product(aff, tab, base, g, hl):
    count = aff.shape[0]
    if isinstance(g, int):
        low = g - 1 if g > 0 else tab[base + count]
        high = g + 1 if g + 1 < count else tab[base + count + 1]
    else:
        low = jnp.where(g > 0, g - 1, tab[base + count])
        high = jnp.where(g + 1 < count, g + 1, tab[base + count + 1])
    left = jnp.concatenate([aff[g, 0], aff[g, 1]], axis=1)
    right = jnp.concatenate([hl[g], hl[low]], axis=0)
    out = dot(left, right)
    left = jnp.concatenate([aff[g, 2], aff[g, 3]], axis=1)
    right = jnp.concatenate([hl[high], hl[tab[base + g]]], axis=0)
    return folded(out + dot(left, right))


def shifted(value, shift, t):
    return value if shift == 0.0 else value - shift * t


def offsets(count):
    full = count + 2
    lists = 2 * full
    cross = lists + 2 * NAMED
    return full, lists, cross, cross + 3 * ENTRIES


def fill_table(tile_col, tab, up_rows, low_rows, axis):
    count = tile_col.shape[1]
    total = count * lax.axis_size(axis)
    me = lax.axis_index(axis)
    even = lax.rem(me, 2) == 0
    full, lists, cross, _ = offsets(count)
    zero = count + 2 * NAMED
    up_base = jnp.where(even, 0, NAMED)
    low_base = NAMED - up_base
    relative, ups, lows = [], [], []
    up_mask = jnp.int32(1)
    low_mask = jnp.int32(1 << (HALO_W - 1))
    for g in range(count):
        rel = tile_col[3, g] - me * count
        rel = jnp.where(rel < 0, rel + total, rel)
        up = (rel >= count) & (rel < count + HALO_W)
        low = rel >= total - HALO_W
        place = jnp.where(up, rel - count, rel - (total - HALO_W))
        place = jnp.clip(place, 0, HALO_W - 1)
        bit = lax.shift_left(jnp.int32(1), place)
        up_mask = up_mask | jnp.where(up, bit, 0)
        low_mask = low_mask | jnp.where(low, bit, 0)
        relative.append((rel, place, bit))
        ups.append(up)
        lows.append(low)
    yield
    up_count = low_count = up_cross = low_cross = jnp.int32(0)
    for g in range(count):
        if g == count // 2:
            yield
        rel, place, bit = relative[g]
        below = jnp.where(ups[g], up_mask, low_mask) & (bit - 1)
        rank = below & 1
        for p in range(1, HALO_W - 1):
            rank = rank + (lax.shift_right_logical(below, jnp.int32(p)) & 1)
        halo = jnp.where(ups[g], up_base, low_base) + jnp.minimum(rank, NAMED - 1)
        local = rel < count
        tab[g] = jnp.where(local, rel, zero)
        tab[full + g] = jnp.where(local, rel, count + halo)
        up_rows[0, up_count] = g
        low_rows[0, low_count] = g
        up_rows[1, up_cross] = g
        low_rows[1, low_cross] = g
        up_rows[2, up_cross] = halo
        low_rows[2, low_cross] = halo
        up_cross = up_cross + jnp.where(ups[g], 1, 0)
        low_cross = low_cross + jnp.where(lows[g], 1, 0)
        up_count = up_count + (1 if g == count - 1 else jnp.where(ups[g], 1, 0))
        low_count = low_count + (1 if g == 0 else jnp.where(lows[g], 1, 0))
    tab[count] = zero
    tab[count + 1] = zero
    tab[full + count] = count + low_base + NAMED - 1
    tab[full + count + 1] = count + up_base
    for j in range(NAMED):
        up, low = up_rows[0, j], low_rows[0, j]
        tab[lists + j] = jnp.where(even, up, low)
        tab[lists + NAMED + j] = jnp.where(even, low, up)
    chains = ((0, 1, low_base + NAMED - 1), (count - 1, 2, up_base))
    for side, (rows, used) in enumerate(((low_rows, low_cross), (up_rows, up_cross))):
        for i in range(3):
            tab[cross + 3 * side * (1 + NAMED) + i] = jnp.int32(chains[side][i])
        for j in range(NAMED):
            at = cross + 3 * (side * (1 + NAMED) + 1 + j)
            tab[at] = jnp.where(j < used, rows[1, j], 0)
            tab[at + 1] = jnp.int32(3)
            tab[at + 2] = jnp.where(j < used, rows[2, j], 2 * NAMED)
    yield


def pack(tab, shift, aff, t, hl, send, base):
    width = t.shape[2]
    for j in range(NAMED):
        g = tab[base + j]
        send[j] = hl[g, :, :width]
        send[NAMED + j] = shifted(row_product(aff, tab, 0, g, hl), shift, t[g]).astype(BF)


def first_kernel(
    desc, queries, affinity, tile_col, t0, hl, send_b, aff, tab,
    buf, wide, tall, cols, up_rows, low_rows, sems, *, bounds, axis,
):
    count, rows = t0.shape[0], t0.shape[1]
    chunks = len(bounds) - 1
    parts = [pl.ds(a * rows, (b - a) * rows) for a, b in zip(bounds, bounds[1:])]
    _, lists, _, _ = offsets(count)
    load_q = pltpu.make_async_copy(queries, wide, sems.at[chunks])
    load_c = pltpu.make_async_copy(tile_col, cols, sems.at[chunks + 1])
    load_q.start()
    load_c.start()
    copies = []
    for c in range(chunks):
        copy = pltpu.make_async_copy(desc.at[parts[c]], buf.at[parts[c]], sems.at[c])
        copy.start()
        copies.append(copy)
    load_a = pltpu.make_async_copy(affinity, aff, sems.at[chunks + 2])
    load_a.start()
    hl[count + 2 * NAMED] = jnp.zeros(hl.shape[1:], BF)
    load_q.wait()
    tall[...] = wide[...].T
    load_c.wait()

    def finish(c):
        for g in range(bounds[c], bounds[c + 1]):
            value = jnp.maximum(t0[g], 0.0)
            value = value * value * value
            t0[g] = value
            put_rounded(hl, g, value)

    stages = fill_table(cols, tab, up_rows, low_rows, axis)
    for c in range(chunks):
        copies[c].wait()
        next(stages, None)
        scores = dot(buf[parts[c], :], tall[...])
        for i, g in enumerate(range(bounds[c], bounds[c + 1])):
            t0[g] = scores[i * rows : (i + 1) * rows]
        if c > 0:
            finish(c - 1)
    finish(chunks - 1)
    load_a.wait()
    pack(tab, SHIFTS[0], aff, t0, hl, send_b, lists + NAMED)


def add_products(sums, pairs, fields):
    count, rows, _ = fields[0].shape
    group = 32

    def body(i, sums):
        sums = list(sums)
        g = i // (rows // group)
        start = (i % (rows // group)) * group
        for part in range(group // 8):
            at = pl.ds(pl.multiple_of(start + 8 * part, 8), 8)
            v = [f[g, at, :] for f in fields]
            for n, (a, b) in enumerate(pairs):
                sums[n] = sums[n] + v[a] * v[b]
        return tuple(sums)

    return list(lax.fori_loop(0, count * rows // group, body, tuple(sums)))


def halo_products(tab, aff, hl, sums, factor):
    _, _, cross, _ = offsets(aff.shape[0])
    sums[...] = jnp.zeros(sums.shape, F32)
    for e in range(ENTRIES):
        g, slot, h = (tab[cross + 3 * e + i] for i in range(3))
        both = folded(dot_t(aff[g, slot], hl[g]))
        sums[h] += both if factor == 1.0 else factor * both


def rest_kernel(tab, aff, t, hl, part, hl_next, halo_part, send_a, sums, *, step):
    count = t.shape[0]
    _, lists, _, _ = offsets(count)
    pack(tab, SHIFTS[step], aff, t, hl, send_a, lists)
    hl_next[count + 2 * NAMED] = jnp.zeros(hl_next.shape[1:], BF)
    for g in range(count):
        value = shifted(row_product(aff, tab, 0, g, hl), SHIFTS[step], t[g])
        part[g] = value
        put_rounded(hl_next, g, value)
    halo_products(tab, aff, hl, sums, 1.0)
    for h in range(2 * NAMED):
        halo_part[h] = sums[h]


def early_kernel(t0, t1, t2, out):
    sums = [jnp.zeros((8, t0.shape[2]), F32) for _ in EARLY]
    for n, total in enumerate(add_products(sums, EARLY, (t0, t1, t2))):
        out[pl.ds(n, 1), :] = jnp.sum(total, axis=0, keepdims=True)


def two_steps(tab, aff, hl1, t1, halo_part, recv_a, recv_b, t2, hl2, halo, step):
    count, _, _ = t2.shape
    full, lists, cross, _ = offsets(count)
    hl1[count + 2 * NAMED] = jnp.zeros(hl1.shape[1:], BF)
    hl2[count + 2 * NAMED] = jnp.zeros(hl2.shape[1:], BF)
    halo[2 * NAMED] = jnp.zeros(halo.shape[1:], BF)
    for h in range(NAMED):
        halo[h] = recv_a[h]
        halo[NAMED + h] = recv_b[h]
        low, high = h, NAMED + h
        put_rounded(hl1, count + low, recv_a[NAMED + h].astype(F32) + halo_part[low])
        put_rounded(hl1, count + high, recv_b[NAMED + h].astype(F32) + halo_part[high])
    for e in range(ENTRIES):
        g, slot, h = (tab[cross + 3 * e + i] for i in range(3))
        t1[g] += dot(aff[g, slot], halo[h])
    for j in range(2 * NAMED):
        g = tab[lists + j]
        put_rounded(hl1, g, t1[g])
    for g in range(count):
        value = shifted(row_product(aff, tab, full, g, hl1), SHIFTS[step + 1], t1[g])
        t2[g] = value
        put_rounded(hl2, g, value)


def middle_kernel(tab, aff, *refs, parity, axis):
    halo_part, recv_a, recv_b = refs[-9:-6]
    hl1, t1, t2, hl2, send_b, halo = refs[-6:]
    _, lists, _, _ = offsets(t1.shape[0])
    active = lax.rem(lax.axis_index(axis), 2) == parity

    @pl.when(active)
    def _():
        two_steps(tab, aff, hl1, t1, halo_part, recv_a, recv_b, t2, hl2, halo, 0)
        pack(tab, SHIFTS[2], aff, t2, hl2, send_b, lists + NAMED)

    @pl.when(jnp.logical_not(active))
    def _():
        send_b[...] = jnp.zeros(send_b.shape, BF)


def last_kernel(tab, aff, *refs, parity, axis):
    halo_part, recv_a, recv_b = refs[-10:-7]
    hl3, t3, t4, hl4, send_b, send_a, halo = refs[-7:]
    width = t3.shape[2]
    _, lists, _, _ = offsets(t3.shape[0])
    active = lax.rem(lax.axis_index(axis), 2) == parity

    @pl.when(active)
    def _():
        two_steps(tab, aff, hl3, t3, halo_part, recv_a, recv_b, t4, hl4, halo, 2)
        for j in range(NAMED):
            send_b[j] = hl4[tab[lists + NAMED + j], :, :width]
            send_a[j] = hl4[tab[lists + j], :, :width]

    @pl.when(jnp.logical_not(active))
    def _():
        send_b[...] = jnp.zeros(send_b.shape, BF)


def gram_kernel(tab, aff, t2, t3, t4, hl, early, out):
    count, rows, width = t2.shape
    sums = [jnp.zeros((8, width), F32) for _ in range(len(LATE) + 1)]
    fields = (None, None, t2, t3, t4)
    for g in range(count):
        local = row_product(aff, tab, 0, g, hl)
        v = [None if f is None else f[g] for f in fields]
        terms = [v[i] * v[j] for i, j in LATE] + [v[-1] * local]
        for n, term in enumerate(terms):
            sums[n] = sums[n] + term.reshape(rows // 8, 8, width).sum(0)
    out[pl.ds(0, len(EARLY)), :] = early[...]
    for n, total in enumerate(sums):
        out[pl.ds(len(EARLY) + n, 1), :] = jnp.sum(total, axis=0, keepdims=True)


def weight_kernel(tab, aff, hl, weight, sums):
    halo_products(tab, aff, hl, sums, 2.0)
    for h in range(2 * NAMED):
        weight[h] = sums[h]


def cross_kernel(weight, recv_a, recv_even, recv_odd, gram, other, out, recv_b, *, axis):
    _, rows, width = weight.shape
    even = lax.rem(lax.axis_index(axis), 2) == 0

    @pl.when(even)
    def _():
        recv_b[...] = recv_even[...]

    @pl.when(jnp.logical_not(even))
    def _():
        recv_b[...] = recv_odd[...]

    total = jnp.zeros((8, width), F32)
    for h in range(NAMED):
        part = weight[h] * recv_a[h].astype(F32) + weight[NAMED + h] * recv_b[h].astype(F32)
        total = total + part.reshape(rows // 8, 8, width).sum(0)
    value = gram[...] + other[...]
    extra = jnp.sum(total, axis=0, keepdims=True)
    index = lax.broadcasted_iota(jnp.int32, value.shape, 0)
    value = value + jnp.where(index == ROWS - 1, extra, 0.0)
    for d in range(out.shape[0]):
        out[d] = value


def final_kernel(parts, t0, t1, t2, t3, t4, out, buf, sems):
    n = ITERATIONS
    value = parts[0]
    for d in range(1, parts.shape[0]):
        value = value + parts[d]
    gram = {}
    for k, (i, j) in enumerate(PAIRS):
        gram[i, j] = gram[j, i] = value[k : k + 1]
    for j in range(2, n - 1):
        for i in range(n - 2):
            if (i, j + 1) not in gram:
                entry = gram[i + 1, j] + (SHIFTS[i] - SHIFTS[j]) * gram[i, j]
                gram[i, j + 1] = gram[j + 1, i] = entry
    matrix = {}
    for i in range(n):
        for j in range(i, n):
            if i + 1 < n and j + 1 == n:
                product = gram[i + 1, j] + SHIFTS[i] * gram[i, j]
            elif j + 1 < n:
                product = gram[i, j + 1] + SHIFTS[j] * gram[i, j]
            else:
                product = value[ROWS - 1 : ROWS]
            matrix[i, j] = gram[i, j] - DAMP * product
    scale = [
        jnp.where(matrix[i, i] > 0.0, lax.rsqrt(jnp.maximum(matrix[i, i], 1e-37)), 0.0)
        for i in range(n)
    ]
    for i in range(n):
        for j in range(i, n):
            matrix[i, j] = matrix[i, j] * (scale[i] * scale[j])
    right = [gram[i, 0] * scale[i] for i in range(n)]
    inverse = []
    for k in range(n):
        pivot = matrix[k, k]
        inverse.append(jnp.where(pivot > PIVOT_MIN, 1.0 / jnp.maximum(pivot, PIVOT_MIN), 0.0))
        for i in range(k + 1, n):
            factor = matrix[k, i] * inverse[k]
            for j in range(i, n):
                matrix[i, j] = matrix[i, j] - factor * matrix[k, j]
            right[i] = right[i] - factor * right[k]
    coef = [None] * n
    for k in range(n - 1, -1, -1):
        rest = right[k]
        for j in range(k + 1, n):
            rest = rest - matrix[k, j] * coef[j]
        coef[k] = rest * inverse[k]
    coef = [coef[k] * scale[k] for k in range(n)]
    fields = (t0, t1, t2, t3, t4)
    count, rows, _ = t0.shape
    chunks = sems.shape[0]
    per = count // chunks
    copies = []
    for c in range(chunks):
        for g in range(c * per, (c + 1) * per):
            total = None
            for f, k in zip(fields, coef):
                term = f[g] * k
                total = term if total is None else total + term
            buf[pl.ds(g * rows, rows), :] = total
        part = pl.ds(c * per * rows, per * rows)
        copy = pltpu.make_async_copy(buf.at[part], out.at[part], sems.at[c])
        copy.start()
        copies.append(copy)
    for copy in copies:
        copy.wait()


def to_chip_partner(block, axis):
    return lax.ppermute(block, axis, [(i, i ^ 1) for i in range(lax.axis_size(axis))])


def shift(block, by, axis):
    n = lax.axis_size(axis)
    return lax.ppermute(block, axis, [(i, (i + by) % n) for i in range(n)])


def shards(descriptors, queries, affinity, tile_col):
    count, _, rows, _ = affinity.shape
    width = queries.shape[0]
    depth = descriptors.shape[1]
    axis = "dom"
    devices = lax.axis_size(axis)
    size = 128 * pl.cdiv(offsets(count)[-1], 128)
    blocks = count + 2 * NAMED + 1
    field = jax.ShapeDtypeStruct((count, rows, width), F32)
    rounded = jax.ShapeDtypeStruct((blocks, rows, width), BF)
    split = jax.ShapeDtypeStruct((blocks, rows, 2 * width), BF)
    edge = jax.ShapeDtypeStruct((2 * NAMED, rows, width), BF)
    half = jax.ShapeDtypeStruct((NAMED, rows, width), BF)
    early = jax.ShapeDtypeStruct((len(EARLY), width), F32)
    edge_sum = jax.ShapeDtypeStruct((2 * NAMED, rows, width), F32)
    sums_h = pltpu.VMEM((2 * NAMED + 1, rows, width), F32)
    work = [pltpu.VMEM((2 * NAMED + 1, rows, width), BF)]
    bounds = (0, count // 6, count // 2, count - count // 6, count)
    flops = 2 * count * rows * 4 * rows * 2 * width

    def call(kernel, out_shape, products, scratch=(), aliases=None, limit=24):
        outs = out_shape if isinstance(out_shape, tuple) else (out_shape,)

        def run(*args):
            specs = [SMEM if x.dtype == jnp.int32 else VMEM for x in args]
            args = [
                pltpu.with_memory_space_constraint(x, pltpu.SMEM) if x.dtype == jnp.int32 else x
                for x in args
            ]
            return pl.pallas_call(
                kernel,
                out_shape=out_shape,
                in_specs=specs,
                out_specs=(VMEM,) * len(outs) if isinstance(out_shape, tuple) else VMEM,
                scratch_shapes=list(scratch),
                input_output_aliases=aliases or {},
                compiler_params=params(limit),
                cost_estimate=pl.CostEstimate(
                    flops=int(products * flops), bytes_accessed=4 << 20, transcendentals=0
                ),
            )(*args)

        return run

    operands = (descriptors, queries, affinity, tile_col.T)
    t0, hl0, send_b, aff, tab = pl.pallas_call(
        functools.partial(first_kernel, bounds=bounds, axis=axis),
        out_shape=(
            field,
            rounded,
            edge,
            jax.ShapeDtypeStruct(affinity.shape, BF),
            pltpu.SMEM((size,), jnp.int32),
        ),
        in_specs=[HBM] * 4,
        out_specs=(VMEM,) * 4 + (SMEM,),
        scratch_shapes=[
            pltpu.VMEM((count * rows, depth), BF),
            pltpu.VMEM((width, depth), BF),
            pltpu.VMEM((depth, width), BF),
            pltpu.SMEM((4, count), jnp.int32),
            pltpu.SMEM((3, count + 1), jnp.int32),
            pltpu.SMEM((3, count + 1), jnp.int32),
            pltpu.SemaphoreType.DMA((len(bounds) + 2,)),
        ],
        compiler_params=params(24),
        cost_estimate=pl.CostEstimate(flops=flops, bytes_accessed=4 << 20, transcendentals=0),
        name="first",
    )(*(pltpu.with_memory_space_constraint(x, pltpu.HBM) for x in operands))
    recv_even = shift(send_b, 1, axis)
    recv_odd = shift(send_b, -1, axis)
    part, hl1, halo_part, send_a = call(
        functools.partial(rest_kernel, step=0), (field, split, edge_sum, edge), 1, [sums_h]
    )(tab, aff, t0, hl0)
    recv_a = to_chip_partner(send_a, axis)

    def by_parity(kernel, parity, before, edges, aliases):
        return call(
            functools.partial(kernel, parity=parity, axis=axis),
            (before, field, field, rounded, *edges),
            2,
            work,
            dict(aliases),
        )

    first_half = {2: 0, 3: 1}
    second_half = {2: 0, 3: 1, 4: 2, 5: 3}
    hl1, t1, t2, hl2, send = by_parity(middle_kernel, 0, split, (edge,), first_half)(
        tab, aff, hl1, part, halo_part, recv_a, recv_even
    )
    got_odd = shift(send, -1, axis)
    hl1, t1, t2, hl2, send = by_parity(middle_kernel, 1, split, (edge,), second_half)(
        tab, aff, hl1, t1, t2, hl2, halo_part, recv_a, recv_odd
    )
    got_even = shift(send, 1, axis)
    part, hl3, halo_part, send_a = call(
        functools.partial(rest_kernel, step=2), (field, rounded, edge_sum, edge), 1, [sums_h]
    )(tab, aff, t2, hl2)
    recv_a = to_chip_partner(send_a, axis)
    gram = call(early_kernel, early, 0.1)(t0, t1, t2)
    last1 = by_parity(last_kernel, 1, rounded, (half, half), first_half)
    hl3, t3, t4, hl4, send, send_a = last1(
        tab, aff, hl3, part, halo_part, recv_a, got_odd
    )
    recv_even = shift(send, 1, axis)
    last0 = by_parity(last_kernel, 0, rounded, (half, half), {**second_half, 6: 5})
    _, t3, t4, hl4, send, send_a = last0(
        tab, aff, hl3, t3, t4, hl4, send_a, halo_part, recv_a, got_even
    )
    recv_odd = shift(send, -1, axis)
    recv_a = to_chip_partner(send_a, axis)
    gram = call(
        gram_kernel, jax.ShapeDtypeStruct((ROWS, width), F32), 1
    )(tab, aff, t2, t3, t4, hl4, gram)
    other = to_chip_partner(gram, axis)
    weight = call(weight_kernel, edge_sum, 0.2, [sums_h])(tab, aff, hl4)
    parts = call(
        functools.partial(cross_kernel, axis=axis),
        jax.ShapeDtypeStruct((devices // 2, ROWS, width), F32),
        0.1,
        [pltpu.VMEM((NAMED, rows, width), BF)],
        limit=8,
    )(weight, recv_a, recv_even, recv_odd, gram, other)
    groups = [list(range(core, devices, 2)) for core in range(2)]
    parts = lax.all_to_all(parts, axis, 0, 0, axis_index_groups=groups)
    return pl.pallas_call(
        final_kernel,
        out_shape=jax.ShapeDtypeStruct((count * rows, width), F32),
        in_specs=[VMEM] * 6,
        out_specs=HBM,
        scratch_shapes=[
            pltpu.VMEM((count * rows, width), F32),
            pltpu.SemaphoreType.DMA((count // 3,)),
        ],
        compiler_params=params(24),
        name="final",
    )(parts, t0, t1, t2, t3, t4)


def solution(mesh):
    return jax.shard_map(
        shards,
        mesh=mesh,
        in_specs=(
            P(("region", "dom"), None),
            P("region", None),
            P(("region", "dom"), None, None, None),
            P(("region", "dom"), None),
        ),
        out_specs=P(("region", "dom"), None),
        check_vma=False,
    )
```

```python
import functools

import jax
import jax.numpy as jnp
from jax import lax
from jax.experimental import pallas as pl
from jax.experimental.pallas import tpu as pltpu
from jax.sharding import PartitionSpec as P

HALO_W = 6
NAMED = 3
ITERATIONS = 5
DAMP = 0.99
SHIFTS = (0.0, 1.0, -0.25, 0.5)
PIVOT_MIN = 1e-6
BF = jnp.bfloat16
F32 = jnp.float32
EARLY = [(i, j) for i in range(3) for j in range(i, 3)]
LATE = [(2, 3), (3, 3), (3, 4), (4, 4)]
PAIRS = EARLY + LATE
ROWS = len(PAIRS) + 1
ENTRIES = 2 + 2 * NAMED

VMEM = pl.BlockSpec(memory_space=pltpu.VMEM)
SMEM = pl.BlockSpec(memory_space=pltpu.SMEM)
HBM = pl.BlockSpec(memory_space=pltpu.HBM)


def params(mib):
    return pltpu.CompilerParams(vmem_limit_bytes=mib << 20)


def dot(a, b):
    return jnp.dot(a, b, preferred_element_type=F32)


def dot_t(a, b):
    return lax.dot_general(a, b, (((0,), (0,)), ((), ())), preferred_element_type=F32)


def put_rounded(ref, index, value):
    high = value.astype(BF)
    width = value.shape[-1]
    ref[index, :, :width] = high
    if ref.shape[2] > width:
        ref[index, :, width:] = (value - high.astype(F32)).astype(BF)


def folded(out):
    width = out.shape[0]
    return out if out.shape[1] == width else out[:, :width] + out[:, width:]


def row_product(aff, tab, base, g, hl):
    count = aff.shape[0]
    if isinstance(g, int):
        low = g - 1 if g > 0 else tab[base + count]
        high = g + 1 if g + 1 < count else tab[base + count + 1]
    else:
        low = jnp.where(g > 0, g - 1, tab[base + count])
        high = jnp.where(g + 1 < count, g + 1, tab[base + count + 1])
    left = jnp.concatenate([aff[g, 0], aff[g, 1]], axis=1)
    right = jnp.concatenate([hl[g], hl[low]], axis=0)
    out = dot(left, right)
    left = jnp.concatenate([aff[g, 2], aff[g, 3]], axis=1)
    right = jnp.concatenate([hl[high], hl[tab[base + g]]], axis=0)
    return folded(out + dot(left, right))


def shifted(value, shift, t):
    return value if shift == 0.0 else value - shift * t


def offsets(count):
    full = count + 2
    lists = 2 * full
    cross = lists + 2 * NAMED
    return full, lists, cross, cross + 3 * ENTRIES


def fill_table(tile_col, tab, up_rows, low_rows, axis):
    count = tile_col.shape[1]
    total = count * lax.axis_size(axis)
    me = lax.axis_index(axis)
    even = lax.rem(me, 2) == 0
    full, lists, cross, _ = offsets(count)
    zero = count + 2 * NAMED
    up_base = jnp.where(even, 0, NAMED)
    low_base = NAMED - up_base
    relative, ups, lows = [], [], []
    up_mask = jnp.int32(1)
    low_mask = jnp.int32(1 << (HALO_W - 1))
    for g in range(count):
        rel = tile_col[3, g] - me * count
        rel = jnp.where(rel < 0, rel + total, rel)
        up = (rel >= count) & (rel < count + HALO_W)
        low = rel >= total - HALO_W
        place = jnp.where(up, rel - count, rel - (total - HALO_W))
        place = jnp.clip(place, 0, HALO_W - 1)
        bit = lax.shift_left(jnp.int32(1), place)
        up_mask = up_mask | jnp.where(up, bit, 0)
        low_mask = low_mask | jnp.where(low, bit, 0)
        relative.append((rel, place, bit))
        ups.append(up)
        lows.append(low)
    up_count = low_count = up_cross = low_cross = jnp.int32(0)
    for g in range(count):
        rel, place, bit = relative[g]
        below = jnp.where(ups[g], up_mask, low_mask) & (bit - 1)
        rank = below & 1
        for p in range(1, HALO_W - 1):
            rank = rank + (lax.shift_right_logical(below, jnp.int32(p)) & 1)
        halo = jnp.where(ups[g], up_base, low_base) + jnp.minimum(rank, NAMED - 1)
        local = rel < count
        tab[g] = jnp.where(local, rel, zero)
        tab[full + g] = jnp.where(local, rel, count + halo)
        up_rows[0, up_count] = g
        low_rows[0, low_count] = g
        up_rows[1, up_cross] = g
        low_rows[1, low_cross] = g
        up_rows[2, up_cross] = halo
        low_rows[2, low_cross] = halo
        up_cross = up_cross + jnp.where(ups[g], 1, 0)
        low_cross = low_cross + jnp.where(lows[g], 1, 0)
        up_count = up_count + (1 if g == count - 1 else jnp.where(ups[g], 1, 0))
        low_count = low_count + (1 if g == 0 else jnp.where(lows[g], 1, 0))
    tab[count] = zero
    tab[count + 1] = zero
    tab[full + count] = count + low_base + NAMED - 1
    tab[full + count + 1] = count + up_base
    for j in range(NAMED):
        up, low = up_rows[0, j], low_rows[0, j]
        tab[lists + j] = jnp.where(even, up, low)
        tab[lists + NAMED + j] = jnp.where(even, low, up)
    chains = ((0, 1, low_base + NAMED - 1), (count - 1, 2, up_base))
    for side, (rows, used) in enumerate(((low_rows, low_cross), (up_rows, up_cross))):
        for i in range(3):
            tab[cross + 3 * side * (1 + NAMED) + i] = jnp.int32(chains[side][i])
        for j in range(NAMED):
            at = cross + 3 * (side * (1 + NAMED) + 1 + j)
            tab[at] = jnp.where(j < used, rows[1, j], 0)
            tab[at + 1] = jnp.int32(3)
            tab[at + 2] = jnp.where(j < used, rows[2, j], 2 * NAMED)


def pack(tab, shift, aff, t, hl, send, base):
    width = t.shape[2]
    for j in range(NAMED):
        g = tab[base + j]
        send[j] = hl[g, :, :width]
        send[NAMED + j] = shifted(row_product(aff, tab, 0, g, hl), shift, t[g]).astype(BF)


def first_kernel(
    desc, queries, affinity, tile_col, t0, hl, send_b, aff, tab,
    buf, wide, tall, cols, up_rows, low_rows, sems, *, bounds, axis,
):
    count, rows = t0.shape[0], t0.shape[1]
    chunks = len(bounds) - 1
    parts = [pl.ds(a * rows, (b - a) * rows) for a, b in zip(bounds, bounds[1:])]
    _, lists, _, _ = offsets(count)
    load_q = pltpu.make_async_copy(queries, wide, sems.at[chunks])
    load_c = pltpu.make_async_copy(tile_col, cols, sems.at[chunks + 1])
    load_q.start()
    load_c.start()
    copies = []
    for c in range(chunks):
        copy = pltpu.make_async_copy(desc.at[parts[c]], buf.at[parts[c]], sems.at[c])
        copy.start()
        copies.append(copy)
    load_a = pltpu.make_async_copy(affinity, aff, sems.at[chunks + 2])
    load_a.start()
    hl[count + 2 * NAMED] = jnp.zeros(hl.shape[1:], BF)
    load_q.wait()
    tall[...] = wide[...].T
    load_c.wait()

    def finish(c):
        for g in range(bounds[c], bounds[c + 1]):
            value = jnp.maximum(t0[g], 0.0)
            value = value * value * value
            t0[g] = value
            put_rounded(hl, g, value)

    for c in range(chunks):
        copies[c].wait()
        if c == 0:
            fill_table(cols, tab, up_rows, low_rows, axis)
        scores = dot(buf[parts[c], :], tall[...])
        for i, g in enumerate(range(bounds[c], bounds[c + 1])):
            t0[g] = scores[i * rows : (i + 1) * rows]
        if c > 0:
            finish(c - 1)
    finish(chunks - 1)
    load_a.wait()
    pack(tab, SHIFTS[0], aff, t0, hl, send_b, lists + NAMED)


def add_products(sums, pairs, fields):
    count, rows, _ = fields[0].shape
    group = 32

    def body(i, sums):
        sums = list(sums)
        g = i // (rows // group)
        start = (i % (rows // group)) * group
        for part in range(group // 8):
            at = pl.ds(pl.multiple_of(start + 8 * part, 8), 8)
            v = [f[g, at, :] for f in fields]
            for n, (a, b) in enumerate(pairs):
                sums[n] = sums[n] + v[a] * v[b]
        return tuple(sums)

    return list(lax.fori_loop(0, count * rows // group, body, tuple(sums)))


def halo_products(tab, aff, hl, sums, factor):
    _, _, cross, _ = offsets(aff.shape[0])
    sums[...] = jnp.zeros(sums.shape, F32)
    for e in range(ENTRIES):
        g, slot, h = (tab[cross + 3 * e + i] for i in range(3))
        both = folded(dot_t(aff[g, slot], hl[g]))
        sums[h] += both if factor == 1.0 else factor * both


def rest_kernel(tab, aff, t, hl, part, hl_next, halo_part, send_a, sums, *, step):
    count = t.shape[0]
    _, lists, _, _ = offsets(count)
    pack(tab, SHIFTS[step], aff, t, hl, send_a, lists)
    hl_next[count + 2 * NAMED] = jnp.zeros(hl_next.shape[1:], BF)
    for g in range(count):
        value = shifted(row_product(aff, tab, 0, g, hl), SHIFTS[step], t[g])
        part[g] = value
        put_rounded(hl_next, g, value)
    halo_products(tab, aff, hl, sums, 1.0)
    for h in range(2 * NAMED):
        halo_part[h] = sums[h]


def early_kernel(t0, t1, t2, out):
    sums = [jnp.zeros((8, t0.shape[2]), F32) for _ in EARLY]
    for n, total in enumerate(add_products(sums, EARLY, (t0, t1, t2))):
        out[pl.ds(n, 1), :] = jnp.sum(total, axis=0, keepdims=True)


def two_steps(tab, aff, hl1, t1, halo_part, recv_a, recv_b, t2, hl2, halo, step):
    count, _, _ = t2.shape
    full, lists, cross, _ = offsets(count)
    hl1[count + 2 * NAMED] = jnp.zeros(hl1.shape[1:], BF)
    hl2[count + 2 * NAMED] = jnp.zeros(hl2.shape[1:], BF)
    halo[2 * NAMED] = jnp.zeros(halo.shape[1:], BF)
    for h in range(NAMED):
        halo[h] = recv_a[h]
        halo[NAMED + h] = recv_b[h]
        low, high = h, NAMED + h
        put_rounded(hl1, count + low, recv_a[NAMED + h].astype(F32) + halo_part[low])
        put_rounded(hl1, count + high, recv_b[NAMED + h].astype(F32) + halo_part[high])
    for e in range(ENTRIES):
        g, slot, h = (tab[cross + 3 * e + i] for i in range(3))
        t1[g] += dot(aff[g, slot], halo[h])
    for j in range(2 * NAMED):
        g = tab[lists + j]
        put_rounded(hl1, g, t1[g])
    for g in range(count):
        value = shifted(row_product(aff, tab, full, g, hl1), SHIFTS[step + 1], t1[g])
        t2[g] = value
        put_rounded(hl2, g, value)


def middle_kernel(tab, aff, *refs, parity, axis):
    halo_part, recv_a, recv_b = refs[-9:-6]
    hl1, t1, t2, hl2, send_b, halo = refs[-6:]
    _, lists, _, _ = offsets(t1.shape[0])
    active = lax.rem(lax.axis_index(axis), 2) == parity

    @pl.when(active)
    def _():
        two_steps(tab, aff, hl1, t1, halo_part, recv_a, recv_b, t2, hl2, halo, 0)
        pack(tab, SHIFTS[2], aff, t2, hl2, send_b, lists + NAMED)

    @pl.when(jnp.logical_not(active))
    def _():
        send_b[...] = jnp.zeros(send_b.shape, BF)


def last_kernel(tab, aff, *refs, parity, axis):
    outs = 5 if parity == 0 else 6
    halo_part, recv_a, recv_b = refs[-outs - 4 : -outs - 1]
    hl3, t3, t4, hl4, send_a, *send_b, halo = refs[-outs - 1 :]
    width = t3.shape[2]
    _, lists, _, _ = offsets(t3.shape[0])
    active = lax.rem(lax.axis_index(axis), 2) == parity

    @pl.when(active)
    def _():
        two_steps(tab, aff, hl3, t3, halo_part, recv_a, recv_b, t4, hl4, halo, 2)
        for j in range(NAMED):
            send_a[j] = hl4[tab[lists + j], :, :width]
            for ref in send_b:
                ref[j] = hl4[tab[lists + NAMED + j], :, :width]

    if send_b:

        @pl.when(jnp.logical_not(active))
        def _():
            send_b[0][...] = jnp.zeros(send_b[0].shape, BF)


def gram_kernel(tab, aff, t2, t3, t4, hl, early, out):
    count, rows, width = t2.shape
    sums = [jnp.zeros((8, width), F32) for _ in range(len(LATE) + 1)]
    fields = (None, None, t2, t3, t4)
    for g in range(count):
        local = row_product(aff, tab, 0, g, hl)
        v = [None if f is None else f[g] for f in fields]
        terms = [v[i] * v[j] for i, j in LATE] + [v[-1] * local]
        for n, term in enumerate(terms):
            sums[n] = sums[n] + term.reshape(rows // 8, 8, width).sum(0)
    out[pl.ds(0, len(EARLY)), :] = early[...]
    for n, total in enumerate(sums):
        out[pl.ds(len(EARLY) + n, 1), :] = jnp.sum(total, axis=0, keepdims=True)


def weight_kernel(tab, aff, hl, weight, sums):
    halo_products(tab, aff, hl, sums, 2.0)
    for h in range(2 * NAMED):
        weight[h] = sums[h]


def cross_kernel(weight, recv_a, recv_b, gram, out, *, axis):
    _, rows, width = weight.shape
    even = lax.rem(lax.axis_index(axis), 2) == 0
    out[...] = gram[...]

    @pl.when(even)
    def _():
        total = jnp.zeros((8, width), F32)
        for h in range(NAMED):
            part = weight[h] * recv_a[h].astype(F32) + weight[NAMED + h] * recv_b[h].astype(F32)
            total = total + part.reshape(rows // 8, 8, width).sum(0)
        last = pl.ds(ROWS - 1, 1)
        out[last, :] = out[last, :] + jnp.sum(total, axis=0, keepdims=True)


def spread_kernel(own, other, out):
    value = own[...] + other[...]
    for d in range(out.shape[0]):
        out[d] = value


def final_kernel(parts, t0, t1, t2, t3, t4, out, buf, sems):
    n = ITERATIONS
    value = parts[0]
    for d in range(1, parts.shape[0]):
        value = value + parts[d]
    gram = {}
    for k, (i, j) in enumerate(PAIRS):
        gram[i, j] = gram[j, i] = value[k : k + 1]
    for j in range(2, n - 1):
        for i in range(n - 2):
            if (i, j + 1) not in gram:
                entry = gram[i + 1, j] + (SHIFTS[i] - SHIFTS[j]) * gram[i, j]
                gram[i, j + 1] = gram[j + 1, i] = entry
    matrix = {}
    for i in range(n):
        for j in range(i, n):
            if i + 1 < n and j + 1 == n:
                product = gram[i + 1, j] + SHIFTS[i] * gram[i, j]
            elif j + 1 < n:
                product = gram[i, j + 1] + SHIFTS[j] * gram[i, j]
            else:
                product = value[ROWS - 1 : ROWS]
            matrix[i, j] = gram[i, j] - DAMP * product
    scale = [
        jnp.where(matrix[i, i] > 0.0, lax.rsqrt(jnp.maximum(matrix[i, i], 1e-37)), 0.0)
        for i in range(n)
    ]
    for i in range(n):
        for j in range(i, n):
            matrix[i, j] = matrix[i, j] * (scale[i] * scale[j])
    right = [gram[i, 0] * scale[i] for i in range(n)]
    inverse = []
    for k in range(n):
        pivot = matrix[k, k]
        inverse.append(jnp.where(pivot > PIVOT_MIN, 1.0 / jnp.maximum(pivot, PIVOT_MIN), 0.0))
        for i in range(k + 1, n):
            factor = matrix[k, i] * inverse[k]
            for j in range(i, n):
                matrix[i, j] = matrix[i, j] - factor * matrix[k, j]
            right[i] = right[i] - factor * right[k]
    coef = [None] * n
    for k in range(n - 1, -1, -1):
        rest = right[k]
        for j in range(k + 1, n):
            rest = rest - matrix[k, j] * coef[j]
        coef[k] = rest * inverse[k]
    coef = [coef[k] * scale[k] for k in range(n)]
    fields = (t0, t1, t2, t3, t4)
    count, rows, _ = t0.shape
    chunks = sems.shape[0]
    per = count // chunks
    copies = []
    for c in range(chunks):
        for g in range(c * per, (c + 1) * per):
            total = None
            for f, k in zip(fields, coef):
                term = f[g] * k
                total = term if total is None else total + term
            buf[pl.ds(g * rows, rows), :] = total
        part = pl.ds(c * per * rows, per * rows)
        copy = pltpu.make_async_copy(buf.at[part], out.at[part], sems.at[c])
        copy.start()
        copies.append(copy)
    for copy in copies:
        copy.wait()


def to_chip_partner(block, axis):
    return lax.ppermute(block, axis, [(i, i ^ 1) for i in range(lax.axis_size(axis))])


def shift(block, by, axis):
    n = lax.axis_size(axis)
    return lax.ppermute(block, axis, [(i, (i + by) % n) for i in range(n)])


def shards(descriptors, queries, affinity, tile_col):
    count, _, rows, _ = affinity.shape
    width = queries.shape[0]
    depth = descriptors.shape[1]
    axis = "dom"
    devices = lax.axis_size(axis)
    size = 128 * pl.cdiv(offsets(count)[-1], 128)
    blocks = count + 2 * NAMED + 1
    field = jax.ShapeDtypeStruct((count, rows, width), F32)
    rounded = jax.ShapeDtypeStruct((blocks, rows, width), BF)
    split = jax.ShapeDtypeStruct((blocks, rows, 2 * width), BF)
    edge = jax.ShapeDtypeStruct((2 * NAMED, rows, width), BF)
    half = jax.ShapeDtypeStruct((NAMED, rows, width), BF)
    early = jax.ShapeDtypeStruct((len(EARLY), width), F32)
    edge_sum = jax.ShapeDtypeStruct((2 * NAMED, rows, width), F32)
    sums_h = pltpu.VMEM((2 * NAMED + 1, rows, width), F32)
    work = [pltpu.VMEM((2 * NAMED + 1, rows, width), BF)]
    bounds = (0, count)
    flops = 2 * count * rows * 4 * rows * 2 * width

    def call(kernel, out_shape, products, scratch=(), aliases=None, limit=24):
        outs = out_shape if isinstance(out_shape, tuple) else (out_shape,)

        def run(*args):
            specs = [SMEM if x.dtype == jnp.int32 else VMEM for x in args]
            args = [
                pltpu.with_memory_space_constraint(x, pltpu.SMEM) if x.dtype == jnp.int32 else x
                for x in args
            ]
            return pl.pallas_call(
                kernel,
                out_shape=out_shape,
                in_specs=specs,
                out_specs=(VMEM,) * len(outs) if isinstance(out_shape, tuple) else VMEM,
                scratch_shapes=list(scratch),
                input_output_aliases=aliases or {},
                compiler_params=params(limit),
                cost_estimate=pl.CostEstimate(
                    flops=int(products * flops), bytes_accessed=4 << 20, transcendentals=0
                ),
            )(*args)

        return run

    operands = (descriptors, queries, affinity, tile_col.T)
    t0, hl0, send_b, aff, tab = pl.pallas_call(
        functools.partial(first_kernel, bounds=bounds, axis=axis),
        out_shape=(
            field,
            rounded,
            edge,
            jax.ShapeDtypeStruct(affinity.shape, BF),
            pltpu.SMEM((size,), jnp.int32),
        ),
        in_specs=[HBM] * 4,
        out_specs=(VMEM,) * 4 + (SMEM,),
        scratch_shapes=[
            pltpu.VMEM((count * rows, depth), BF),
            pltpu.VMEM((width, depth), BF),
            pltpu.VMEM((depth, width), BF),
            pltpu.SMEM((4, count), jnp.int32),
            pltpu.SMEM((3, count + 1), jnp.int32),
            pltpu.SMEM((3, count + 1), jnp.int32),
            pltpu.SemaphoreType.DMA((len(bounds) + 2,)),
        ],
        compiler_params=params(24),
        cost_estimate=pl.CostEstimate(flops=flops, bytes_accessed=4 << 20, transcendentals=0),
        name="first",
    )(*(pltpu.with_memory_space_constraint(x, pltpu.HBM) for x in operands))
    recv_even = shift(send_b, 1, axis)
    recv_odd = shift(send_b, -1, axis)
    part, hl1, halo_part, send_a = call(
        functools.partial(rest_kernel, step=0), (field, split, edge_sum, edge), 1, [sums_h]
    )(tab, aff, t0, hl0)
    recv_a = to_chip_partner(send_a, axis)

    def by_parity(kernel, parity, before, edges, aliases):
        return call(
            functools.partial(kernel, parity=parity, axis=axis),
            (before, field, field, rounded, *edges),
            2,
            work,
            dict(aliases),
        )

    first_half = {2: 0, 3: 1}
    second_half = {2: 0, 3: 1, 4: 2, 5: 3}
    hl1, t1, t2, hl2, send = by_parity(middle_kernel, 0, split, (edge,), first_half)(
        tab, aff, hl1, part, halo_part, recv_a, recv_even
    )
    got_odd = shift(send, -1, axis)
    hl1, t1, t2, hl2, send = by_parity(middle_kernel, 1, split, (edge,), second_half)(
        tab, aff, hl1, t1, t2, hl2, halo_part, recv_a, recv_odd
    )
    got_even = shift(send, 1, axis)
    part, hl3, halo_part, send_a = call(
        functools.partial(rest_kernel, step=2), (field, rounded, edge_sum, edge), 1, [sums_h]
    )(tab, aff, t2, hl2)
    recv_a = to_chip_partner(send_a, axis)
    gram = call(early_kernel, early, 0.1)(t0, t1, t2)
    last1 = by_parity(last_kernel, 1, rounded, (half, half), first_half)
    hl3, t3, t4, hl4, send_a, send = last1(
        tab, aff, hl3, part, halo_part, recv_a, got_odd
    )
    recv_b = shift(send, 1, axis)
    last0 = by_parity(last_kernel, 0, rounded, (half,), {**second_half, 6: 4})
    _, t3, t4, hl4, send_a = last0(
        tab, aff, hl3, t3, t4, hl4, send_a, halo_part, recv_a, got_even
    )
    recv_a = to_chip_partner(send_a, axis)
    gram = call(
        gram_kernel, jax.ShapeDtypeStruct((ROWS, width), F32), 1
    )(tab, aff, t2, t3, t4, hl4, gram)
    weight = call(weight_kernel, edge_sum, 0.2, [sums_h])(tab, aff, hl4)
    entries = jax.ShapeDtypeStruct((ROWS, width), F32)
    gram = call(functools.partial(cross_kernel, axis=axis), entries, 0.1, limit=8)(
        weight, recv_a, recv_b, gram
    )
    other = to_chip_partner(gram, axis)
    copies = jax.ShapeDtypeStruct((devices // 2, ROWS, width), F32)
    parts = call(spread_kernel, copies, 0.1, limit=8)(gram, other)
    groups = [[2 * k + (k + core) % 2 for k in range(devices // 2)] for core in range(2)]
    parts = lax.all_to_all(parts, axis, 0, 0, axis_index_groups=groups)
    return pl.pallas_call(
        final_kernel,
        out_shape=jax.ShapeDtypeStruct((count * rows, width), F32),
        in_specs=[VMEM] * 6,
        out_specs=HBM,
        scratch_shapes=[
            pltpu.VMEM((count * rows, width), F32),
            pltpu.SemaphoreType.DMA((count // 3,)),
        ],
        compiler_params=params(24),
        name="final",
    )(parts, t0, t1, t2, t3, t4)


def solution(mesh):
    return jax.shard_map(
        shards,
        mesh=mesh,
        in_specs=(
            P(("region", "dom"), None),
            P("region", None),
            P(("region", "dom"), None, None, None),
            P(("region", "dom"), None),
        ),
        out_specs=P(("region", "dom"), None),
        check_vma=False,
    )
```

```python
import functools

import jax
import jax.numpy as jnp
from jax import lax
from jax.experimental import pallas as pl
from jax.experimental.pallas import tpu as pltpu
from jax.sharding import PartitionSpec as P

HALO_W = 6
NAMED = 3
ITERATIONS = 5
DAMP = 0.99
SHIFTS = (0.0, 1.0, -0.25, 0.5)
PIVOT_MIN = 1e-6
BF = jnp.bfloat16
F32 = jnp.float32
EARLY = [(i, j) for i in range(3) for j in range(i, 3)]
LATE = [(2, 3), (3, 3), (3, 4), (4, 4)]
PAIRS = EARLY + LATE
ROWS = len(PAIRS) + 1
ENTRIES = 2 + 2 * NAMED

VMEM = pl.BlockSpec(memory_space=pltpu.VMEM)
SMEM = pl.BlockSpec(memory_space=pltpu.SMEM)
HBM = pl.BlockSpec(memory_space=pltpu.HBM)


def params(mib):
    return pltpu.CompilerParams(vmem_limit_bytes=mib << 20)


def dot(a, b):
    return jnp.dot(a, b, preferred_element_type=F32)


def dot_t(a, b):
    return lax.dot_general(a, b, (((0,), (0,)), ((), ())), preferred_element_type=F32)


def put_rounded(ref, index, value):
    high = value.astype(BF)
    width = value.shape[-1]
    ref[index, :, :width] = high
    if ref.shape[2] > width:
        ref[index, :, width:] = (value - high.astype(F32)).astype(BF)


def folded(out):
    width = out.shape[0]
    return out if out.shape[1] == width else out[:, :width] + out[:, width:]


def row_product(aff, tab, base, g, hl):
    count = aff.shape[0]
    if isinstance(g, int):
        low = g - 1 if g > 0 else tab[base + count]
        high = g + 1 if g + 1 < count else tab[base + count + 1]
    else:
        low = jnp.where(g > 0, g - 1, tab[base + count])
        high = jnp.where(g + 1 < count, g + 1, tab[base + count + 1])
    left = jnp.concatenate([aff[g, 0], aff[g, 1]], axis=1)
    right = jnp.concatenate([hl[g], hl[low]], axis=0)
    out = dot(left, right)
    left = jnp.concatenate([aff[g, 2], aff[g, 3]], axis=1)
    right = jnp.concatenate([hl[high], hl[tab[base + g]]], axis=0)
    return folded(out + dot(left, right))


def shifted(value, shift, t):
    return value if shift == 0.0 else value - shift * t


def offsets(count):
    full = count + 2
    lists = 2 * full
    cross = lists + 2 * NAMED
    return full, lists, cross, cross + 3 * ENTRIES


def fill_table(tile_col, tab, up_rows, low_rows, axis):
    count = tile_col.shape[1]
    total = count * lax.axis_size(axis)
    me = lax.axis_index(axis)
    even = lax.rem(me, 2) == 0
    full, lists, cross, _ = offsets(count)
    zero = count + 2 * NAMED
    up_base = jnp.where(even, 0, NAMED)
    low_base = NAMED - up_base
    relative, ups, lows = [], [], []
    up_mask = jnp.int32(1)
    low_mask = jnp.int32(1 << (HALO_W - 1))
    for g in range(count):
        rel = tile_col[3, g] - me * count
        rel = jnp.where(rel < 0, rel + total, rel)
        up = (rel >= count) & (rel < count + HALO_W)
        low = rel >= total - HALO_W
        place = jnp.where(up, rel - count, rel - (total - HALO_W))
        place = jnp.clip(place, 0, HALO_W - 1)
        bit = lax.shift_left(jnp.int32(1), place)
        up_mask = up_mask | jnp.where(up, bit, 0)
        low_mask = low_mask | jnp.where(low, bit, 0)
        relative.append((rel, place, bit))
        ups.append(up)
        lows.append(low)
    up_count = low_count = up_cross = low_cross = jnp.int32(0)
    for g in range(count):
        rel, place, bit = relative[g]
        below = jnp.where(ups[g], up_mask, low_mask) & (bit - 1)
        rank = below & 1
        for p in range(1, HALO_W - 1):
            rank = rank + (lax.shift_right_logical(below, jnp.int32(p)) & 1)
        halo = jnp.where(ups[g], up_base, low_base) + jnp.minimum(rank, NAMED - 1)
        local = rel < count
        tab[g] = jnp.where(local, rel, zero)
        tab[full + g] = jnp.where(local, rel, count + halo)
        up_rows[0, up_count] = g
        low_rows[0, low_count] = g
        up_rows[1, up_cross] = g
        low_rows[1, low_cross] = g
        up_rows[2, up_cross] = halo
        low_rows[2, low_cross] = halo
        up_cross = up_cross + jnp.where(ups[g], 1, 0)
        low_cross = low_cross + jnp.where(lows[g], 1, 0)
        up_count = up_count + (1 if g == count - 1 else jnp.where(ups[g], 1, 0))
        low_count = low_count + (1 if g == 0 else jnp.where(lows[g], 1, 0))
    tab[count] = zero
    tab[count + 1] = zero
    tab[full + count] = count + low_base + NAMED - 1
    tab[full + count + 1] = count + up_base
    for j in range(NAMED):
        up, low = up_rows[0, j], low_rows[0, j]
        tab[lists + j] = jnp.where(even, up, low)
        tab[lists + NAMED + j] = jnp.where(even, low, up)
    chains = ((0, 1, low_base + NAMED - 1), (count - 1, 2, up_base))
    for side, (rows, used) in enumerate(((low_rows, low_cross), (up_rows, up_cross))):
        for i in range(3):
            tab[cross + 3 * side * (1 + NAMED) + i] = jnp.int32(chains[side][i])
        for j in range(NAMED):
            at = cross + 3 * (side * (1 + NAMED) + 1 + j)
            tab[at] = jnp.where(j < used, rows[1, j], 0)
            tab[at + 1] = jnp.int32(3)
            tab[at + 2] = jnp.where(j < used, rows[2, j], 2 * NAMED)


def pack(tab, shift, aff, t, hl, send, base):
    width = t.shape[2]
    for j in range(NAMED):
        g = tab[base + j]
        send[j] = hl[g, :, :width]
        send[NAMED + j] = shifted(row_product(aff, tab, 0, g, hl), shift, t[g]).astype(BF)


def first_kernel(
    desc, queries, affinity, tile_col, t0, hl, send_b, aff, tab,
    buf, wide, tall, cols, up_rows, low_rows, sems, *, bounds, axis,
):
    count, rows = t0.shape[0], t0.shape[1]
    chunks = len(bounds) - 1
    parts = [pl.ds(a * rows, (b - a) * rows) for a, b in zip(bounds, bounds[1:])]
    _, lists, _, _ = offsets(count)
    load_q = pltpu.make_async_copy(queries, wide, sems.at[chunks])
    load_c = pltpu.make_async_copy(tile_col, cols, sems.at[chunks + 1])
    load_q.start()
    load_c.start()
    copies = []
    for c in range(chunks):
        copy = pltpu.make_async_copy(desc.at[parts[c]], buf.at[parts[c]], sems.at[c])
        copy.start()
        copies.append(copy)
    load_a = pltpu.make_async_copy(affinity, aff, sems.at[chunks + 2])
    load_a.start()
    hl[count + 2 * NAMED] = jnp.zeros(hl.shape[1:], BF)
    load_q.wait()
    tall[...] = wide[...].T
    load_c.wait()

    def finish(c):
        for g in range(bounds[c], bounds[c + 1]):
            value = jnp.maximum(t0[g], 0.0)
            value = value * value * value
            t0[g] = value
            put_rounded(hl, g, value)

    for c in range(chunks):
        copies[c].wait()
        if c == 0:
            fill_table(cols, tab, up_rows, low_rows, axis)
        scores = dot(buf[parts[c], :], tall[...])
        for i, g in enumerate(range(bounds[c], bounds[c + 1])):
            t0[g] = scores[i * rows : (i + 1) * rows]
        if c > 0:
            finish(c - 1)
    finish(chunks - 1)
    load_a.wait()
    pack(tab, SHIFTS[0], aff, t0, hl, send_b, lists + NAMED)


def add_products(sums, pairs, fields):
    count, rows, _ = fields[0].shape
    group = 32

    def body(i, sums):
        sums = list(sums)
        g = i // (rows // group)
        start = (i % (rows // group)) * group
        for part in range(group // 8):
            at = pl.ds(pl.multiple_of(start + 8 * part, 8), 8)
            v = [f[g, at, :] for f in fields]
            for n, (a, b) in enumerate(pairs):
                sums[n] = sums[n] + v[a] * v[b]
        return tuple(sums)

    return list(lax.fori_loop(0, count * rows // group, body, tuple(sums)))


def halo_products(tab, aff, hl, sums, factor):
    _, _, cross, _ = offsets(aff.shape[0])
    sums[...] = jnp.zeros(sums.shape, F32)
    for e in range(ENTRIES):
        g, slot, h = (tab[cross + 3 * e + i] for i in range(3))
        both = folded(dot_t(aff[g, slot], hl[g]))
        sums[h] += both if factor == 1.0 else factor * both


def rest_kernel(tab, aff, t, hl, part, hl_next, halo_part, send_a, sums, *, step):
    count = t.shape[0]
    _, lists, _, _ = offsets(count)
    pack(tab, SHIFTS[step], aff, t, hl, send_a, lists)
    hl_next[count + 2 * NAMED] = jnp.zeros(hl_next.shape[1:], BF)
    for g in range(count):
        value = shifted(row_product(aff, tab, 0, g, hl), SHIFTS[step], t[g])
        part[g] = value
        put_rounded(hl_next, g, value)
    halo_products(tab, aff, hl, sums, 1.0)
    for h in range(2 * NAMED):
        halo_part[h] = sums[h]


def early_kernel(t0, t1, t2, out):
    sums = [jnp.zeros((8, t0.shape[2]), F32) for _ in EARLY]
    for n, total in enumerate(add_products(sums, EARLY, (t0, t1, t2))):
        out[pl.ds(n, 1), :] = jnp.sum(total, axis=0, keepdims=True)


def complete(tab, aff, hl1, t1, halo_part, recv_a, recv_b, halo):
    count = t1.shape[0]
    _, lists, cross, _ = offsets(count)
    hl1[count + 2 * NAMED] = jnp.zeros(hl1.shape[1:], BF)
    halo[2 * NAMED] = jnp.zeros(halo.shape[1:], BF)
    for h in range(NAMED):
        halo[h] = recv_a[h]
        halo[NAMED + h] = recv_b[h]
        low, high = h, NAMED + h
        put_rounded(hl1, count + low, recv_a[NAMED + h].astype(F32) + halo_part[low])
        put_rounded(hl1, count + high, recv_b[NAMED + h].astype(F32) + halo_part[high])
    for e in range(ENTRIES):
        g, slot, h = (tab[cross + 3 * e + i] for i in range(3))
        t1[g] += dot(aff[g, slot], halo[h])
    for j in range(2 * NAMED):
        g = tab[lists + j]
        put_rounded(hl1, g, t1[g])


def advance(tab, aff, hl1, t1, t2, hl2, step):
    count = t1.shape[0]
    full = offsets(count)[0]
    hl2[count + 2 * NAMED] = jnp.zeros(hl2.shape[1:], BF)
    for g in range(count):
        value = shifted(row_product(aff, tab, full, g, hl1), SHIFTS[step], t1[g])
        t2[g] = value
        put_rounded(hl2, g, value)


def middle_kernel(tab, aff, *refs, parity, axis):
    halo_part, recv_a, recv_b = refs[-9:-6]
    hl1, t1, t2, hl2, send_b, halo = refs[-6:]
    _, lists, _, _ = offsets(t1.shape[0])
    active = lax.rem(lax.axis_index(axis), 2) == parity

    @pl.when(active)
    def _():
        complete(tab, aff, hl1, t1, halo_part, recv_a, recv_b, halo)
        advance(tab, aff, hl1, t1, t2, hl2, 1)
        pack(tab, SHIFTS[2], aff, t2, hl2, send_b, lists + NAMED)

    @pl.when(jnp.logical_not(active))
    def _():
        send_b[...] = jnp.zeros(send_b.shape, BF)


def edge_kernel(tab, aff, _, __, halo_part, recv_a, recv_b, hl3, t3, send_b, halo, *, axis):
    full, lists, _, _ = offsets(t3.shape[0])
    odd = lax.rem(lax.axis_index(axis), 2) == 1

    @pl.when(odd)
    def _():
        complete(tab, aff, hl3, t3, halo_part, recv_a, recv_b, halo)
        for j in range(NAMED):
            g = tab[lists + NAMED + j]
            product = row_product(aff, tab, full, g, hl3)
            send_b[j] = shifted(product, SHIFTS[3], t3[g]).astype(BF)

    @pl.when(jnp.logical_not(odd))
    def _():
        send_b[...] = jnp.zeros(send_b.shape, BF)


def last_kernel(
    tab, aff, _, __, halo_part, recv_a, recv_b, hl3, t3, t4, hl4, send_a, halo, *, axis
):
    count, _, width = t3.shape
    _, lists, _, _ = offsets(count)

    @pl.when(lax.rem(lax.axis_index(axis), 2) == 0)
    def _():
        complete(tab, aff, hl3, t3, halo_part, recv_a, recv_b, halo)

    advance(tab, aff, hl3, t3, t4, hl4, 3)
    for j in range(NAMED):
        send_a[j] = hl4[tab[lists + j], :, :width]


def gram_kernel(tab, aff, t2, t3, t4, hl, early, out):
    count, rows, width = t2.shape
    sums = [jnp.zeros((8, width), F32) for _ in range(len(LATE) + 1)]
    fields = (None, None, t2, t3, t4)
    for g in range(count):
        local = row_product(aff, tab, 0, g, hl)
        v = [None if f is None else f[g] for f in fields]
        terms = [v[i] * v[j] for i, j in LATE] + [v[-1] * local]
        for n, term in enumerate(terms):
            sums[n] = sums[n] + term.reshape(rows // 8, 8, width).sum(0)
    out[pl.ds(0, len(EARLY)), :] = early[...]
    for n, total in enumerate(sums):
        out[pl.ds(len(EARLY) + n, 1), :] = jnp.sum(total, axis=0, keepdims=True)


def weight_kernel(tab, aff, hl, weight, sums):
    halo_products(tab, aff, hl, sums, 2.0)
    for h in range(2 * NAMED):
        weight[h] = sums[h]


def cross_kernel(weight, recv_a, recv_b, gram, out, *, axis):
    _, rows, width = weight.shape
    even = lax.rem(lax.axis_index(axis), 2) == 0
    out[...] = gram[...]

    @pl.when(even)
    def _():
        total = jnp.zeros((8, width), F32)
        for h in range(NAMED):
            part = weight[h] * recv_a[h].astype(F32) + weight[NAMED + h] * recv_b[h].astype(F32)
            total = total + part.reshape(rows // 8, 8, width).sum(0)
        last = pl.ds(ROWS - 1, 1)
        out[last, :] = out[last, :] + jnp.sum(total, axis=0, keepdims=True)


def spread_kernel(own, other, out):
    value = own[...] + other[...]
    for d in range(out.shape[0]):
        out[d] = value


def final_kernel(parts, t0, t1, t2, t3, t4, out, buf, sems):
    n = ITERATIONS
    value = parts[0]
    for d in range(1, parts.shape[0]):
        value = value + parts[d]
    gram = {}
    for k, (i, j) in enumerate(PAIRS):
        gram[i, j] = gram[j, i] = value[k : k + 1]
    for j in range(2, n - 1):
        for i in range(n - 2):
            if (i, j + 1) not in gram:
                entry = gram[i + 1, j] + (SHIFTS[i] - SHIFTS[j]) * gram[i, j]
                gram[i, j + 1] = gram[j + 1, i] = entry
    matrix = {}
    for i in range(n):
        for j in range(i, n):
            if i + 1 < n and j + 1 == n:
                product = gram[i + 1, j] + SHIFTS[i] * gram[i, j]
            elif j + 1 < n:
                product = gram[i, j + 1] + SHIFTS[j] * gram[i, j]
            else:
                product = value[ROWS - 1 : ROWS]
            matrix[i, j] = gram[i, j] - DAMP * product
    scale = [
        jnp.where(matrix[i, i] > 0.0, lax.rsqrt(jnp.maximum(matrix[i, i], 1e-37)), 0.0)
        for i in range(n)
    ]
    for i in range(n):
        for j in range(i, n):
            matrix[i, j] = matrix[i, j] * (scale[i] * scale[j])
    right = [gram[i, 0] * scale[i] for i in range(n)]
    inverse = []
    for k in range(n):
        pivot = matrix[k, k]
        inverse.append(jnp.where(pivot > PIVOT_MIN, 1.0 / jnp.maximum(pivot, PIVOT_MIN), 0.0))
        for i in range(k + 1, n):
            factor = matrix[k, i] * inverse[k]
            for j in range(i, n):
                matrix[i, j] = matrix[i, j] - factor * matrix[k, j]
            right[i] = right[i] - factor * right[k]
    coef = [None] * n
    for k in range(n - 1, -1, -1):
        rest = right[k]
        for j in range(k + 1, n):
            rest = rest - matrix[k, j] * coef[j]
        coef[k] = rest * inverse[k]
    coef = [coef[k] * scale[k] for k in range(n)]
    fields = (t0, t1, t2, t3, t4)
    count, rows, _ = t0.shape
    chunks = sems.shape[0]
    per = count // chunks
    copies = []
    for c in range(chunks):
        for g in range(c * per, (c + 1) * per):
            total = None
            for f, k in zip(fields, coef):
                term = f[g] * k
                total = term if total is None else total + term
            buf[pl.ds(g * rows, rows), :] = total
        part = pl.ds(c * per * rows, per * rows)
        copy = pltpu.make_async_copy(buf.at[part], out.at[part], sems.at[c])
        copy.start()
        copies.append(copy)
    for copy in copies:
        copy.wait()


def to_chip_partner(block, axis):
    return lax.ppermute(block, axis, [(i, i ^ 1) for i in range(lax.axis_size(axis))])


def shift(block, by, axis):
    n = lax.axis_size(axis)
    return lax.ppermute(block, axis, [(i, (i + by) % n) for i in range(n)])


def shards(descriptors, queries, affinity, tile_col):
    count, _, rows, _ = affinity.shape
    width = queries.shape[0]
    depth = descriptors.shape[1]
    axis = "dom"
    devices = lax.axis_size(axis)
    size = 128 * pl.cdiv(offsets(count)[-1], 128)
    blocks = count + 2 * NAMED + 1
    field = jax.ShapeDtypeStruct((count, rows, width), F32)
    rounded = jax.ShapeDtypeStruct((blocks, rows, width), BF)
    split = jax.ShapeDtypeStruct((blocks, rows, 2 * width), BF)
    edge = jax.ShapeDtypeStruct((2 * NAMED, rows, width), BF)
    half = jax.ShapeDtypeStruct((NAMED, rows, width), BF)
    early = jax.ShapeDtypeStruct((len(EARLY), width), F32)
    edge_sum = jax.ShapeDtypeStruct((2 * NAMED, rows, width), F32)
    sums_h = pltpu.VMEM((2 * NAMED + 1, rows, width), F32)
    work = [pltpu.VMEM((2 * NAMED + 1, rows, width), BF)]
    bounds = (0, count)
    flops = 2 * count * rows * 4 * rows * 2 * width

    def call(kernel, out_shape, products, scratch=(), aliases=None, limit=24):
        outs = out_shape if isinstance(out_shape, tuple) else (out_shape,)

        def run(*args):
            specs = [SMEM if x.dtype == jnp.int32 else VMEM for x in args]
            args = [
                pltpu.with_memory_space_constraint(x, pltpu.SMEM) if x.dtype == jnp.int32 else x
                for x in args
            ]
            return pl.pallas_call(
                kernel,
                out_shape=out_shape,
                in_specs=specs,
                out_specs=(VMEM,) * len(outs) if isinstance(out_shape, tuple) else VMEM,
                scratch_shapes=list(scratch),
                input_output_aliases=aliases or {},
                compiler_params=params(limit),
                cost_estimate=pl.CostEstimate(
                    flops=int(products * flops), bytes_accessed=4 << 20, transcendentals=0
                ),
            )(*args)

        return run

    operands = (descriptors, queries, affinity, tile_col.T)
    t0, hl0, send_b, aff, tab = pl.pallas_call(
        functools.partial(first_kernel, bounds=bounds, axis=axis),
        out_shape=(
            field,
            rounded,
            edge,
            jax.ShapeDtypeStruct(affinity.shape, BF),
            pltpu.SMEM((size,), jnp.int32),
        ),
        in_specs=[HBM] * 4,
        out_specs=(VMEM,) * 4 + (SMEM,),
        scratch_shapes=[
            pltpu.VMEM((count * rows, depth), BF),
            pltpu.VMEM((width, depth), BF),
            pltpu.VMEM((depth, width), BF),
            pltpu.SMEM((4, count), jnp.int32),
            pltpu.SMEM((3, count + 1), jnp.int32),
            pltpu.SMEM((3, count + 1), jnp.int32),
            pltpu.SemaphoreType.DMA((len(bounds) + 2,)),
        ],
        compiler_params=params(24),
        cost_estimate=pl.CostEstimate(flops=flops, bytes_accessed=4 << 20, transcendentals=0),
        name="first",
    )(*(pltpu.with_memory_space_constraint(x, pltpu.HBM) for x in operands))
    recv_even = shift(send_b, 1, axis)
    recv_odd = shift(send_b, -1, axis)
    part, hl1, halo_part, send_a = call(
        functools.partial(rest_kernel, step=0), (field, split, edge_sum, edge), 1, [sums_h]
    )(tab, aff, t0, hl0)
    recv_a = to_chip_partner(send_a, axis)

    def by_parity(kernel, parity, before, edges, aliases):
        return call(
            functools.partial(kernel, parity=parity, axis=axis),
            (before, field, field, rounded, *edges),
            2,
            work,
            dict(aliases),
        )

    first_half = {2: 0, 3: 1}
    second_half = {2: 0, 3: 1, 4: 2, 5: 3}
    hl1, t1, t2, hl2, send = by_parity(middle_kernel, 0, split, (edge,), first_half)(
        tab, aff, hl1, part, halo_part, recv_a, recv_even
    )
    got_odd = shift(send, -1, axis)
    hl1, t1, t2, hl2, send = by_parity(middle_kernel, 1, split, (edge,), second_half)(
        tab, aff, hl1, t1, t2, hl2, halo_part, recv_a, recv_odd
    )
    got_even = shift(send, 1, axis)
    part, hl3, halo_part, send_a = call(
        functools.partial(rest_kernel, step=2), (field, rounded, edge_sum, edge), 1, [sums_h]
    )(tab, aff, t2, hl2)
    recv_a = to_chip_partner(send_a, axis)
    gram = call(early_kernel, early, 0.1)(t0, t1, t2)
    hl3, t3, send = call(
        functools.partial(edge_kernel, axis=axis), (rounded, field, half), 0.5, work, first_half
    )(tab, aff, hl3, part, halo_part, recv_a, got_odd)
    recv_b = shift(send, 1, axis)
    _, t3, t4, hl4, send_a = call(
        functools.partial(last_kernel, axis=axis),
        (rounded, field, field, rounded, half),
        1,
        work,
        first_half,
    )(tab, aff, hl3, t3, halo_part, recv_a, got_even)
    recv_a = to_chip_partner(send_a, axis)
    gram = call(
        gram_kernel, jax.ShapeDtypeStruct((ROWS, width), F32), 1
    )(tab, aff, t2, t3, t4, hl4, gram)
    weight = call(weight_kernel, edge_sum, 0.2, [sums_h])(tab, aff, hl4)
    entries = jax.ShapeDtypeStruct((ROWS, width), F32)
    gram = call(functools.partial(cross_kernel, axis=axis), entries, 0.1, limit=8)(
        weight, recv_a, recv_b, gram
    )
    other = to_chip_partner(gram, axis)
    copies = jax.ShapeDtypeStruct((devices // 2, ROWS, width), F32)
    parts = call(spread_kernel, copies, 0.1, limit=8)(gram, other)
    groups = [[2 * k + (k + core) % 2 for k in range(devices // 2)] for core in range(2)]
    parts = lax.all_to_all(parts, axis, 0, 0, axis_index_groups=groups)
    return pl.pallas_call(
        final_kernel,
        out_shape=jax.ShapeDtypeStruct((count * rows, width), F32),
        in_specs=[VMEM] * 6,
        out_specs=HBM,
        scratch_shapes=[
            pltpu.VMEM((count * rows, width), F32),
            pltpu.SemaphoreType.DMA((count // 3,)),
        ],
        compiler_params=params(24),
        name="final",
    )(parts, t0, t1, t2, t3, t4)


def solution(mesh):
    return jax.shard_map(
        shards,
        mesh=mesh,
        in_specs=(
            P(("region", "dom"), None),
            P("region", None),
            P(("region", "dom"), None, None, None),
            P(("region", "dom"), None),
        ),
        out_specs=P(("region", "dom"), None),
        check_vma=False,
    )
```

```python
import functools

import jax
import jax.numpy as jnp
from jax import lax
from jax.experimental import pallas as pl
from jax.experimental.pallas import tpu as pltpu
from jax.sharding import PartitionSpec as P

HALO_W = 6
NAMED = 3
ITERATIONS = 5
DAMP = 0.99
SHIFTS = (0.0, 1.0, -0.25, 0.5)
PIVOT_MIN = 1e-6
BF = jnp.bfloat16
F32 = jnp.float32
EARLY = [(i, j) for i in range(3) for j in range(i, 3)]
LATE = [(2, 3), (3, 3), (3, 4), (4, 4)]
PAIRS = EARLY + LATE
ROWS = len(PAIRS) + 1
ENTRIES = 2 + 2 * NAMED

VMEM = pl.BlockSpec(memory_space=pltpu.VMEM)
SMEM = pl.BlockSpec(memory_space=pltpu.SMEM)
HBM = pl.BlockSpec(memory_space=pltpu.HBM)


def params(mib):
    return pltpu.CompilerParams(vmem_limit_bytes=mib << 20)


def dot(a, b):
    return jnp.dot(a, b, preferred_element_type=F32)


def dot_t(a, b):
    return lax.dot_general(a, b, (((0,), (0,)), ((), ())), preferred_element_type=F32)


def put_rounded(ref, index, value):
    high = value.astype(BF)
    width = value.shape[-1]
    ref[index, :, :width] = high
    if ref.shape[2] > width:
        ref[index, :, width:] = (value - high.astype(F32)).astype(BF)


def folded(out):
    width = out.shape[0]
    return out if out.shape[1] == width else out[:, :width] + out[:, width:]


def row_product(aff, tab, base, g, hl):
    count = aff.shape[0]
    if isinstance(g, int):
        low = g - 1 if g > 0 else tab[base + count]
        high = g + 1 if g + 1 < count else tab[base + count + 1]
    else:
        low = jnp.where(g > 0, g - 1, tab[base + count])
        high = jnp.where(g + 1 < count, g + 1, tab[base + count + 1])
    left = jnp.concatenate([aff[g, 0], aff[g, 1]], axis=1)
    right = jnp.concatenate([hl[g], hl[low]], axis=0)
    out = dot(left, right)
    left = jnp.concatenate([aff[g, 2], aff[g, 3]], axis=1)
    right = jnp.concatenate([hl[high], hl[tab[base + g]]], axis=0)
    return folded(out + dot(left, right))


def shifted(value, shift, t):
    return value if shift == 0.0 else value - shift * t


def offsets(count):
    full = count + 2
    lists = 2 * full
    cross = lists + 2 * NAMED
    return full, lists, cross, cross + 3 * ENTRIES


def fill_table(tile_col, tab, up_rows, low_rows, axis):
    count = tile_col.shape[1]
    total = count * lax.axis_size(axis)
    me = lax.axis_index(axis)
    even = lax.rem(me, 2) == 0
    full, lists, cross, _ = offsets(count)
    zero = count + 2 * NAMED
    up_base = jnp.where(even, 0, NAMED)
    low_base = NAMED - up_base
    relative, ups, lows = [], [], []
    up_mask = jnp.int32(1)
    low_mask = jnp.int32(1 << (HALO_W - 1))
    for g in range(count):
        rel = tile_col[3, g] - me * count
        rel = jnp.where(rel < 0, rel + total, rel)
        up = (rel >= count) & (rel < count + HALO_W)
        low = rel >= total - HALO_W
        place = jnp.where(up, rel - count, rel - (total - HALO_W))
        place = jnp.clip(place, 0, HALO_W - 1)
        bit = lax.shift_left(jnp.int32(1), place)
        up_mask = up_mask | jnp.where(up, bit, 0)
        low_mask = low_mask | jnp.where(low, bit, 0)
        relative.append((rel, place, bit))
        ups.append(up)
        lows.append(low)
    up_count = low_count = up_cross = low_cross = jnp.int32(0)
    for g in range(count):
        rel, place, bit = relative[g]
        below = jnp.where(ups[g], up_mask, low_mask) & (bit - 1)
        rank = below & 1
        for p in range(1, HALO_W - 1):
            rank = rank + (lax.shift_right_logical(below, jnp.int32(p)) & 1)
        halo = jnp.where(ups[g], up_base, low_base) + jnp.minimum(rank, NAMED - 1)
        local = rel < count
        tab[g] = jnp.where(local, rel, zero)
        tab[full + g] = jnp.where(local, rel, count + halo)
        up_rows[0, up_count] = g
        low_rows[0, low_count] = g
        up_rows[1, up_cross] = g
        low_rows[1, low_cross] = g
        up_rows[2, up_cross] = halo
        low_rows[2, low_cross] = halo
        up_cross = up_cross + jnp.where(ups[g], 1, 0)
        low_cross = low_cross + jnp.where(lows[g], 1, 0)
        up_count = up_count + (1 if g == count - 1 else jnp.where(ups[g], 1, 0))
        low_count = low_count + (1 if g == 0 else jnp.where(lows[g], 1, 0))
    tab[count] = zero
    tab[count + 1] = zero
    tab[full + count] = count + low_base + NAMED - 1
    tab[full + count + 1] = count + up_base
    for j in range(NAMED):
        up, low = up_rows[0, j], low_rows[0, j]
        tab[lists + j] = jnp.where(even, up, low)
        tab[lists + NAMED + j] = jnp.where(even, low, up)
    chains = ((0, 1, low_base + NAMED - 1), (count - 1, 2, up_base))
    for side, (rows, used) in enumerate(((low_rows, low_cross), (up_rows, up_cross))):
        for i in range(3):
            tab[cross + 3 * side * (1 + NAMED) + i] = jnp.int32(chains[side][i])
        for j in range(NAMED):
            at = cross + 3 * (side * (1 + NAMED) + 1 + j)
            tab[at] = jnp.where(j < used, rows[1, j], 0)
            tab[at + 1] = jnp.int32(3)
            tab[at + 2] = jnp.where(j < used, rows[2, j], 2 * NAMED)


def pack(tab, shift, aff, t, hl, send, base):
    width = t.shape[2]
    for j in range(NAMED):
        g = tab[base + j]
        send[j] = hl[g, :, :width]
        send[NAMED + j] = shifted(row_product(aff, tab, 0, g, hl), shift, t[g]).astype(BF)


def first_kernel(
    desc, queries, affinity, tile_col, t0, hl, send_b, aff, tab,
    buf, wide, tall, cols, up_rows, low_rows, sems, *, bounds, axis,
):
    count, rows = t0.shape[0], t0.shape[1]
    chunks = len(bounds) - 1
    parts = [pl.ds(a * rows, (b - a) * rows) for a, b in zip(bounds, bounds[1:])]
    _, lists, _, _ = offsets(count)
    load_q = pltpu.make_async_copy(queries, wide, sems.at[chunks])
    load_c = pltpu.make_async_copy(tile_col, cols, sems.at[chunks + 1])
    load_q.start()
    load_c.start()
    copies = []
    for c in range(chunks):
        copy = pltpu.make_async_copy(desc.at[parts[c]], buf.at[parts[c]], sems.at[c])
        copy.start()
        copies.append(copy)
    load_a = pltpu.make_async_copy(affinity, aff, sems.at[chunks + 2])
    load_a.start()
    hl[count + 2 * NAMED] = jnp.zeros(hl.shape[1:], BF)
    load_q.wait()
    tall[...] = wide[...].T
    load_c.wait()

    def finish(c):
        for g in range(bounds[c], bounds[c + 1]):
            value = jnp.maximum(t0[g], 0.0)
            value = value * value * value
            t0[g] = value
            put_rounded(hl, g, value)

    for c in range(chunks):
        copies[c].wait()
        if c == 0:
            fill_table(cols, tab, up_rows, low_rows, axis)
        scores = dot(buf[parts[c], :], tall[...])
        for i, g in enumerate(range(bounds[c], bounds[c + 1])):
            t0[g] = scores[i * rows : (i + 1) * rows]
        if c > 0:
            finish(c - 1)
    finish(chunks - 1)
    load_a.wait()
    pack(tab, SHIFTS[0], aff, t0, hl, send_b, lists + NAMED)


def add_products(sums, pairs, fields):
    count, rows, _ = fields[0].shape
    group = 32

    def body(i, sums):
        sums = list(sums)
        g = i // (rows // group)
        start = (i % (rows // group)) * group
        for part in range(group // 8):
            at = pl.ds(pl.multiple_of(start + 8 * part, 8), 8)
            v = [f[g, at, :] for f in fields]
            for n, (a, b) in enumerate(pairs):
                sums[n] = sums[n] + v[a] * v[b]
        return tuple(sums)

    return list(lax.fori_loop(0, count * rows // group, body, tuple(sums)))


def halo_products(tab, aff, hl, sums, factor):
    _, _, cross, _ = offsets(aff.shape[0])
    sums[...] = jnp.zeros(sums.shape, F32)
    for e in range(ENTRIES):
        g, slot, h = (tab[cross + 3 * e + i] for i in range(3))
        both = folded(dot_t(aff[g, slot], hl[g]))
        sums[h] += both if factor == 1.0 else factor * both


def rest_kernel(tab, aff, t, hl, part, hl_next, halo_part, send_a, sums, *, step):
    count = t.shape[0]
    _, lists, _, _ = offsets(count)
    pack(tab, SHIFTS[step], aff, t, hl, send_a, lists)
    hl_next[count + 2 * NAMED] = jnp.zeros(hl_next.shape[1:], BF)
    for g in range(count):
        value = shifted(row_product(aff, tab, 0, g, hl), SHIFTS[step], t[g])
        part[g] = value
        put_rounded(hl_next, g, value)
    halo_products(tab, aff, hl, sums, 1.0)
    for h in range(2 * NAMED):
        halo_part[h] = sums[h]


def early_kernel(t0, t1, t2, out):
    sums = [jnp.zeros((8, t0.shape[2]), F32) for _ in EARLY]
    for n, total in enumerate(add_products(sums, EARLY, (t0, t1, t2))):
        out[pl.ds(n, 1), :] = jnp.sum(total, axis=0, keepdims=True)


def complete(tab, aff, hl1, t1, halo_part, recv_a, recv_b, halo):
    count = t1.shape[0]
    _, lists, cross, _ = offsets(count)
    hl1[count + 2 * NAMED] = jnp.zeros(hl1.shape[1:], BF)
    halo[2 * NAMED] = jnp.zeros(halo.shape[1:], BF)
    for h in range(NAMED):
        halo[h] = recv_a[h]
        halo[NAMED + h] = recv_b[h]
        low, high = h, NAMED + h
        put_rounded(hl1, count + low, recv_a[NAMED + h].astype(F32) + halo_part[low])
        put_rounded(hl1, count + high, recv_b[NAMED + h].astype(F32) + halo_part[high])
    for e in range(ENTRIES):
        g, slot, h = (tab[cross + 3 * e + i] for i in range(3))
        t1[g] += dot(aff[g, slot], halo[h])
    for j in range(2 * NAMED):
        g = tab[lists + j]
        put_rounded(hl1, g, t1[g])


def advance(tab, aff, hl1, t1, t2, hl2, step, blocks=None):
    count = t1.shape[0]
    full = offsets(count)[0]
    hl2[count + 2 * NAMED] = jnp.zeros(hl2.shape[1:], BF)
    for g in range(count) if blocks is None else blocks:
        value = shifted(row_product(aff, tab, full, g, hl1), SHIFTS[step], t1[g])
        t2[g] = value
        put_rounded(hl2, g, value)


def near_kernel(
    tab, aff, _, __, halo_part, recv_a, recv_b, hl1, t1, send_b, halo, t2, hl2, *, axis
):
    count = t1.shape[0]
    _, lists, _, _ = offsets(count)
    even = lax.rem(lax.axis_index(axis), 2) == 0

    @pl.when(even)
    def _():
        complete(tab, aff, hl1, t1, halo_part, recv_a, recv_b, halo)
        partner = jnp.where(tab[0] < count, tab[0], 0)
        advance(tab, aff, hl1, t1, t2, hl2, 1, [*range(HALO_W + 1), partner])
        pack(tab, SHIFTS[2], aff, t2, hl2, send_b, lists + NAMED)

    @pl.when(jnp.logical_not(even))
    def _():
        send_b[...] = jnp.zeros(send_b.shape, BF)


def middle_kernel(
    tab, aff, _, __, halo_part, recv_a, recv_b, hl1, t1, t2, hl2, send_b, halo, *, axis
):
    _, lists, _, _ = offsets(t1.shape[0])
    odd = lax.rem(lax.axis_index(axis), 2) == 1

    @pl.when(odd)
    def _():
        complete(tab, aff, hl1, t1, halo_part, recv_a, recv_b, halo)
        advance(tab, aff, hl1, t1, t2, hl2, 1)
        pack(tab, SHIFTS[2], aff, t2, hl2, send_b, lists + NAMED)

    @pl.when(jnp.logical_not(odd))
    def _():
        advance(tab, aff, hl1, t1, t2, hl2, 1)
        send_b[...] = jnp.zeros(send_b.shape, BF)


def edge_kernel(tab, aff, _, __, halo_part, recv_a, recv_b, hl3, t3, send_b, halo, *, axis):
    full, lists, _, _ = offsets(t3.shape[0])
    odd = lax.rem(lax.axis_index(axis), 2) == 1

    @pl.when(odd)
    def _():
        complete(tab, aff, hl3, t3, halo_part, recv_a, recv_b, halo)
        for j in range(NAMED):
            g = tab[lists + NAMED + j]
            product = row_product(aff, tab, full, g, hl3)
            send_b[j] = shifted(product, SHIFTS[3], t3[g]).astype(BF)

    @pl.when(jnp.logical_not(odd))
    def _():
        send_b[...] = jnp.zeros(send_b.shape, BF)


def last_kernel(
    tab, aff, _, __, halo_part, recv_a, recv_b, hl3, t3, t4, hl4, send_a, halo, *, axis
):
    count, _, width = t3.shape
    _, lists, _, _ = offsets(count)

    @pl.when(lax.rem(lax.axis_index(axis), 2) == 0)
    def _():
        complete(tab, aff, hl3, t3, halo_part, recv_a, recv_b, halo)

    advance(tab, aff, hl3, t3, t4, hl4, 3)
    for j in range(NAMED):
        send_a[j] = hl4[tab[lists + j], :, :width]


def gram_kernel(tab, aff, t2, t3, t4, hl, early, out):
    count, rows, width = t2.shape
    sums = [jnp.zeros((8, width), F32) for _ in range(len(LATE) + 1)]
    fields = (None, None, t2, t3, t4)
    for g in range(count):
        local = row_product(aff, tab, 0, g, hl)
        v = [None if f is None else f[g] for f in fields]
        terms = [v[i] * v[j] for i, j in LATE] + [v[-1] * local]
        for n, term in enumerate(terms):
            sums[n] = sums[n] + term.reshape(rows // 8, 8, width).sum(0)
    out[pl.ds(0, len(EARLY)), :] = early[...]
    for n, total in enumerate(sums):
        out[pl.ds(len(EARLY) + n, 1), :] = jnp.sum(total, axis=0, keepdims=True)


def weight_kernel(tab, aff, hl, weight, sums):
    halo_products(tab, aff, hl, sums, 2.0)
    for h in range(2 * NAMED):
        weight[h] = sums[h]


def cross_kernel(weight, recv_a, recv_b, gram, out, *, axis):
    _, rows, width = weight.shape
    even = lax.rem(lax.axis_index(axis), 2) == 0
    out[...] = gram[...]

    @pl.when(even)
    def _():
        total = jnp.zeros((8, width), F32)
        for h in range(NAMED):
            part = weight[h] * recv_a[h].astype(F32) + weight[NAMED + h] * recv_b[h].astype(F32)
            total = total + part.reshape(rows // 8, 8, width).sum(0)
        last = pl.ds(ROWS - 1, 1)
        out[last, :] = out[last, :] + jnp.sum(total, axis=0, keepdims=True)


def spread_kernel(own, other, out):
    value = own[...] + other[...]
    for d in range(out.shape[0]):
        out[d] = value


def final_kernel(parts, t0, t1, t2, t3, t4, out, buf, sems):
    n = ITERATIONS
    value = parts[0]
    for d in range(1, parts.shape[0]):
        value = value + parts[d]
    gram = {}
    for k, (i, j) in enumerate(PAIRS):
        gram[i, j] = gram[j, i] = value[k : k + 1]
    for j in range(2, n - 1):
        for i in range(n - 2):
            if (i, j + 1) not in gram:
                entry = gram[i + 1, j] + (SHIFTS[i] - SHIFTS[j]) * gram[i, j]
                gram[i, j + 1] = gram[j + 1, i] = entry
    matrix = {}
    for i in range(n):
        for j in range(i, n):
            if i + 1 < n and j + 1 == n:
                product = gram[i + 1, j] + SHIFTS[i] * gram[i, j]
            elif j + 1 < n:
                product = gram[i, j + 1] + SHIFTS[j] * gram[i, j]
            else:
                product = value[ROWS - 1 : ROWS]
            matrix[i, j] = gram[i, j] - DAMP * product
    scale = [
        jnp.where(matrix[i, i] > 0.0, lax.rsqrt(jnp.maximum(matrix[i, i], 1e-37)), 0.0)
        for i in range(n)
    ]
    for i in range(n):
        for j in range(i, n):
            matrix[i, j] = matrix[i, j] * (scale[i] * scale[j])
    right = [gram[i, 0] * scale[i] for i in range(n)]
    inverse = []
    for k in range(n):
        pivot = matrix[k, k]
        inverse.append(jnp.where(pivot > PIVOT_MIN, 1.0 / jnp.maximum(pivot, PIVOT_MIN), 0.0))
        for i in range(k + 1, n):
            factor = matrix[k, i] * inverse[k]
            for j in range(i, n):
                matrix[i, j] = matrix[i, j] - factor * matrix[k, j]
            right[i] = right[i] - factor * right[k]
    coef = [None] * n
    for k in range(n - 1, -1, -1):
        rest = right[k]
        for j in range(k + 1, n):
            rest = rest - matrix[k, j] * coef[j]
        coef[k] = rest * inverse[k]
    coef = [coef[k] * scale[k] for k in range(n)]
    fields = (t0, t1, t2, t3, t4)
    count, rows, _ = t0.shape
    chunks = sems.shape[0]
    per = count // chunks
    copies = []
    for c in range(chunks):
        for g in range(c * per, (c + 1) * per):
            total = None
            for f, k in zip(fields, coef):
                term = f[g] * k
                total = term if total is None else total + term
            buf[pl.ds(g * rows, rows), :] = total
        part = pl.ds(c * per * rows, per * rows)
        copy = pltpu.make_async_copy(buf.at[part], out.at[part], sems.at[c])
        copy.start()
        copies.append(copy)
    for copy in copies:
        copy.wait()


def to_chip_partner(block, axis):
    return lax.ppermute(block, axis, [(i, i ^ 1) for i in range(lax.axis_size(axis))])


def shift(block, by, axis):
    n = lax.axis_size(axis)
    return lax.ppermute(block, axis, [(i, (i + by) % n) for i in range(n)])


def shards(descriptors, queries, affinity, tile_col):
    count, _, rows, _ = affinity.shape
    width = queries.shape[0]
    depth = descriptors.shape[1]
    axis = "dom"
    devices = lax.axis_size(axis)
    size = 128 * pl.cdiv(offsets(count)[-1], 128)
    blocks = count + 2 * NAMED + 1
    field = jax.ShapeDtypeStruct((count, rows, width), F32)
    rounded = jax.ShapeDtypeStruct((blocks, rows, width), BF)
    split = jax.ShapeDtypeStruct((blocks, rows, 2 * width), BF)
    edge = jax.ShapeDtypeStruct((2 * NAMED, rows, width), BF)
    half = jax.ShapeDtypeStruct((NAMED, rows, width), BF)
    early = jax.ShapeDtypeStruct((len(EARLY), width), F32)
    edge_sum = jax.ShapeDtypeStruct((2 * NAMED, rows, width), F32)
    sums_h = pltpu.VMEM((2 * NAMED + 1, rows, width), F32)
    work = [pltpu.VMEM((2 * NAMED + 1, rows, width), BF)]
    bounds = (0, count)
    flops = 2 * count * rows * 4 * rows * 2 * width

    def call(kernel, out_shape, products, scratch=(), aliases=None, limit=24):
        outs = out_shape if isinstance(out_shape, tuple) else (out_shape,)

        def run(*args):
            specs = [SMEM if x.dtype == jnp.int32 else VMEM for x in args]
            args = [
                pltpu.with_memory_space_constraint(x, pltpu.SMEM) if x.dtype == jnp.int32 else x
                for x in args
            ]
            return pl.pallas_call(
                kernel,
                out_shape=out_shape,
                in_specs=specs,
                out_specs=(VMEM,) * len(outs) if isinstance(out_shape, tuple) else VMEM,
                scratch_shapes=list(scratch),
                input_output_aliases=aliases or {},
                compiler_params=params(limit),
                cost_estimate=pl.CostEstimate(
                    flops=int(products * flops), bytes_accessed=4 << 20, transcendentals=0
                ),
            )(*args)

        return run

    operands = (descriptors, queries, affinity, tile_col.T)
    t0, hl0, send_b, aff, tab = pl.pallas_call(
        functools.partial(first_kernel, bounds=bounds, axis=axis),
        out_shape=(
            field,
            rounded,
            edge,
            jax.ShapeDtypeStruct(affinity.shape, BF),
            pltpu.SMEM((size,), jnp.int32),
        ),
        in_specs=[HBM] * 4,
        out_specs=(VMEM,) * 4 + (SMEM,),
        scratch_shapes=[
            pltpu.VMEM((count * rows, depth), BF),
            pltpu.VMEM((width, depth), BF),
            pltpu.VMEM((depth, width), BF),
            pltpu.SMEM((4, count), jnp.int32),
            pltpu.SMEM((3, count + 1), jnp.int32),
            pltpu.SMEM((3, count + 1), jnp.int32),
            pltpu.SemaphoreType.DMA((len(bounds) + 2,)),
        ],
        compiler_params=params(24),
        cost_estimate=pl.CostEstimate(flops=flops, bytes_accessed=4 << 20, transcendentals=0),
        name="first",
    )(*(pltpu.with_memory_space_constraint(x, pltpu.HBM) for x in operands))
    recv_even = shift(send_b, 1, axis)
    recv_odd = shift(send_b, -1, axis)
    part, hl1, halo_part, send_a = call(
        functools.partial(rest_kernel, step=0), (field, split, edge_sum, edge), 1, [sums_h]
    )(tab, aff, t0, hl0)
    recv_a = to_chip_partner(send_a, axis)
    first_half = {2: 0, 3: 1}
    hl1, t1, send = call(
        functools.partial(near_kernel, axis=axis),
        (split, field, edge),
        1,
        work
        + [pltpu.VMEM((count, rows, width), F32), pltpu.VMEM((blocks, rows, width), BF)],
        first_half,
    )(tab, aff, hl1, part, halo_part, recv_a, recv_even)
    got_odd = shift(send, -1, axis)
    _, t1, t2, hl2, send = call(
        functools.partial(middle_kernel, axis=axis),
        (split, field, field, rounded, edge),
        2,
        work,
        first_half,
    )(tab, aff, hl1, t1, halo_part, recv_a, recv_odd)
    got_even = shift(send, 1, axis)
    part, hl3, halo_part, send_a = call(
        functools.partial(rest_kernel, step=2), (field, rounded, edge_sum, edge), 1, [sums_h]
    )(tab, aff, t2, hl2)
    recv_a = to_chip_partner(send_a, axis)
    gram = call(early_kernel, early, 0.1)(t0, t1, t2)
    hl3, t3, send = call(
        functools.partial(edge_kernel, axis=axis), (rounded, field, half), 0.5, work, first_half
    )(tab, aff, hl3, part, halo_part, recv_a, got_odd)
    recv_b = shift(send, 1, axis)
    _, t3, t4, hl4, send_a = call(
        functools.partial(last_kernel, axis=axis),
        (rounded, field, field, rounded, half),
        1,
        work,
        first_half,
    )(tab, aff, hl3, t3, halo_part, recv_a, got_even)
    recv_a = to_chip_partner(send_a, axis)
    gram = call(
        gram_kernel, jax.ShapeDtypeStruct((ROWS, width), F32), 1
    )(tab, aff, t2, t3, t4, hl4, gram)
    weight = call(weight_kernel, edge_sum, 0.2, [sums_h])(tab, aff, hl4)
    entries = jax.ShapeDtypeStruct((ROWS, width), F32)
    gram = call(functools.partial(cross_kernel, axis=axis), entries, 0.1, limit=8)(
        weight, recv_a, recv_b, gram
    )
    other = to_chip_partner(gram, axis)
    copies = jax.ShapeDtypeStruct((devices // 2, ROWS, width), F32)
    parts = call(spread_kernel, copies, 0.1, limit=8)(gram, other)
    groups = [[2 * k + (k + core) % 2 for k in range(devices // 2)] for core in range(2)]
    parts = lax.all_to_all(parts, axis, 0, 0, axis_index_groups=groups)
    return pl.pallas_call(
        final_kernel,
        out_shape=jax.ShapeDtypeStruct((count * rows, width), F32),
        in_specs=[VMEM] * 6,
        out_specs=HBM,
        scratch_shapes=[
            pltpu.VMEM((count * rows, width), F32),
            pltpu.SemaphoreType.DMA((count // 3,)),
        ],
        compiler_params=params(24),
        name="final",
    )(parts, t0, t1, t2, t3, t4)


def solution(mesh):
    return jax.shard_map(
        shards,
        mesh=mesh,
        in_specs=(
            P(("region", "dom"), None),
            P("region", None),
            P(("region", "dom"), None, None, None),
            P(("region", "dom"), None),
        ),
        out_specs=P(("region", "dom"), None),
        check_vma=False,
    )
```
